128 devices in a mesh: req: 32 (over y, z, core), grp: 4 (over x).
Axes of the slice: x: 4, y: 4, z: 4, core: 2. Of those that a mesh axis runs over, the one named last changes fastest.
Arguments:
- hidden_in: bfloat16 [16384, 2048], P('req'), may hold values from -6 to 6
- attn_gain: float32 [2048], replicated, may hold values from 0.1 to 1.9
- mlp_gain: float32 [2048], replicated, may hold values from 0.1 to 1.9
- w_query: bfloat16 [2048, 2048], P(None, 'grp'), may hold values from -0.75 to 0.75
- w_key: bfloat16 [2048, 512], P(None, 'grp'), may hold values from -0.125 to 0.125
- w_value: bfloat16 [2048, 512], P(None, 'grp'), may hold values from -0.125 to 0.125
- w_out: bfloat16 [2048, 2048], P('grp'), may hold values from -0.125 to 0.125
- w_gate: bfloat16 [2048, 8192], P(None, 'req'), may hold values from -0.125 to 0.125
- w_up: bfloat16 [2048, 8192], P(None, 'req'), may hold values from -0.125 to 0.125
- w_down: bfloat16 [8192, 2048], P('req'), may hold values from -0.0625 to 0.0625
- cache_k: bfloat16 [16384, 16, 512], P('req', None, 'grp'), may hold values from -4000 to 4000
- cache_v: bfloat16 [16384, 16, 512], P('req', None, 'grp'), may hold values from -6 to 6
- owner_of_row: int32 [16384], P('req'), may hold values from 0 to 31, as said below
- new_len: int32 [32, 32], P('req'), may hold values from 0 to 32, as said below
- prior_len: int32 [32, 32], P('req'), may hold values from 0 to 256, as said below
- page_table: int32 [32, 512], P('req'), may hold values from 0 to 511, each once within a row
Outputs:
- layer_out: bfloat16 [16384, 2048], P(('req', 'grp'))
- new_cache_k: bfloat16 [16384, 16, 512], P('req', None, 'grp')
- new_cache_v: bfloat16 [16384, 16, 512], P('req', None, 'grp')
The draws below stay inside these ranges and needn't reach their ends.
Inputs may be any that keep to these rules, and one draw needn't show every extreme that they name: `owner_of_row`: rows of one block of 512 that name the same owner are consecutive; each block holds at most one request for each owner, of at most 32 rows; in every draw one owner receives a request of exactly 32 rows from every block. new_len[o, s] is the number of rows of block s of owner_of_row that name o. prior_len[o, s] + new_len[o, s] <= 256.
All inputs are finite; a program needn't handle non-finite values.
Results may differ from the reference program's by a relative error of at most 0.0063.
Values may be sent and summed in bfloat16 or wider, within the bound.
A program may use at most 128 MiB of HBM per device.

```python
import jax
import jax.numpy as jnp
from jax import lax

D = 2048
HEADS = 32
KVH = 8
HD = 64
FF = 8192
ROWS = 512
PAGE = 16
MAXP = 16
TOKENS = 16384
PAIR = 32
CONTEXT = 256
POOL = 512
HEAD_BLOCKS = 4
QCOLS = 512
UNIT_BLOCKS = 32
FF_DEV = 256
N_REQ = 32


def make_plan(key):
    hot_key = jax.random.fold_in(key, 11)
    hottest = jax.random.randint(hot_key, (), 0, N_REQ)
    owners = jnp.arange(N_REQ, dtype=jnp.int32)

    def per_source(source):
        source_key = jax.random.fold_in(key, 1000 + source)
        key_shift, key_rank, key_first, key_pack = jax.random.split(source_key, 4)
        shift = jax.random.randint(key_shift, (), 1, N_REQ)
        vacant = (hottest + shift) % N_REQ
        ranks = jax.random.permutation(key_rank, N_REQ).astype(jnp.int32)
        special = jnp.logical_or(owners == hottest, owners == vacant)
        scores = ranks + N_REQ * special.astype(jnp.int32)
        order = jnp.argsort(scores, stable=True)
        firsts = jax.random.randint(key_first, (N_REQ // 2,), 1, PAIR)
        paired = jnp.stack([firsts, PAIR - firsts], axis=1).reshape(-1)
        sorted_len = jnp.where(jnp.arange(N_REQ, dtype=jnp.int32) < N_REQ - 2, paired, 0)
        lengths = jnp.zeros((N_REQ,), jnp.int32).at[order].set(sorted_len.astype(jnp.int32))
        lengths = jnp.where(owners == hottest, PAIR, lengths)
        lengths = jnp.where(owners == vacant, 0, lengths)
        packing = jax.random.permutation(key_pack, N_REQ).astype(jnp.int32)
        ends = jnp.cumsum(lengths[packing])
        row_ids = jnp.arange(ROWS, dtype=jnp.int32)
        which = jnp.sum((ends[None, :] <= row_ids[:, None]).astype(jnp.int32), axis=1)
        return (packing[which], lengths)
    row_owner, lengths = jax.vmap(per_source)(jnp.arange(N_REQ, dtype=jnp.int32))
    return (row_owner.reshape(-1).astype(jnp.int32), jnp.transpose(lengths).astype(jnp.int32), hottest)


def draw_owner_of_row(key, part):
    return make_plan(key)[0]


def draw_new_len(key, part):
    return make_plan(key)[1]


def draw_prior_len(key, part):
    plan = make_plan(key)
    lengths = plan[1]
    hottest = plan[2]
    prior_key = jax.random.fold_in(key, 23)
    room = CONTEXT - lengths
    prior = jax.random.randint(prior_key, (N_REQ, N_REQ), 0, room + 1)
    prior = jnp.where(lengths == 0, CONTEXT, prior)
    prior = prior.at[hottest, hottest].set(0)
    return prior.astype(jnp.int32)


def draw_cache_k(key, part):
    shape = (N_REQ * POOL, PAGE, KVH * HD)
    base_key = jax.random.fold_in(key, 0)
    values = jnp.clip(jax.random.normal(base_key, shape, jnp.float32), -6.0, 6.0)
    return values.astype(jnp.bfloat16)


def block_scale(key, extent, shards, low, high):
    factor_of, own = 1.0, jax.random.fold_in(key, 6)
    for axis_at, parts in shards:
        draws = jnp.exp(jax.random.uniform(jax.random.fold_in(own, axis_at), (parts,), jnp.float32, low / len(shards), high / len(shards)))
        factor_of = factor_of * jnp.repeat(draws, extent[axis_at] // parts).reshape([-1 if axis == axis_at else 1 for axis in range(len(extent))])
    return factor_of


def normal_values(own_key, shape, scale, most, shards=(), kind=jnp.bfloat16):
    entries = scale * jax.random.normal(own_key, shape, jnp.float32)
    if shards:
        entries = entries * block_scale(own_key, shape, shards, -0.22, 0.18)
    return jnp.clip(entries, -most, most).astype(kind)


def setup_inputs(seed: int = 0) -> dict:
    key_of = jax.random.split(jax.random.key(seed), 17)
    hidden_in = normal_values(key_of[0], (TOKENS, D), 1.0, 6.0, ((0, 32),))
    attn_gain = jnp.clip(1.0 + 0.18 * jax.random.normal(key_of[1], (D,), jnp.float32), 0.1, 1.9)
    mlp_gain = jnp.clip(1.0 + 0.18 * jax.random.normal(key_of[2], (D,), jnp.float32), 0.1, 1.9)
    w_query = normal_values(key_of[3], (D, HEADS * HD), (D // 32) ** -0.5, 0.75, ((1, 4),))
    w_key = normal_values(key_of[4], (D, KVH * HD), D ** -0.5, 0.125, ((1, 4),))
    w_value = normal_values(key_of[5], (D, KVH * HD), D ** -0.5, 0.125, ((1, 4),))
    w_out = normal_values(key_of[6], (HEADS * HD, D), (HEADS * HD) ** -0.5, 0.125, ((0, 4),))
    w_gate = normal_values(key_of[7], (D, FF), D ** -0.5, 0.125, ((1, 32),))
    w_up = normal_values(key_of[8], (D, FF), D ** -0.5, 0.125, ((1, 32),))
    w_down = normal_values(key_of[9], (FF, D), FF ** -0.5, 0.0625, ((0, 32),))
    cache_k = draw_cache_k(jax.random.fold_in(key_of[16], 71), 0)
    cache_v = normal_values(key_of[11], (N_REQ * POOL, PAGE, KVH * HD), 1.0, 6.0, ((0, 32), (2, 4)))
    owner_of_row = draw_owner_of_row(jax.random.fold_in(key_of[16], 71), 0)
    new_len = draw_new_len(jax.random.fold_in(key_of[16], 71), 0)
    prior_len = draw_prior_len(jax.random.fold_in(key_of[16], 71), 0)
    page_table = jax.vmap(lambda own: jax.random.permutation(own, POOL))(jax.random.split(key_of[15], N_REQ)).reshape((N_REQ, POOL)).astype(jnp.int32)
    return {"hidden_in": hidden_in, "attn_gain": attn_gain, "mlp_gain": mlp_gain, "w_query": w_query, "w_key": w_key, "w_value": w_value, "w_out": w_out, "w_gate": w_gate, "w_up": w_up, "w_down": w_down, "cache_k": cache_k, "cache_v": cache_v, "owner_of_row": owner_of_row, "new_len": new_len, "prior_len": prior_len, "page_table": page_table}


EPSILON = 1e-05
RESIDUAL_MULT = 0.22
SCORE_MULT = 0.015625
ROPE_BASE = 10000000.0

def normalize(values, gain):
    mean_square = lax.optimization_barrier(jnp.mean(values * values, axis=-1, keepdims=True))
    return values * lax.rsqrt(mean_square + EPSILON) * gain

def rotary(values, positions):
    dim = values.shape[-1]
    half = dim // 2
    freq = jnp.power(ROPE_BASE, -2.0 * jnp.arange(half, dtype=jnp.int32).astype(jnp.float32) / dim)
    angle = positions.astype(jnp.float32)[:, :, None] * freq
    cosine = jnp.cos(angle)[:, :, None, :]
    sine = jnp.sin(angle)[:, :, None, :]
    first = values[..., :half].astype(jnp.float32)
    second = values[..., half:].astype(jnp.float32)
    return jnp.concatenate([first * cosine - second * sine, second * cosine + first * sine], axis=-1)

def source_layout(owner_block, peers, pair_rows):
    row_count = owner_block.shape[0]
    owners = jnp.arange(peers, dtype=jnp.int32)
    member = owner_block[None, :] == owners[:, None]
    counts = lax.optimization_barrier(jnp.sum(member.astype(jnp.int32), axis=1))
    row_ids = jnp.arange(row_count, dtype=jnp.int32)
    starts = lax.optimization_barrier(jnp.min(jnp.where(member, row_ids[None, :], row_count), axis=1))
    slots = jnp.arange(pair_rows, dtype=jnp.int32)
    gather_rows = jnp.where(slots[None, :] < counts[:, None], starts[:, None] + slots[None, :], row_count)
    row_start = lax.optimization_barrier(jnp.sum(jnp.where(member, starts[:, None], 0), axis=0))
    back_rows = owner_block * pair_rows + (row_ids - row_start)
    return (gather_rows.reshape(-1).astype(jnp.int32), back_rows.astype(jnp.int32))

def owner_attention(query_in, key_in, value_in, cache_keys, cache_values, lengths, priors, table):
    sources, pair_rows, qcols = query_in.shape
    kcols = key_in.shape[-1]
    kv_heads = kcols // HD
    group = qcols // kcols
    pool_pages = cache_keys.shape[0]
    slots = jnp.arange(pair_rows, dtype=jnp.int32)
    positions = priors[:, None] + slots[None, :]
    live = slots[None, :] < lengths[:, None]
    query_rot = rotary(query_in.reshape(sources, pair_rows, qcols // HD, HD), positions).astype(jnp.bfloat16)
    key_rot = rotary(key_in.reshape(sources, pair_rows, kv_heads, HD), positions).astype(jnp.bfloat16)
    key_rot = key_rot.reshape(sources, pair_rows, kcols)
    pages = table.reshape(sources, MAXP)
    page_index = jnp.minimum(positions // PAGE, MAXP - 1)
    target = jnp.take_along_axis(pages, page_index, axis=1)
    target = jnp.where(live, target, pool_pages).reshape(-1)
    offset = (positions % PAGE).reshape(-1)
    keys_out = cache_keys.at[target, offset].set(key_rot.reshape(-1, kcols), mode='drop')
    values_out = cache_values.at[target, offset].set(value_in.reshape(-1, kcols), mode='drop')
    key_block = jnp.take(keys_out, pages.reshape(-1), axis=0).reshape(sources, CONTEXT, kv_heads, HD)
    value_block = jnp.take(values_out, pages.reshape(-1), axis=0).reshape(sources, CONTEXT, kv_heads, HD)
    grouped = query_rot.reshape(sources, pair_rows, kv_heads, group, HD)
    scores = jnp.einsum('stkgd,sjkd->skgtj', grouped.astype(jnp.float32), key_block.astype(jnp.float32)) * SCORE_MULT
    allowed = jnp.arange(CONTEXT, dtype=jnp.int32)[None, None, None, None, :] <= positions[:, None, None, :, None]
    scores = jnp.where(allowed, scores, -jnp.inf)
    top = lax.optimization_barrier(jnp.max(scores, axis=-1, keepdims=True))
    weights = jnp.exp(scores - top)
    probs = (weights / lax.optimization_barrier(jnp.sum(weights, axis=-1, keepdims=True))).astype(jnp.bfloat16)
    mixed = jnp.einsum('skgtj,sjkd->stkgd', probs.astype(jnp.float32), value_block.astype(jnp.float32))
    return (mixed.astype(jnp.bfloat16).reshape(sources, pair_rows, qcols), keys_out, values_out)

def reference(hidden_in, attn_gain, mlp_gain, w_query, w_key, w_value, w_out, w_gate, w_up, w_down, cache_k, cache_v, owner_of_row, new_len, prior_len, page_table):
    inputs = hidden_in.astype(jnp.float32)
    normed = normalize(inputs, attn_gain).astype(jnp.bfloat16)
    query_all = jnp.dot(normed, w_query, preferred_element_type=jnp.float32).astype(jnp.bfloat16)
    key_all = jnp.dot(normed, w_key, preferred_element_type=jnp.float32).astype(jnp.bfloat16)
    value_all = jnp.dot(normed, w_value, preferred_element_type=jnp.float32).astype(jnp.bfloat16)
    owner_blocks = owner_of_row.reshape(N_REQ, ROWS)
    gather_rows, back_rows = jax.vmap(lambda block: source_layout(block, N_REQ, PAIR))(owner_blocks)

    def sendout(table_rows, indices):
        picked = jnp.take(table_rows, indices, axis=0, mode='fill', fill_value=0)
        return picked.reshape(N_REQ, PAIR, -1)
    send_query = jax.vmap(sendout)(query_all.reshape(N_REQ, ROWS, -1), gather_rows)
    send_key = jax.vmap(sendout)(key_all.reshape(N_REQ, ROWS, -1), gather_rows)
    send_value = jax.vmap(sendout)(value_all.reshape(N_REQ, ROWS, -1), gather_rows)
    recv_query = jnp.swapaxes(send_query, 0, 1)
    recv_key = jnp.swapaxes(send_key, 0, 1)
    recv_value = jnp.swapaxes(send_value, 0, 1)
    owner_keys = cache_k.reshape(N_REQ, POOL, PAGE, KVH * HD)
    owner_values = cache_v.reshape(N_REQ, POOL, PAGE, KVH * HD)

    def per_owner(items):
        return owner_attention(*items)
    mixed, keys_new, values_new = lax.map(per_owner, (recv_query, recv_key, recv_value, owner_keys, owner_values, new_len, prior_len, page_table))
    back = jnp.swapaxes(mixed, 0, 1).reshape(N_REQ, N_REQ * PAIR, -1)
    attn = jax.vmap(lambda block, indices: jnp.take(block, indices, axis=0))(back, back_rows).reshape(TOKENS, -1)
    attn_sum = jnp.zeros((TOKENS, D), jnp.float32)
    for block in range(HEAD_BLOCKS):
        part = jnp.dot(attn[:, block * QCOLS:(block + 1) * QCOLS], w_out[block * QCOLS:(block + 1) * QCOLS], preferred_element_type=jnp.float32)
        part = lax.optimization_barrier(part.astype(jnp.bfloat16))
        attn_sum = attn_sum + part.astype(jnp.float32)
    residual = inputs + RESIDUAL_MULT * attn_sum
    mlp_in = normalize(residual, mlp_gain).astype(jnp.bfloat16)
    gate_blocks = jnp.transpose(w_gate.reshape(D, UNIT_BLOCKS, FF_DEV), (1, 0, 2))
    up_blocks = jnp.transpose(w_up.reshape(D, UNIT_BLOCKS, FF_DEV), (1, 0, 2))
    down_blocks = w_down.reshape(UNIT_BLOCKS, FF_DEV, D)

    def add_block(total, weights):
        gate = jnp.dot(mlp_in, weights[0], preferred_element_type=jnp.float32)
        upper = jnp.dot(mlp_in, weights[1], preferred_element_type=jnp.float32)
        hidden = (jax.nn.silu(gate) * upper).astype(jnp.bfloat16)
        term = jnp.dot(hidden, weights[2], preferred_element_type=jnp.float32).astype(jnp.bfloat16)
        term = lax.optimization_barrier(term)
        return (total + term.astype(jnp.float32), None)
    down, _ = lax.scan(add_block, jnp.zeros((TOKENS, D), jnp.float32), (gate_blocks, up_blocks, down_blocks))
    layer_out = (residual + RESIDUAL_MULT * down).astype(jnp.bfloat16)
    return (layer_out, keys_new.reshape(N_REQ * POOL, PAGE, KVH * HD), values_new.reshape(N_REQ * POOL, PAGE, KVH * HD))
```

```python
import jax
import jax.numpy as jnp
from jax import lax
from jax.sharding import Mesh, PartitionSpec as P

HD = 64
PAGE = 16
MAXP = 16
CONTEXT = 256


EPSILON = 1e-05
RESIDUAL_MULT = 0.22
SCORE_MULT = 0.015625
ROPE_BASE = 10000000.0


def normalize(values, gain):
    mean_square = jnp.mean(values * values, axis=-1, keepdims=True)
    return values * lax.rsqrt(mean_square + EPSILON) * gain


def rotary(values, positions):
    dim = values.shape[-1]
    half = dim // 2
    freq = jnp.power(ROPE_BASE, -2.0 * jnp.arange(half, dtype=jnp.int32).astype(jnp.float32) / dim)
    angle = positions.astype(jnp.float32)[:, :, None] * freq
    cosine = jnp.cos(angle)[:, :, None, :]
    sine = jnp.sin(angle)[:, :, None, :]
    first = values[..., :half].astype(jnp.float32)
    second = values[..., half:].astype(jnp.float32)
    return jnp.concatenate(
        [first * cosine - second * sine, second * cosine + first * sine], axis=-1
    )


def source_layout(owner_block, peers, pair_rows):
    row_count = owner_block.shape[0]
    owners = jnp.arange(peers, dtype=jnp.int32)
    member = owner_block[None, :] == owners[:, None]
    counts = jnp.sum(member.astype(jnp.int32), axis=1)
    row_ids = jnp.arange(row_count, dtype=jnp.int32)
    starts = jnp.min(jnp.where(member, row_ids[None, :], row_count), axis=1)
    slots = jnp.arange(pair_rows, dtype=jnp.int32)
    gather_rows = jnp.where(
        slots[None, :] < counts[:, None], starts[:, None] + slots[None, :], row_count
    )
    row_start = jnp.sum(jnp.where(member, starts[:, None], 0), axis=0)
    back_rows = owner_block * pair_rows + (row_ids - row_start)
    return (gather_rows.reshape(-1), back_rows)


def owner_attention(query_in, key_in, value_in, cache_keys, cache_values, lengths, priors, table):
    sources, pair_rows, qcols = query_in.shape
    kcols = key_in.shape[-1]
    kv_heads = kcols // HD
    group = qcols // kcols
    pool_pages = cache_keys.shape[0]
    slots = jnp.arange(pair_rows, dtype=jnp.int32)
    positions = priors[:, None] + slots[None, :]
    live = slots[None, :] < lengths[:, None]
    query_rot = rotary(query_in.reshape(sources, pair_rows, qcols // HD, HD), positions).astype(
        jnp.bfloat16
    )
    key_rot = rotary(key_in.reshape(sources, pair_rows, kv_heads, HD), positions).astype(
        jnp.bfloat16
    )
    key_rot = key_rot.reshape(sources, pair_rows, kcols)
    pages = table.reshape(sources, MAXP)
    page_index = jnp.minimum(positions // PAGE, MAXP - 1)
    target = jnp.take_along_axis(pages, page_index, axis=1)
    target = jnp.where(live, target, pool_pages).reshape(-1)
    offset = (positions % PAGE).reshape(-1)
    keys_out = cache_keys.at[target, offset].set(key_rot.reshape(-1, kcols), mode="drop")
    values_out = cache_values.at[target, offset].set(value_in.reshape(-1, kcols), mode="drop")
    key_block = jnp.take(keys_out, pages.reshape(-1), axis=0).reshape(
        sources, CONTEXT, kv_heads, HD
    )
    value_block = jnp.take(values_out, pages.reshape(-1), axis=0).reshape(
        sources, CONTEXT, kv_heads, HD
    )
    grouped = query_rot.reshape(sources, pair_rows, kv_heads, group, HD)
    scores = (
        jnp.einsum("stkgd,sjkd->skgtj", grouped, key_block, preferred_element_type=jnp.float32)
        * SCORE_MULT
    )
    allowed = (
        jnp.arange(CONTEXT, dtype=jnp.int32)[None, None, None, None, :]
        <= positions[:, None, None, :, None]
    )
    scores = jnp.where(allowed, scores, -jnp.inf)
    top = jnp.max(scores, axis=-1, keepdims=True)
    weights = jnp.exp(scores - top)
    probs = (weights / jnp.sum(weights, axis=-1, keepdims=True)).astype(jnp.bfloat16)
    mixed = jnp.einsum("skgtj,sjkd->stkgd", probs, value_block, preferred_element_type=jnp.float32)
    return (mixed.astype(jnp.bfloat16).reshape(sources, pair_rows, qcols), keys_out, values_out)


def body(
    hidden_in,
    attn_gain,
    mlp_gain,
    w_query,
    w_key,
    w_value,
    w_out,
    w_gate,
    w_up,
    w_down,
    cache_k,
    cache_v,
    owner_of_row,
    new_len,
    prior_len,
    page_table,
):
    peers = lax.axis_size(REQ)
    groups = lax.axis_size("grp")
    row_count = hidden_in.shape[0]
    pair_rows = 2 * row_count // peers
    quarter = row_count // groups
    group_index = lax.axis_index("grp")
    gate_w = lax.all_gather(w_gate, "rb", axis=1, tiled=True)
    up_w = lax.all_gather(w_up, "rb", axis=1, tiled=True)
    down_w = lax.all_gather(w_down, "rb", axis=0, tiled=True)
    normed = normalize(hidden_in.astype(jnp.float32), attn_gain).astype(jnp.bfloat16)
    qcols = w_query.shape[1]
    kcols = w_key.shape[1]
    query_rows = jnp.dot(normed, w_query, preferred_element_type=jnp.float32).astype(jnp.bfloat16)
    key_rows = jnp.dot(normed, w_key, preferred_element_type=jnp.float32).astype(jnp.bfloat16)
    value_rows = jnp.dot(normed, w_value, preferred_element_type=jnp.float32).astype(jnp.bfloat16)
    qkv_rows = jnp.concatenate([query_rows, key_rows, value_rows], axis=1)
    gather_rows, back_rows = source_layout(owner_of_row, peers, pair_rows)
    send_qkv = jnp.take(qkv_rows, gather_rows, axis=0, mode="fill", fill_value=0).reshape(
        peers, pair_rows, -1
    )
    recv_qkv = lax.all_to_all(send_qkv, REQ, split_axis=0, concat_axis=0, tiled=True)
    recv_query = recv_qkv[..., :qcols]
    recv_key = recv_qkv[..., qcols : qcols + kcols]
    recv_value = recv_qkv[..., qcols + kcols :]
    mixed, keys_out, values_out = owner_attention(
        recv_query, recv_key, recv_value, cache_k, cache_v, new_len[0], prior_len[0], page_table[0]
    )
    gate_w, up_w, down_w, mixed = lax.optimization_barrier((gate_w, up_w, down_w, mixed))
    returned = lax.all_to_all(mixed, REQ, split_axis=0, concat_axis=0, tiled=True)
    attn_rows = jnp.take(returned.reshape(peers * pair_rows, -1), back_rows, axis=0)
    projected = jnp.dot(attn_rows, w_out, preferred_element_type=jnp.float32)
    attn_part = lax.psum_scatter(
        projected.astype(jnp.bfloat16), "grp", scatter_dimension=0, tiled=True
    ).astype(jnp.float32)
    own_rows = lax.dynamic_slice_in_dim(hidden_in, group_index * quarter, quarter, 0).astype(
        jnp.float32
    )
    residual = own_rows + RESIDUAL_MULT * attn_part
    mlp_in = normalize(residual, mlp_gain).astype(jnp.bfloat16)
    piece = lax.all_gather(mlp_in, "ra", axis=0, tiled=True)
    gate = jnp.dot(piece, gate_w, preferred_element_type=jnp.float32)
    upper = jnp.dot(piece, up_w, preferred_element_type=jnp.float32)
    hidden = (jax.nn.silu(gate) * upper).astype(jnp.bfloat16)
    down = lax.psum_scatter(
        jnp.dot(hidden, down_w, preferred_element_type=jnp.float32).astype(jnp.bfloat16),
        "ra",
        scatter_dimension=0,
        tiled=True,
    ).astype(jnp.float32)
    layer_out = (residual + RESIDUAL_MULT * down).astype(jnp.bfloat16)
    return (layer_out, keys_out, values_out)


REQ = ("ra", "rb")


def solution(mesh):
    req_size = mesh.shape["req"]
    split = 4
    inner = Mesh(
        mesh.devices.reshape(req_size // split, split, mesh.shape["grp"]), ("ra", "rb", "grp")
    )
    in_specs = (
        P(REQ, None),
        P(),
        P(),
        P(None, "grp"),
        P(None, "grp"),
        P(None, "grp"),
        P("grp", None),
        P(None, REQ),
        P(None, REQ),
        P(REQ, None),
        P(REQ, None, "grp"),
        P(REQ, None, "grp"),
        P(REQ),
        P(REQ, None),
        P(REQ, None),
        P(REQ, None),
    )
    out_specs = (P(REQ + ("grp",), None), P(REQ, None, "grp"), P(REQ, None, "grp"))
    return jax.shard_map(body, mesh=inner, in_specs=in_specs, out_specs=out_specs, check_vma=False)
```

```python
import jax
import jax.numpy as jnp
from jax import lax
from jax.sharding import Mesh, PartitionSpec as P

HD = 64
PAGE = 16
MAXP = 16
CONTEXT = 256


EPSILON = 1e-05
RESIDUAL_MULT = 0.22
SCORE_MULT = 0.015625
ROPE_BASE = 10000000.0


def normalize(values, gain):
    mean_square = jnp.mean(values * values, axis=-1, keepdims=True)
    return values * lax.rsqrt(mean_square + EPSILON) * gain


def rotary(values, positions):
    dim = values.shape[-1]
    half = dim // 2
    freq = jnp.power(ROPE_BASE, -2.0 * jnp.arange(half, dtype=jnp.int32).astype(jnp.float32) / dim)
    angle = positions.astype(jnp.float32)[:, :, None] * freq
    cosine = jnp.cos(angle)[:, :, None, :]
    sine = jnp.sin(angle)[:, :, None, :]
    first = values[..., :half].astype(jnp.float32)
    second = values[..., half:].astype(jnp.float32)
    return jnp.concatenate(
        [first * cosine - second * sine, second * cosine + first * sine], axis=-1
    )


def source_layout(owner_block, peers, pair_rows):
    row_count = owner_block.shape[0]
    owners = jnp.arange(peers, dtype=jnp.int32)
    member = owner_block[None, :] == owners[:, None]
    counts = jnp.sum(member.astype(jnp.int32), axis=1)
    row_ids = jnp.arange(row_count, dtype=jnp.int32)
    starts = jnp.min(jnp.where(member, row_ids[None, :], row_count), axis=1)
    slots = jnp.arange(pair_rows, dtype=jnp.int32)
    gather_rows = jnp.where(
        slots[None, :] < counts[:, None], starts[:, None] + slots[None, :], row_count
    )
    row_start = jnp.sum(jnp.where(member, starts[:, None], 0), axis=0)
    back_rows = owner_block * pair_rows + (row_ids - row_start)
    return (gather_rows.reshape(-1), back_rows)


def owner_attention(query_in, key_in, value_in, cache_keys, cache_values, lengths, priors, table):
    sources, pair_rows, qcols = query_in.shape
    kcols = key_in.shape[-1]
    kv_heads = kcols // HD
    group = qcols // kcols
    pool_pages = cache_keys.shape[0]
    slots = jnp.arange(pair_rows, dtype=jnp.int32)
    positions = priors[:, None] + slots[None, :]
    live = slots[None, :] < lengths[:, None]
    query_rot = rotary(query_in.reshape(sources, pair_rows, qcols // HD, HD), positions).astype(
        jnp.bfloat16
    )
    key_rot = rotary(key_in.reshape(sources, pair_rows, kv_heads, HD), positions).astype(
        jnp.bfloat16
    )
    key_rot = key_rot.reshape(sources, pair_rows, kcols)
    pages = table.reshape(sources, MAXP)
    page_index = jnp.minimum(positions // PAGE, MAXP - 1)
    target = jnp.take_along_axis(pages, page_index, axis=1)
    target = jnp.where(live, target, pool_pages).reshape(-1)
    offset = (positions % PAGE).reshape(-1)
    keys_out = cache_keys.at[target, offset].set(key_rot.reshape(-1, kcols), mode="drop")
    values_out = cache_values.at[target, offset].set(value_in.reshape(-1, kcols), mode="drop")
    key_block = jnp.take(keys_out, pages.reshape(-1), axis=0).reshape(
        sources, CONTEXT, kv_heads, HD
    )
    value_block = jnp.take(values_out, pages.reshape(-1), axis=0).reshape(
        sources, CONTEXT, kv_heads, HD
    )
    grouped = query_rot.reshape(sources, pair_rows, kv_heads, group, HD)
    scores = (
        jnp.einsum("stkgd,sjkd->skgtj", grouped, key_block, preferred_element_type=jnp.float32)
        * SCORE_MULT
    )
    allowed = (
        jnp.arange(CONTEXT, dtype=jnp.int32)[None, None, None, None, :]
        <= positions[:, None, None, :, None]
    )
    scores = jnp.where(allowed, scores, -jnp.inf)
    top = jnp.max(scores, axis=-1, keepdims=True)
    weights = jnp.exp(scores - top)
    probs = (weights / jnp.sum(weights, axis=-1, keepdims=True)).astype(jnp.bfloat16)
    mixed = jnp.einsum("skgtj,sjkd->stkgd", probs, value_block, preferred_element_type=jnp.float32)
    return (mixed.astype(jnp.bfloat16).reshape(sources, pair_rows, qcols), keys_out, values_out)


def body(
    hidden_in,
    attn_gain,
    mlp_gain,
    w_query,
    w_key,
    w_value,
    w_out,
    w_gate,
    w_up,
    w_down,
    cache_k,
    cache_v,
    owner_of_row,
    new_len,
    prior_len,
    page_table,
):
    peers = lax.axis_size(REQ)
    groups = lax.axis_size("grp")
    row_count = hidden_in.shape[0]
    pair_rows = 2 * row_count // peers
    quarter = row_count // groups
    group_index = lax.axis_index("grp")
    gate_w = lax.all_gather(w_gate, "ry", axis=1, tiled=True)
    up_w = lax.all_gather(w_up, "ry", axis=1, tiled=True)
    down_w = lax.all_gather(w_down, "ry", axis=0, tiled=True)
    normed = normalize(hidden_in.astype(jnp.float32), attn_gain).astype(jnp.bfloat16)
    qcols = w_query.shape[1]
    kcols = w_key.shape[1]
    query_rows = jnp.dot(normed, w_query, preferred_element_type=jnp.float32).astype(jnp.bfloat16)
    key_rows = jnp.dot(normed, w_key, preferred_element_type=jnp.float32).astype(jnp.bfloat16)
    value_rows = jnp.dot(normed, w_value, preferred_element_type=jnp.float32).astype(jnp.bfloat16)
    qkv_rows = jnp.concatenate([query_rows, key_rows, value_rows], axis=1)
    gather_rows, back_rows = source_layout(owner_of_row, peers, pair_rows)
    send_qkv = jnp.take(qkv_rows, gather_rows, axis=0, mode="fill", fill_value=0).reshape(
        peers, pair_rows, -1
    )
    recv_qkv = lax.all_to_all(send_qkv, REQ, split_axis=0, concat_axis=0, tiled=True)
    recv_query = recv_qkv[..., :qcols]
    recv_key = recv_qkv[..., qcols : qcols + kcols]
    recv_value = recv_qkv[..., qcols + kcols :]
    mixed, keys_out, values_out = owner_attention(
        recv_query, recv_key, recv_value, cache_k, cache_v, new_len[0], prior_len[0], page_table[0]
    )
    gate_w, up_w, down_w, mixed = lax.optimization_barrier((gate_w, up_w, down_w, mixed))
    returned = lax.all_to_all(mixed, REQ, split_axis=0, concat_axis=0, tiled=True)
    attn_rows = jnp.take(returned.reshape(peers * pair_rows, -1), back_rows, axis=0)
    projected = jnp.dot(attn_rows, w_out, preferred_element_type=jnp.float32)
    attn_part = lax.psum_scatter(
        projected.astype(jnp.bfloat16), "grp", scatter_dimension=0, tiled=True
    ).astype(jnp.float32)
    own_rows = lax.dynamic_slice_in_dim(hidden_in, group_index * quarter, quarter, 0).astype(
        jnp.float32
    )
    residual = own_rows + RESIDUAL_MULT * attn_part
    mlp_in = normalize(residual, mlp_gain).astype(jnp.bfloat16)
    piece = lax.all_gather(mlp_in, "rzc", axis=0, tiled=True)
    gate = jnp.dot(piece, gate_w, preferred_element_type=jnp.float32)
    upper = jnp.dot(piece, up_w, preferred_element_type=jnp.float32)
    hidden = (jax.nn.silu(gate) * upper).astype(jnp.bfloat16)
    down = lax.psum_scatter(
        jnp.dot(hidden, down_w, preferred_element_type=jnp.float32).astype(jnp.bfloat16),
        "rzc",
        scatter_dimension=0,
        tiled=True,
    ).astype(jnp.float32)
    layer_out = (residual + RESIDUAL_MULT * down).astype(jnp.bfloat16)
    return (layer_out, keys_out, values_out)


REQ = ("ry", "rzc")


def solution(mesh):
    req_size = mesh.shape["req"]
    major = 4
    inner = Mesh(
        mesh.devices.reshape(major, req_size // major, mesh.shape["grp"]), ("ry", "rzc", "grp")
    )
    in_specs = (
        P(REQ, None),
        P(),
        P(),
        P(None, "grp"),
        P(None, "grp"),
        P(None, "grp"),
        P("grp", None),
        P(None, REQ),
        P(None, REQ),
        P(REQ, None),
        P(REQ, None, "grp"),
        P(REQ, None, "grp"),
        P(REQ),
        P(REQ, None),
        P(REQ, None),
        P(REQ, None),
    )
    out_specs = (P(REQ + ("grp",), None), P(REQ, None, "grp"), P(REQ, None, "grp"))
    return jax.shard_map(body, mesh=inner, in_specs=in_specs, out_specs=out_specs, check_vma=False)
```

```python
import jax
import jax.numpy as jnp
from jax import lax
from jax.experimental import pallas as pl
from jax.experimental.pallas import tpu as pltpu
from jax.sharding import Mesh, PartitionSpec as P

HD = 64
PAGE = 16
MAXP = 16
CONTEXT = 256


EPSILON = 1e-05
RESIDUAL_MULT = 0.22
SCORE_MULT = 0.015625
ROPE_BASE = 10000000.0


def normalize(values, gain):
    mean_square = jnp.mean(values * values, axis=-1, keepdims=True)
    return values * lax.rsqrt(mean_square + EPSILON) * gain


def rotary(values, positions):
    dim = values.shape[-1]
    half = dim // 2
    freq = jnp.power(ROPE_BASE, -2.0 * jnp.arange(half, dtype=jnp.int32).astype(jnp.float32) / dim)
    angle = positions.astype(jnp.float32)[:, :, None] * freq
    cosine = jnp.cos(angle)[:, :, None, :]
    sine = jnp.sin(angle)[:, :, None, :]
    first = values[..., :half].astype(jnp.float32)
    second = values[..., half:].astype(jnp.float32)
    return jnp.concatenate(
        [first * cosine - second * sine, second * cosine + first * sine], axis=-1
    )


def source_layout(owner_block, peers, pair_rows):
    row_count = owner_block.shape[0]
    owners = jnp.arange(peers, dtype=jnp.int32)
    member = owner_block[None, :] == owners[:, None]
    counts = jnp.sum(member.astype(jnp.int32), axis=1)
    row_ids = jnp.arange(row_count, dtype=jnp.int32)
    starts = jnp.min(jnp.where(member, row_ids[None, :], row_count), axis=1)
    slots = jnp.arange(pair_rows, dtype=jnp.int32)
    gather_rows = jnp.where(
        slots[None, :] < counts[:, None], starts[:, None] + slots[None, :], row_count
    )
    row_start = jnp.sum(jnp.where(member, starts[:, None], 0), axis=0)
    back_rows = owner_block * pair_rows + (row_ids - row_start)
    return (gather_rows.reshape(-1), back_rows)


def attention_kernel(table_ref, prior_ref, len_ref, q_ref, k_ref, v_ref, ck_ref, cv_ref,
                     out_ref, nk_ref, nv_ref, kbuf, vbuf):
    sources, pair_rows, qcols = q_ref.shape
    kcols = k_ref.shape[-1]
    kv_heads = kcols // HD
    group = qcols // kcols

    def per_source(s, carry):
        prior = prior_ref[s]
        length = len_ref[s]
        for i in range(MAXP):
            page = table_ref[s * MAXP + i]
            kbuf[i * PAGE:(i + 1) * PAGE, :] = ck_ref[page]
            vbuf[i * PAGE:(i + 1) * PAGE, :] = cv_ref[page]
        j_col = lax.broadcasted_iota(jnp.int32, (CONTEXT, pair_rows), 0)
        t_row = lax.broadcasted_iota(jnp.int32, (CONTEXT, pair_rows), 1)
        select = jnp.logical_and(j_col == prior + t_row, t_row < length).astype(jnp.bfloat16)
        j_only = lax.broadcasted_iota(jnp.int32, (CONTEXT, kcols), 0)
        fresh = jnp.logical_and(j_only >= prior, j_only < prior + length)
        k_new = jnp.dot(select, k_ref[s], preferred_element_type=jnp.float32).astype(jnp.bfloat16)
        v_new = jnp.dot(select, v_ref[s], preferred_element_type=jnp.float32).astype(jnp.bfloat16)
        keys = jnp.where(fresh, k_new, kbuf[...])
        values = jnp.where(fresh, v_new, vbuf[...])
        for i in range(MAXP):
            page = table_ref[s * MAXP + i]
            nk_ref[page] = keys[i * PAGE:(i + 1) * PAGE, :]
            nv_ref[page] = values[i * PAGE:(i + 1) * PAGE, :]
        q_all = q_ref[s]
        rows = group * pair_rows
        r_idx = lax.broadcasted_iota(jnp.int32, (rows, CONTEXT), 0)
        j_idx = lax.broadcasted_iota(jnp.int32, (rows, CONTEXT), 1)
        allowed = j_idx <= prior + r_idx % pair_rows
        for h in range(kv_heads):
            q_h = jnp.concatenate(
                [q_all[:, (h * group + g) * HD:(h * group + g + 1) * HD] for g in range(group)],
                axis=0,
            )
            k_h = keys[:, h * HD:(h + 1) * HD]
            v_h = values[:, h * HD:(h + 1) * HD]
            scores = lax.dot_general(
                q_h, k_h, (((1,), (1,)), ((), ())), preferred_element_type=jnp.float32
            ) * SCORE_MULT
            scores = jnp.where(allowed, scores, -jnp.inf)
            top = jnp.max(scores, axis=-1, keepdims=True)
            weights = jnp.exp(scores - top)
            probs = (weights / jnp.sum(weights, axis=-1, keepdims=True)).astype(jnp.bfloat16)
            mixed = jnp.dot(probs, v_h, preferred_element_type=jnp.float32).astype(jnp.bfloat16)
            for g in range(group):
                c = h * group + g
                out_ref[s, :, c * HD:(c + 1) * HD] = mixed[g * pair_rows:(g + 1) * pair_rows, :]
        return carry

    lax.fori_loop(0, sources, per_source, 0)


def owner_attention(query_in, key_in, value_in, cache_keys, cache_values, lengths, priors, table):
    sources, pair_rows, qcols = query_in.shape
    kcols = key_in.shape[-1]
    kv_heads = kcols // HD
    slots = jnp.arange(pair_rows, dtype=jnp.int32)
    positions = priors[:, None] + slots[None, :]
    query_rot = rotary(query_in.reshape(sources, pair_rows, qcols // HD, HD), positions).astype(
        jnp.bfloat16
    ).reshape(sources, pair_rows, qcols)
    key_rot = rotary(key_in.reshape(sources, pair_rows, kv_heads, HD), positions).astype(
        jnp.bfloat16
    ).reshape(sources, pair_rows, kcols)
    pool_pages = cache_keys.shape[0]
    smem = pl.BlockSpec(memory_space=pltpu.SMEM)
    vmem = pl.BlockSpec(memory_space=pltpu.VMEM)
    return pl.pallas_call(
        attention_kernel,
        out_shape=(
            jax.ShapeDtypeStruct((sources, pair_rows, qcols), jnp.bfloat16),
            jax.ShapeDtypeStruct(cache_keys.shape, cache_keys.dtype),
            jax.ShapeDtypeStruct(cache_values.shape, cache_values.dtype),
        ),
        in_specs=[smem, smem, smem, vmem, vmem, vmem, vmem, vmem],
        out_specs=(vmem, vmem, vmem),
        scratch_shapes=[
            pltpu.VMEM((CONTEXT, kcols), jnp.bfloat16),
            pltpu.VMEM((CONTEXT, kcols), jnp.bfloat16),
        ],
        compiler_params=pltpu.CompilerParams(vmem_limit_bytes=48 * 1024 * 1024),
    )(table, priors, lengths, query_rot, key_rot, value_in, cache_keys, cache_values)


def body(
    hidden_in,
    attn_gain,
    mlp_gain,
    w_query,
    w_key,
    w_value,
    w_out,
    w_gate,
    w_up,
    w_down,
    cache_k,
    cache_v,
    owner_of_row,
    new_len,
    prior_len,
    page_table,
):
    peers = lax.axis_size(REQ)
    groups = lax.axis_size("grp")
    row_count = hidden_in.shape[0]
    pair_rows = 2 * row_count // peers
    quarter = row_count // groups
    group_index = lax.axis_index("grp")
    gate_w = lax.all_gather(w_gate, "ry", axis=1, tiled=True)
    up_w = lax.all_gather(w_up, "ry", axis=1, tiled=True)
    down_w = lax.all_gather(w_down, "ry", axis=0, tiled=True)
    normed = normalize(hidden_in.astype(jnp.float32), attn_gain).astype(jnp.bfloat16)
    qcols = w_query.shape[1]
    kcols = w_key.shape[1]
    query_rows = jnp.dot(normed, w_query, preferred_element_type=jnp.float32).astype(jnp.bfloat16)
    key_rows = jnp.dot(normed, w_key, preferred_element_type=jnp.float32).astype(jnp.bfloat16)
    value_rows = jnp.dot(normed, w_value, preferred_element_type=jnp.float32).astype(jnp.bfloat16)
    qkv_rows = jnp.concatenate([query_rows, key_rows, value_rows], axis=1)
    gather_rows, back_rows = source_layout(owner_of_row, peers, pair_rows)
    send_qkv = jnp.take(qkv_rows, gather_rows, axis=0, mode="fill", fill_value=0).reshape(
        peers, pair_rows, -1
    )
    recv_qkv = lax.all_to_all(send_qkv, REQ, split_axis=0, concat_axis=0, tiled=True)
    recv_query = recv_qkv[..., :qcols]
    recv_key = recv_qkv[..., qcols : qcols + kcols]
    recv_value = recv_qkv[..., qcols + kcols :]
    mixed, keys_out, values_out = owner_attention(
        recv_query, recv_key, recv_value, cache_k, cache_v, new_len[0], prior_len[0], page_table[0]
    )
    gate_w, up_w, down_w, mixed = lax.optimization_barrier((gate_w, up_w, down_w, mixed))
    returned = lax.all_to_all(mixed, REQ, split_axis=0, concat_axis=0, tiled=True)
    attn_rows = jnp.take(returned.reshape(peers * pair_rows, -1), back_rows, axis=0)
    projected = jnp.dot(attn_rows, w_out, preferred_element_type=jnp.float32)
    attn_part = lax.psum_scatter(
        projected.astype(jnp.bfloat16), "grp", scatter_dimension=0, tiled=True
    ).astype(jnp.float32)
    own_rows = lax.dynamic_slice_in_dim(hidden_in, group_index * quarter, quarter, 0).astype(
        jnp.float32
    )
    residual = own_rows + RESIDUAL_MULT * attn_part
    mlp_in = normalize(residual, mlp_gain).astype(jnp.bfloat16)
    piece = lax.all_gather(mlp_in, "rzc", axis=0, tiled=True)
    gate = jnp.dot(piece, gate_w, preferred_element_type=jnp.float32)
    upper = jnp.dot(piece, up_w, preferred_element_type=jnp.float32)
    hidden = (jax.nn.silu(gate) * upper).astype(jnp.bfloat16)
    down = lax.psum_scatter(
        jnp.dot(hidden, down_w, preferred_element_type=jnp.float32).astype(jnp.bfloat16),
        "rzc",
        scatter_dimension=0,
        tiled=True,
    ).astype(jnp.float32)
    layer_out = (residual + RESIDUAL_MULT * down).astype(jnp.bfloat16)
    return (layer_out, keys_out, values_out)


REQ = ("ry", "rzc")


def solution(mesh):
    req_size = mesh.shape["req"]
    major = 4
    inner = Mesh(
        mesh.devices.reshape(major, req_size // major, mesh.shape["grp"]), ("ry", "rzc", "grp")
    )
    in_specs = (
        P(REQ, None),
        P(),
        P(),
        P(None, "grp"),
        P(None, "grp"),
        P(None, "grp"),
        P("grp", None),
        P(None, REQ),
        P(None, REQ),
        P(REQ, None),
        P(REQ, None, "grp"),
        P(REQ, None, "grp"),
        P(REQ),
        P(REQ, None),
        P(REQ, None),
        P(REQ, None),
    )
    out_specs = (P(REQ + ("grp",), None), P(REQ, None, "grp"), P(REQ, None, "grp"))
    return jax.shard_map(body, mesh=inner, in_specs=in_specs, out_specs=out_specs, check_vma=False)
```

```python
import jax
import jax.numpy as jnp
from jax import lax
from jax.experimental import pallas as pl
from jax.experimental.pallas import tpu as pltpu
from jax.sharding import Mesh, PartitionSpec as P

HD = 64
PAGE = 16
MAXP = 16
CONTEXT = 256


EPSILON = 1e-05
RESIDUAL_MULT = 0.22
SCORE_MULT = 0.015625
ROPE_BASE = 10000000.0


def normalize(values, gain):
    mean_square = jnp.mean(values * values, axis=-1, keepdims=True)
    return values * lax.rsqrt(mean_square + EPSILON) * gain


def rotary(values, positions):
    dim = values.shape[-1]
    half = dim // 2
    freq = jnp.power(ROPE_BASE, -2.0 * jnp.arange(half, dtype=jnp.int32).astype(jnp.float32) / dim)
    angle = positions.astype(jnp.float32)[:, :, None] * freq
    cosine = jnp.cos(angle)[:, :, None, :]
    sine = jnp.sin(angle)[:, :, None, :]
    first = values[..., :half].astype(jnp.float32)
    second = values[..., half:].astype(jnp.float32)
    return jnp.concatenate(
        [first * cosine - second * sine, second * cosine + first * sine], axis=-1
    )


def source_layout(owner_block, peers, pair_rows):
    row_count = owner_block.shape[0]
    owners = jnp.arange(peers, dtype=jnp.int32)
    member = owner_block[None, :] == owners[:, None]
    counts = jnp.sum(member.astype(jnp.int32), axis=1)
    row_ids = jnp.arange(row_count, dtype=jnp.int32)
    starts = jnp.min(jnp.where(member, row_ids[None, :], row_count), axis=1)
    slots = jnp.arange(pair_rows, dtype=jnp.int32)
    gather_rows = jnp.where(
        slots[None, :] < counts[:, None], starts[:, None] + slots[None, :], row_count
    )
    row_start = jnp.sum(jnp.where(member, starts[:, None], 0), axis=0)
    back_rows = owner_block * pair_rows + (row_ids - row_start)
    return (gather_rows.reshape(-1), back_rows)


def attention_kernel(table_ref, prior_ref, len_ref, q_ref, k_ref, v_ref, ck_ref, cv_ref,
                     out_ref, nk_ref, nv_ref, kbuf, vbuf):
    sources, pair_rows, qcols = q_ref.shape
    kcols = k_ref.shape[-1]
    kv_heads = kcols // HD
    group = qcols // kcols

    def per_source(s, carry):
        prior = prior_ref[s]
        length = len_ref[s]
        for i in range(MAXP):
            page = table_ref[s * MAXP + i]
            kbuf[i * PAGE:(i + 1) * PAGE, :] = ck_ref[page]
            vbuf[i * PAGE:(i + 1) * PAGE, :] = cv_ref[page]
        j_col = lax.broadcasted_iota(jnp.int32, (CONTEXT, pair_rows), 0)
        t_row = lax.broadcasted_iota(jnp.int32, (CONTEXT, pair_rows), 1)
        select = jnp.logical_and(j_col == prior + t_row, t_row < length).astype(jnp.bfloat16)
        j_only = lax.broadcasted_iota(jnp.int32, (CONTEXT, kcols), 0)
        fresh = jnp.logical_and(j_only >= prior, j_only < prior + length)
        k_new = jnp.dot(select, k_ref[s], preferred_element_type=jnp.float32).astype(jnp.bfloat16)
        v_new = jnp.dot(select, v_ref[s], preferred_element_type=jnp.float32).astype(jnp.bfloat16)
        keys = jnp.where(fresh, k_new, kbuf[...])
        values = jnp.where(fresh, v_new, vbuf[...])
        for i in range(MAXP):
            page = table_ref[s * MAXP + i]
            nk_ref[page] = keys[i * PAGE:(i + 1) * PAGE, :]
            nv_ref[page] = values[i * PAGE:(i + 1) * PAGE, :]
        q_all = q_ref[s]
        rows = group * pair_rows
        r_idx = lax.broadcasted_iota(jnp.int32, (rows, CONTEXT), 0)
        j_idx = lax.broadcasted_iota(jnp.int32, (rows, CONTEXT), 1)
        allowed = j_idx <= prior + r_idx % pair_rows
        for h in range(kv_heads):
            q_h = jnp.concatenate(
                [q_all[:, (h * group + g) * HD:(h * group + g + 1) * HD] for g in range(group)],
                axis=0,
            )
            k_h = keys[:, h * HD:(h + 1) * HD]
            v_h = values[:, h * HD:(h + 1) * HD]
            scores = lax.dot_general(
                q_h, k_h, (((1,), (1,)), ((), ())), preferred_element_type=jnp.float32
            ) * SCORE_MULT
            scores = jnp.where(allowed, scores, -jnp.inf)
            top = jnp.max(scores, axis=-1, keepdims=True)
            weights = jnp.exp(scores - top)
            probs = (weights / jnp.sum(weights, axis=-1, keepdims=True)).astype(jnp.bfloat16)
            mixed = jnp.dot(probs, v_h, preferred_element_type=jnp.float32).astype(jnp.bfloat16)
            for g in range(group):
                c = h * group + g
                out_ref[s, :, c * HD:(c + 1) * HD] = mixed[g * pair_rows:(g + 1) * pair_rows, :]
        return carry

    lax.fori_loop(0, sources, per_source, 0)


def owner_attention(query_in, key_in, value_in, cache_keys, cache_values, lengths, priors, table):
    sources, pair_rows, qcols = query_in.shape
    kcols = key_in.shape[-1]
    kv_heads = kcols // HD
    slots = jnp.arange(pair_rows, dtype=jnp.int32)
    positions = priors[:, None] + slots[None, :]
    query_rot = rotary(query_in.reshape(sources, pair_rows, qcols // HD, HD), positions).astype(
        jnp.bfloat16
    ).reshape(sources, pair_rows, qcols)
    key_rot = rotary(key_in.reshape(sources, pair_rows, kv_heads, HD), positions).astype(
        jnp.bfloat16
    ).reshape(sources, pair_rows, kcols)
    pool_pages = cache_keys.shape[0]
    smem = pl.BlockSpec(memory_space=pltpu.SMEM)
    vmem = pl.BlockSpec(memory_space=pltpu.VMEM)
    return pl.pallas_call(
        attention_kernel,
        out_shape=(
            jax.ShapeDtypeStruct((sources, pair_rows, qcols), jnp.bfloat16),
            jax.ShapeDtypeStruct(cache_keys.shape, cache_keys.dtype),
            jax.ShapeDtypeStruct(cache_values.shape, cache_values.dtype),
        ),
        in_specs=[smem, smem, smem, vmem, vmem, vmem, vmem, vmem],
        out_specs=(vmem, vmem, vmem),
        scratch_shapes=[
            pltpu.VMEM((CONTEXT, kcols), jnp.bfloat16),
            pltpu.VMEM((CONTEXT, kcols), jnp.bfloat16),
        ],
        compiler_params=pltpu.CompilerParams(vmem_limit_bytes=48 * 1024 * 1024),
    )(table, priors, lengths, query_rot, key_rot, value_in, cache_keys, cache_values)


def body(
    hidden_in,
    attn_gain,
    mlp_gain,
    w_query,
    w_key,
    w_value,
    w_out,
    w_gate,
    w_up,
    w_down,
    cache_k,
    cache_v,
    owner_of_row,
    new_len,
    prior_len,
    page_table,
):
    peers = lax.axis_size(REQ)
    groups = lax.axis_size("grp")
    row_count = hidden_in.shape[0]
    pair_rows = 2 * row_count // peers
    quarter = row_count // groups
    group_index = lax.axis_index("grp")
    gate_w = lax.all_gather(w_gate, "rc", axis=1, tiled=True)
    up_w = lax.all_gather(w_up, "rc", axis=1, tiled=True)
    down_w = lax.all_gather(w_down, "rc", axis=0, tiled=True)
    normed = normalize(hidden_in.astype(jnp.float32), attn_gain).astype(jnp.bfloat16)
    qcols = w_query.shape[1]
    kcols = w_key.shape[1]
    query_rows = jnp.dot(normed, w_query, preferred_element_type=jnp.float32).astype(jnp.bfloat16)
    key_rows = jnp.dot(normed, w_key, preferred_element_type=jnp.float32).astype(jnp.bfloat16)
    value_rows = jnp.dot(normed, w_value, preferred_element_type=jnp.float32).astype(jnp.bfloat16)
    qkv_rows = jnp.concatenate([query_rows, key_rows, value_rows], axis=1)
    gather_rows, back_rows = source_layout(owner_of_row, peers, pair_rows)
    send_qkv = jnp.take(qkv_rows, gather_rows, axis=0, mode="fill", fill_value=0).reshape(
        peers, pair_rows, -1
    )
    recv_qkv = lax.all_to_all(send_qkv, REQ, split_axis=0, concat_axis=0, tiled=True)
    recv_query = recv_qkv[..., :qcols]
    recv_key = recv_qkv[..., qcols : qcols + kcols]
    recv_value = recv_qkv[..., qcols + kcols :]
    mixed, keys_out, values_out = owner_attention(
        recv_query, recv_key, recv_value, cache_k, cache_v, new_len[0], prior_len[0], page_table[0]
    )
    gate_w, up_w, down_w, mixed = lax.optimization_barrier((gate_w, up_w, down_w, mixed))
    returned = lax.all_to_all(mixed, REQ, split_axis=0, concat_axis=0, tiled=True)
    attn_rows = jnp.take(returned.reshape(peers * pair_rows, -1), back_rows, axis=0)
    projected = jnp.dot(attn_rows, w_out, preferred_element_type=jnp.float32)
    attn_part = lax.psum_scatter(
        projected.astype(jnp.bfloat16), "grp", scatter_dimension=0, tiled=True
    ).astype(jnp.float32)
    own_rows = lax.dynamic_slice_in_dim(hidden_in, group_index * quarter, quarter, 0).astype(
        jnp.float32
    )
    residual = own_rows + RESIDUAL_MULT * attn_part
    mlp_in = normalize(residual, mlp_gain).astype(jnp.bfloat16)
    piece = lax.all_gather(mlp_in, "ryz", axis=0, tiled=True)
    gate = jnp.dot(piece, gate_w, preferred_element_type=jnp.float32)
    upper = jnp.dot(piece, up_w, preferred_element_type=jnp.float32)
    hidden = (jax.nn.silu(gate) * upper).astype(jnp.bfloat16)
    down = lax.psum_scatter(
        jnp.dot(hidden, down_w, preferred_element_type=jnp.float32).astype(jnp.bfloat16),
        "ryz",
        scatter_dimension=0,
        tiled=True,
    ).astype(jnp.float32)
    layer_out = (residual + RESIDUAL_MULT * down).astype(jnp.bfloat16)
    return (layer_out, keys_out, values_out)


REQ = ("ryz", "rc")


def solution(mesh):
    req_size = mesh.shape["req"]
    cores = 2
    inner = Mesh(
        mesh.devices.reshape(req_size // cores, cores, mesh.shape["grp"]), ("ryz", "rc", "grp")
    )
    in_specs = (
        P(REQ, None),
        P(),
        P(),
        P(None, "grp"),
        P(None, "grp"),
        P(None, "grp"),
        P("grp", None),
        P(None, REQ),
        P(None, REQ),
        P(REQ, None),
        P(REQ, None, "grp"),
        P(REQ, None, "grp"),
        P(REQ),
        P(REQ, None),
        P(REQ, None),
        P(REQ, None),
    )
    out_specs = (P(REQ + ("grp",), None), P(REQ, None, "grp"), P(REQ, None, "grp"))
    return jax.shard_map(body, mesh=inner, in_specs=in_specs, out_specs=out_specs, check_vma=False)
```

```python
import jax
import jax.numpy as jnp
from jax import lax
from jax.experimental import pallas as pl
from jax.experimental.pallas import tpu as pltpu
from jax.sharding import Mesh, PartitionSpec as P

HD = 64
PAGE = 16
MAXP = 16
CONTEXT = 256


EPSILON = 1e-05
RESIDUAL_MULT = 0.22
SCORE_MULT = 0.015625
ROPE_BASE = 10000000.0


def normalize(values, gain):
    mean_square = jnp.mean(values * values, axis=-1, keepdims=True)
    return values * lax.rsqrt(mean_square + EPSILON) * gain


def rotary(values, positions):
    dim = values.shape[-1]
    half = dim // 2
    freq = jnp.power(ROPE_BASE, -2.0 * jnp.arange(half, dtype=jnp.int32).astype(jnp.float32) / dim)
    angle = positions.astype(jnp.float32)[:, :, None] * freq
    cosine = jnp.cos(angle)[:, :, None, :]
    sine = jnp.sin(angle)[:, :, None, :]
    first = values[..., :half].astype(jnp.float32)
    second = values[..., half:].astype(jnp.float32)
    return jnp.concatenate(
        [first * cosine - second * sine, second * cosine + first * sine], axis=-1
    )


def source_layout(owner_block, peers, pair_rows):
    row_count = owner_block.shape[0]
    owners = jnp.arange(peers, dtype=jnp.int32)
    member = owner_block[None, :] == owners[:, None]
    counts = jnp.sum(member.astype(jnp.int32), axis=1)
    row_ids = jnp.arange(row_count, dtype=jnp.int32)
    starts = jnp.min(jnp.where(member, row_ids[None, :], row_count), axis=1)
    slots = jnp.arange(pair_rows, dtype=jnp.int32)
    gather_rows = jnp.where(
        slots[None, :] < counts[:, None], starts[:, None] + slots[None, :], row_count
    )
    row_start = jnp.sum(jnp.where(member, starts[:, None], 0), axis=0)
    back_rows = owner_block * pair_rows + (row_ids - row_start)
    return (gather_rows.reshape(-1), back_rows)


def attention_kernel(table_ref, prior_ref, len_ref, q_ref, k_ref, v_ref, ck_ref, cv_ref,
                     out_ref, nk_ref, nv_ref, kbuf, vbuf):
    sources, pair_rows, qcols = q_ref.shape
    kcols = k_ref.shape[-1]
    kv_heads = kcols // HD
    group = qcols // kcols

    def per_source(s, carry):
        prior = prior_ref[s]
        length = len_ref[s]
        for i in range(MAXP):
            page = table_ref[s * MAXP + i]
            kbuf[i * PAGE:(i + 1) * PAGE, :] = ck_ref[page]
            vbuf[i * PAGE:(i + 1) * PAGE, :] = cv_ref[page]
        j_col = lax.broadcasted_iota(jnp.int32, (CONTEXT, pair_rows), 0)
        t_row = lax.broadcasted_iota(jnp.int32, (CONTEXT, pair_rows), 1)
        select = jnp.logical_and(j_col == prior + t_row, t_row < length).astype(jnp.bfloat16)
        j_only = lax.broadcasted_iota(jnp.int32, (CONTEXT, kcols), 0)
        fresh = jnp.logical_and(j_only >= prior, j_only < prior + length)
        k_new = jnp.dot(select, k_ref[s], preferred_element_type=jnp.float32).astype(jnp.bfloat16)
        v_new = jnp.dot(select, v_ref[s], preferred_element_type=jnp.float32).astype(jnp.bfloat16)
        keys = jnp.where(fresh, k_new, kbuf[...])
        values = jnp.where(fresh, v_new, vbuf[...])
        for i in range(MAXP):
            page = table_ref[s * MAXP + i]
            nk_ref[page] = keys[i * PAGE:(i + 1) * PAGE, :]
            nv_ref[page] = values[i * PAGE:(i + 1) * PAGE, :]
        q_all = q_ref[s]
        rows = group * pair_rows
        r_idx = lax.broadcasted_iota(jnp.int32, (rows, CONTEXT), 0)
        j_idx = lax.broadcasted_iota(jnp.int32, (rows, CONTEXT), 1)
        allowed = j_idx <= prior + r_idx % pair_rows
        for h in range(kv_heads):
            q_h = jnp.concatenate(
                [q_all[:, (h * group + g) * HD:(h * group + g + 1) * HD] for g in range(group)],
                axis=0,
            )
            k_h = keys[:, h * HD:(h + 1) * HD]
            v_h = values[:, h * HD:(h + 1) * HD]
            scores = lax.dot_general(
                q_h, k_h, (((1,), (1,)), ((), ())), preferred_element_type=jnp.float32
            ) * SCORE_MULT
            scores = jnp.where(allowed, scores, -jnp.inf)
            top = jnp.max(scores, axis=-1, keepdims=True)
            weights = jnp.exp(scores - top)
            probs = (weights / jnp.sum(weights, axis=-1, keepdims=True)).astype(jnp.bfloat16)
            mixed = jnp.dot(probs, v_h, preferred_element_type=jnp.float32).astype(jnp.bfloat16)
            for g in range(group):
                c = h * group + g
                out_ref[s, :, c * HD:(c + 1) * HD] = mixed[g * pair_rows:(g + 1) * pair_rows, :]
        return carry

    lax.fori_loop(0, sources, per_source, 0)


def owner_attention(query_in, key_in, value_in, cache_keys, cache_values, lengths, priors, table):
    sources, pair_rows, qcols = query_in.shape
    kcols = key_in.shape[-1]
    kv_heads = kcols // HD
    slots = jnp.arange(pair_rows, dtype=jnp.int32)
    positions = priors[:, None] + slots[None, :]
    query_rot = rotary(query_in.reshape(sources, pair_rows, qcols // HD, HD), positions).astype(
        jnp.bfloat16
    ).reshape(sources, pair_rows, qcols)
    key_rot = rotary(key_in.reshape(sources, pair_rows, kv_heads, HD), positions).astype(
        jnp.bfloat16
    ).reshape(sources, pair_rows, kcols)
    pool_pages = cache_keys.shape[0]
    smem = pl.BlockSpec(memory_space=pltpu.SMEM)
    vmem = pl.BlockSpec(memory_space=pltpu.VMEM)
    return pl.pallas_call(
        attention_kernel,
        out_shape=(
            jax.ShapeDtypeStruct((sources, pair_rows, qcols), jnp.bfloat16),
            jax.ShapeDtypeStruct(cache_keys.shape, cache_keys.dtype),
            jax.ShapeDtypeStruct(cache_values.shape, cache_values.dtype),
        ),
        in_specs=[smem, smem, smem, vmem, vmem, vmem, vmem, vmem],
        out_specs=(vmem, vmem, vmem),
        scratch_shapes=[
            pltpu.VMEM((CONTEXT, kcols), jnp.bfloat16),
            pltpu.VMEM((CONTEXT, kcols), jnp.bfloat16),
        ],
        compiler_params=pltpu.CompilerParams(vmem_limit_bytes=48 * 1024 * 1024),
    )(table, priors, lengths, query_rot, key_rot, value_in, cache_keys, cache_values)


def body(
    hidden_in,
    attn_gain,
    mlp_gain,
    w_query,
    w_key,
    w_value,
    w_out,
    w_gate,
    w_up,
    w_down,
    cache_k,
    cache_v,
    owner_of_row,
    new_len,
    prior_len,
    page_table,
):
    peers = lax.axis_size(REQ)
    groups = lax.axis_size("grp")
    row_count = hidden_in.shape[0]
    pair_rows = 2 * row_count // peers
    quarter = row_count // groups
    group_index = lax.axis_index("grp")
    ring = lax.axis_size("ry")
    gate_up = jnp.concatenate([w_gate, w_up], axis=1)
    gate_up_parts = [gate_up]
    down_parts = [w_down]
    for shift in range(1, ring):
        perm = [(i, (i + shift) % ring) for i in range(ring)]
        gate_up_parts.append(lax.ppermute(gate_up, "ry", perm))
        down_parts.append(lax.ppermute(w_down, "ry", perm))
    units = w_gate.shape[1]
    gate_w = jnp.concatenate([part[:, :units] for part in gate_up_parts], axis=1)
    up_w = jnp.concatenate([part[:, units:] for part in gate_up_parts], axis=1)
    down_w = jnp.concatenate(down_parts, axis=0)
    normed = normalize(hidden_in.astype(jnp.float32), attn_gain).astype(jnp.bfloat16)
    qcols = w_query.shape[1]
    kcols = w_key.shape[1]
    query_rows = jnp.dot(normed, w_query, preferred_element_type=jnp.float32).astype(jnp.bfloat16)
    key_rows = jnp.dot(normed, w_key, preferred_element_type=jnp.float32).astype(jnp.bfloat16)
    value_rows = jnp.dot(normed, w_value, preferred_element_type=jnp.float32).astype(jnp.bfloat16)
    qkv_rows = jnp.concatenate([query_rows, key_rows, value_rows], axis=1)
    gather_rows, back_rows = source_layout(owner_of_row, peers, pair_rows)
    send_qkv = jnp.take(qkv_rows, gather_rows, axis=0, mode="fill", fill_value=0).reshape(
        peers, pair_rows, -1
    )
    recv_qkv = lax.all_to_all(send_qkv, REQ, split_axis=0, concat_axis=0, tiled=True)
    recv_query = recv_qkv[..., :qcols]
    recv_key = recv_qkv[..., qcols : qcols + kcols]
    recv_value = recv_qkv[..., qcols + kcols :]
    mixed, keys_out, values_out = owner_attention(
        recv_query, recv_key, recv_value, cache_k, cache_v, new_len[0], prior_len[0], page_table[0]
    )
    returned = lax.all_to_all(mixed, REQ, split_axis=0, concat_axis=0, tiled=True)
    gate_w, up_w, down_w, returned = lax.optimization_barrier((gate_w, up_w, down_w, returned))
    attn_rows = jnp.take(returned.reshape(peers * pair_rows, -1), back_rows, axis=0)
    projected = jnp.dot(attn_rows, w_out, preferred_element_type=jnp.float32)
    attn_part = lax.psum_scatter(
        projected.astype(jnp.bfloat16), "grp", scatter_dimension=0, tiled=True
    ).astype(jnp.float32)
    own_rows = lax.dynamic_slice_in_dim(hidden_in, group_index * quarter, quarter, 0).astype(
        jnp.float32
    )
    residual = own_rows + RESIDUAL_MULT * attn_part
    mlp_in = normalize(residual, mlp_gain).astype(jnp.bfloat16)
    piece = lax.all_gather(mlp_in, "rzc", axis=0, tiled=True)
    gate = jnp.dot(piece, gate_w, preferred_element_type=jnp.float32)
    upper = jnp.dot(piece, up_w, preferred_element_type=jnp.float32)
    hidden = (jax.nn.silu(gate) * upper).astype(jnp.bfloat16)
    down = lax.psum_scatter(
        jnp.dot(hidden, down_w, preferred_element_type=jnp.float32).astype(jnp.bfloat16),
        "rzc",
        scatter_dimension=0,
        tiled=True,
    ).astype(jnp.float32)
    layer_out = (residual + RESIDUAL_MULT * down).astype(jnp.bfloat16)
    return (layer_out, keys_out, values_out)


REQ = ("ry", "rzc")


def solution(mesh):
    req_size = mesh.shape["req"]
    major = 4
    inner = Mesh(
        mesh.devices.reshape(major, req_size // major, mesh.shape["grp"]), ("ry", "rzc", "grp")
    )
    in_specs = (
        P(REQ, None),
        P(),
        P(),
        P(None, "grp"),
        P(None, "grp"),
        P(None, "grp"),
        P("grp", None),
        P(None, REQ),
        P(None, REQ),
        P(REQ, None),
        P(REQ, None, "grp"),
        P(REQ, None, "grp"),
        P(REQ),
        P(REQ, None),
        P(REQ, None),
        P(REQ, None),
    )
    out_specs = (P(REQ + ("grp",), None), P(REQ, None, "grp"), P(REQ, None, "grp"))
    return jax.shard_map(body, mesh=inner, in_specs=in_specs, out_specs=out_specs, check_vma=False)
```

```python
import jax
import jax.numpy as jnp
from jax import lax
from jax.experimental import pallas as pl
from jax.experimental.pallas import tpu as pltpu
from jax.sharding import Mesh, PartitionSpec as P

HD = 64
PAGE = 16
MAXP = 16
CONTEXT = 256


EPSILON = 1e-05
RESIDUAL_MULT = 0.22
SCORE_MULT = 0.015625
ROPE_BASE = 10000000.0


def normalize(values, gain):
    mean_square = jnp.mean(values * values, axis=-1, keepdims=True)
    return values * lax.rsqrt(mean_square + EPSILON) * gain


def rotary(values, positions):
    dim = values.shape[-1]
    half = dim // 2
    freq = jnp.power(ROPE_BASE, -2.0 * jnp.arange(half, dtype=jnp.int32).astype(jnp.float32) / dim)
    angle = positions.astype(jnp.float32)[:, :, None] * freq
    cosine = jnp.cos(angle)[:, :, None, :]
    sine = jnp.sin(angle)[:, :, None, :]
    first = values[..., :half].astype(jnp.float32)
    second = values[..., half:].astype(jnp.float32)
    return jnp.concatenate(
        [first * cosine - second * sine, second * cosine + first * sine], axis=-1
    )


def source_layout(owner_block, peers, pair_rows):
    row_count = owner_block.shape[0]
    owners = jnp.arange(peers, dtype=jnp.int32)
    member = owner_block[None, :] == owners[:, None]
    counts = jnp.sum(member.astype(jnp.int32), axis=1)
    row_ids = jnp.arange(row_count, dtype=jnp.int32)
    starts = jnp.min(jnp.where(member, row_ids[None, :], row_count), axis=1)
    slots = jnp.arange(pair_rows, dtype=jnp.int32)
    gather_rows = jnp.where(
        slots[None, :] < counts[:, None], starts[:, None] + slots[None, :], row_count
    )
    row_start = jnp.sum(jnp.where(member, starts[:, None], 0), axis=0)
    back_rows = owner_block * pair_rows + (row_ids - row_start)
    return (gather_rows.reshape(-1), back_rows)


def attention_kernel(table_ref, prior_ref, len_ref, q_ref, k_ref, v_ref, ck_ref, cv_ref,
                     out_ref, nk_ref, nv_ref, kbuf, vbuf):
    sources, pair_rows, qcols = q_ref.shape
    kcols = k_ref.shape[-1]
    kv_heads = kcols // HD
    group = qcols // kcols

    def per_source(s, carry):
        prior = prior_ref[s]
        length = len_ref[s]
        for i in range(MAXP):
            page = table_ref[s * MAXP + i]
            kbuf[i * PAGE:(i + 1) * PAGE, :] = ck_ref[page]
            vbuf[i * PAGE:(i + 1) * PAGE, :] = cv_ref[page]
        j_col = lax.broadcasted_iota(jnp.int32, (CONTEXT, pair_rows), 0)
        t_row = lax.broadcasted_iota(jnp.int32, (CONTEXT, pair_rows), 1)
        select = jnp.logical_and(j_col == prior + t_row, t_row < length).astype(jnp.bfloat16)
        j_only = lax.broadcasted_iota(jnp.int32, (CONTEXT, kcols), 0)
        fresh = jnp.logical_and(j_only >= prior, j_only < prior + length)
        k_new = jnp.dot(select, k_ref[s], preferred_element_type=jnp.float32).astype(jnp.bfloat16)
        v_new = jnp.dot(select, v_ref[s], preferred_element_type=jnp.float32).astype(jnp.bfloat16)
        keys = jnp.where(fresh, k_new, kbuf[...])
        values = jnp.where(fresh, v_new, vbuf[...])
        for i in range(MAXP):
            page = table_ref[s * MAXP + i]
            nk_ref[page] = keys[i * PAGE:(i + 1) * PAGE, :]
            nv_ref[page] = values[i * PAGE:(i + 1) * PAGE, :]
        q_all = q_ref[s]
        rows = group * pair_rows
        r_idx = lax.broadcasted_iota(jnp.int32, (rows, CONTEXT), 0)
        j_idx = lax.broadcasted_iota(jnp.int32, (rows, CONTEXT), 1)
        allowed = j_idx <= prior + r_idx % pair_rows
        for h in range(kv_heads):
            q_h = jnp.concatenate(
                [q_all[:, (h * group + g) * HD:(h * group + g + 1) * HD] for g in range(group)],
                axis=0,
            )
            k_h = keys[:, h * HD:(h + 1) * HD]
            v_h = values[:, h * HD:(h + 1) * HD]
            scores = lax.dot_general(
                q_h, k_h, (((1,), (1,)), ((), ())), preferred_element_type=jnp.float32
            ) * SCORE_MULT
            scores = jnp.where(allowed, scores, -jnp.inf)
            top = jnp.max(scores, axis=-1, keepdims=True)
            weights = jnp.exp(scores - top)
            probs = (weights / jnp.sum(weights, axis=-1, keepdims=True)).astype(jnp.bfloat16)
            mixed = jnp.dot(probs, v_h, preferred_element_type=jnp.float32).astype(jnp.bfloat16)
            for g in range(group):
                c = h * group + g
                out_ref[s, :, c * HD:(c + 1) * HD] = mixed[g * pair_rows:(g + 1) * pair_rows, :]
        return carry

    lax.fori_loop(0, sources, per_source, 0)


def owner_attention(query_in, key_in, value_in, cache_keys, cache_values, lengths, priors, table):
    sources, pair_rows, qcols = query_in.shape
    kcols = key_in.shape[-1]
    kv_heads = kcols // HD
    slots = jnp.arange(pair_rows, dtype=jnp.int32)
    positions = priors[:, None] + slots[None, :]
    query_rot = rotary(query_in.reshape(sources, pair_rows, qcols // HD, HD), positions).astype(
        jnp.bfloat16
    ).reshape(sources, pair_rows, qcols)
    key_rot = rotary(key_in.reshape(sources, pair_rows, kv_heads, HD), positions).astype(
        jnp.bfloat16
    ).reshape(sources, pair_rows, kcols)
    pool_pages = cache_keys.shape[0]
    smem = pl.BlockSpec(memory_space=pltpu.SMEM)
    vmem = pl.BlockSpec(memory_space=pltpu.VMEM)
    return pl.pallas_call(
        attention_kernel,
        out_shape=(
            jax.ShapeDtypeStruct((sources, pair_rows, qcols), jnp.bfloat16),
            jax.ShapeDtypeStruct(cache_keys.shape, cache_keys.dtype),
            jax.ShapeDtypeStruct(cache_values.shape, cache_values.dtype),
        ),
        in_specs=[smem, smem, smem, vmem, vmem, vmem, vmem, vmem],
        out_specs=(vmem, vmem, vmem),
        scratch_shapes=[
            pltpu.VMEM((CONTEXT, kcols), jnp.bfloat16),
            pltpu.VMEM((CONTEXT, kcols), jnp.bfloat16),
        ],
        compiler_params=pltpu.CompilerParams(vmem_limit_bytes=48 * 1024 * 1024),
    )(table, priors, lengths, query_rot, key_rot, value_in, cache_keys, cache_values)


def body(
    hidden_in,
    attn_gain,
    mlp_gain,
    w_query,
    w_key,
    w_value,
    w_out,
    w_gate,
    w_up,
    w_down,
    cache_k,
    cache_v,
    owner_of_row,
    new_len,
    prior_len,
    page_table,
):
    peers = lax.axis_size(REQ)
    groups = lax.axis_size("grp")
    row_count = hidden_in.shape[0]
    pair_rows = 2 * row_count // peers
    quarter = row_count // groups
    group_index = lax.axis_index("grp")
    gate_w = lax.all_gather(w_gate, "ry", axis=1, tiled=True)
    up_w = lax.all_gather(w_up, "ry", axis=1, tiled=True)
    ring = lax.axis_size("ry")
    down_parts = [w_down] + [
        lax.ppermute(w_down, "ry", [(i, (i + shift) % ring) for i in range(ring)])
        for shift in range(1, ring)
    ]
    part_at = (lax.axis_index("ry") - jnp.arange(ring, dtype=jnp.int32)) % ring
    down_w = jnp.take(jnp.stack(down_parts), part_at, axis=0).reshape(-1, w_down.shape[1])
    normed = normalize(hidden_in.astype(jnp.float32), attn_gain).astype(jnp.bfloat16)
    qcols = w_query.shape[1]
    kcols = w_key.shape[1]
    query_rows = jnp.dot(normed, w_query, preferred_element_type=jnp.float32).astype(jnp.bfloat16)
    key_rows = jnp.dot(normed, w_key, preferred_element_type=jnp.float32).astype(jnp.bfloat16)
    value_rows = jnp.dot(normed, w_value, preferred_element_type=jnp.float32).astype(jnp.bfloat16)
    qkv_rows = jnp.concatenate([query_rows, key_rows, value_rows], axis=1)
    gather_rows, back_rows = source_layout(owner_of_row, peers, pair_rows)
    send_qkv = jnp.take(qkv_rows, gather_rows, axis=0, mode="fill", fill_value=0).reshape(
        peers, pair_rows, -1
    )
    recv_qkv = lax.all_to_all(send_qkv, REQ, split_axis=0, concat_axis=0, tiled=True)
    recv_query = recv_qkv[..., :qcols]
    recv_key = recv_qkv[..., qcols : qcols + kcols]
    recv_value = recv_qkv[..., qcols + kcols :]
    mixed, keys_out, values_out = owner_attention(
        recv_query, recv_key, recv_value, cache_k, cache_v, new_len[0], prior_len[0], page_table[0]
    )
    gate_w, up_w, mixed = lax.optimization_barrier((gate_w, up_w, mixed))
    returned = lax.all_to_all(mixed, REQ, split_axis=0, concat_axis=0, tiled=True)
    attn_rows = jnp.take(returned.reshape(peers * pair_rows, -1), back_rows, axis=0)
    projected = jnp.dot(attn_rows, w_out, preferred_element_type=jnp.float32)
    attn_part = lax.psum_scatter(
        projected.astype(jnp.bfloat16), "grp", scatter_dimension=0, tiled=True
    ).astype(jnp.float32)
    own_rows = lax.dynamic_slice_in_dim(hidden_in, group_index * quarter, quarter, 0).astype(
        jnp.float32
    )
    residual = own_rows + RESIDUAL_MULT * attn_part
    mlp_in = normalize(residual, mlp_gain).astype(jnp.bfloat16)
    piece = lax.all_gather(mlp_in, "rzc", axis=0, tiled=True)
    down_w, piece = lax.optimization_barrier((down_w, piece))
    gate = jnp.dot(piece, gate_w, preferred_element_type=jnp.float32)
    upper = jnp.dot(piece, up_w, preferred_element_type=jnp.float32)
    hidden = (jax.nn.silu(gate) * upper).astype(jnp.bfloat16)
    down = lax.psum_scatter(
        jnp.dot(hidden, down_w, preferred_element_type=jnp.float32).astype(jnp.bfloat16),
        "rzc",
        scatter_dimension=0,
        tiled=True,
    ).astype(jnp.float32)
    layer_out = (residual + RESIDUAL_MULT * down).astype(jnp.bfloat16)
    return (layer_out, keys_out, values_out)


REQ = ("ry", "rzc")


def solution(mesh):
    req_size = mesh.shape["req"]
    major = 4
    inner = Mesh(
        mesh.devices.reshape(major, req_size // major, mesh.shape["grp"]), ("ry", "rzc", "grp")
    )
    in_specs = (
        P(REQ, None),
        P(),
        P(),
        P(None, "grp"),
        P(None, "grp"),
        P(None, "grp"),
        P("grp", None),
        P(None, REQ),
        P(None, REQ),
        P(REQ, None),
        P(REQ, None, "grp"),
        P(REQ, None, "grp"),
        P(REQ),
        P(REQ, None),
        P(REQ, None),
        P(REQ, None),
    )
    out_specs = (P(REQ + ("grp",), None), P(REQ, None, "grp"), P(REQ, None, "grp"))
    return jax.shard_map(body, mesh=inner, in_specs=in_specs, out_specs=out_specs, check_vma=False)
```

```python
import jax
import jax.numpy as jnp
from jax import lax
from jax.experimental import pallas as pl
from jax.experimental.pallas import tpu as pltpu
from jax.sharding import Mesh, PartitionSpec as P

HD = 64
PAGE = 16
MAXP = 16
CONTEXT = 256


EPSILON = 1e-05
RESIDUAL_MULT = 0.22
SCORE_MULT = 0.015625
ROPE_BASE = 10000000.0


def normalize(values, gain):
    mean_square = jnp.mean(values * values, axis=-1, keepdims=True)
    return values * lax.rsqrt(mean_square + EPSILON) * gain


def rotary(values, positions):
    dim = values.shape[-1]
    half = dim // 2
    freq = jnp.power(ROPE_BASE, -2.0 * jnp.arange(half, dtype=jnp.int32).astype(jnp.float32) / dim)
    angle = positions.astype(jnp.float32)[:, :, None] * freq
    cosine = jnp.cos(angle)[:, :, None, :]
    sine = jnp.sin(angle)[:, :, None, :]
    first = values[..., :half].astype(jnp.float32)
    second = values[..., half:].astype(jnp.float32)
    return jnp.concatenate(
        [first * cosine - second * sine, second * cosine + first * sine], axis=-1
    )


def source_layout(owner_block, peers, pair_rows):
    row_count = owner_block.shape[0]
    owners = jnp.arange(peers, dtype=jnp.int32)
    member = owner_block[None, :] == owners[:, None]
    counts = jnp.sum(member.astype(jnp.int32), axis=1)
    row_ids = jnp.arange(row_count, dtype=jnp.int32)
    starts = jnp.min(jnp.where(member, row_ids[None, :], row_count), axis=1)
    slots = jnp.arange(pair_rows, dtype=jnp.int32)
    gather_rows = jnp.where(
        slots[None, :] < counts[:, None], starts[:, None] + slots[None, :], row_count
    )
    row_start = jnp.sum(jnp.where(member, starts[:, None], 0), axis=0)
    back_rows = owner_block * pair_rows + (row_ids - row_start)
    return (gather_rows.reshape(-1), back_rows)


def attention_kernel(table_ref, prior_ref, len_ref, q_ref, k_ref, v_ref, ck_ref, cv_ref,
                     out_ref, nk_ref, nv_ref, kbuf, vbuf):
    sources, pair_rows, qcols = q_ref.shape
    kcols = k_ref.shape[-1]
    kv_heads = kcols // HD
    group = qcols // kcols

    def per_source(s, carry):
        prior = prior_ref[s]
        length = len_ref[s]
        for i in range(MAXP):
            page = table_ref[s * MAXP + i]
            kbuf[i * PAGE:(i + 1) * PAGE, :] = ck_ref[page]
            vbuf[i * PAGE:(i + 1) * PAGE, :] = cv_ref[page]
        j_col = lax.broadcasted_iota(jnp.int32, (CONTEXT, pair_rows), 0)
        t_row = lax.broadcasted_iota(jnp.int32, (CONTEXT, pair_rows), 1)
        select = jnp.logical_and(j_col == prior + t_row, t_row < length).astype(jnp.bfloat16)
        j_only = lax.broadcasted_iota(jnp.int32, (CONTEXT, kcols), 0)
        fresh = jnp.logical_and(j_only >= prior, j_only < prior + length)
        k_new = jnp.dot(select, k_ref[s], preferred_element_type=jnp.float32).astype(jnp.bfloat16)
        v_new = jnp.dot(select, v_ref[s], preferred_element_type=jnp.float32).astype(jnp.bfloat16)
        keys = jnp.where(fresh, k_new, kbuf[...])
        values = jnp.where(fresh, v_new, vbuf[...])
        for i in range(MAXP):
            page = table_ref[s * MAXP + i]
            nk_ref[page] = keys[i * PAGE:(i + 1) * PAGE, :]
            nv_ref[page] = values[i * PAGE:(i + 1) * PAGE, :]
        q_all = q_ref[s]
        rows = group * pair_rows
        r_idx = lax.broadcasted_iota(jnp.int32, (rows, CONTEXT), 0)
        j_idx = lax.broadcasted_iota(jnp.int32, (rows, CONTEXT), 1)
        allowed = j_idx <= prior + r_idx % pair_rows
        for h in range(kv_heads):
            q_h = jnp.concatenate(
                [q_all[:, (h * group + g) * HD:(h * group + g + 1) * HD] for g in range(group)],
                axis=0,
            )
            k_h = keys[:, h * HD:(h + 1) * HD]
            v_h = values[:, h * HD:(h + 1) * HD]
            scores = lax.dot_general(
                q_h, k_h, (((1,), (1,)), ((), ())), preferred_element_type=jnp.float32
            ) * SCORE_MULT
            scores = jnp.where(allowed, scores, -jnp.inf)
            top = jnp.max(scores, axis=-1, keepdims=True)
            weights = jnp.exp(scores - top)
            probs = (weights / jnp.sum(weights, axis=-1, keepdims=True)).astype(jnp.bfloat16)
            mixed = jnp.dot(probs, v_h, preferred_element_type=jnp.float32).astype(jnp.bfloat16)
            for g in range(group):
                c = h * group + g
                out_ref[s, :, c * HD:(c + 1) * HD] = mixed[g * pair_rows:(g + 1) * pair_rows, :]
        return carry

    lax.fori_loop(0, sources, per_source, 0)


def owner_attention(query_in, key_in, value_in, cache_keys, cache_values, lengths, priors, table):
    sources, pair_rows, qcols = query_in.shape
    kcols = key_in.shape[-1]
    kv_heads = kcols // HD
    slots = jnp.arange(pair_rows, dtype=jnp.int32)
    positions = priors[:, None] + slots[None, :]
    query_rot = rotary(query_in.reshape(sources, pair_rows, qcols // HD, HD), positions).astype(
        jnp.bfloat16
    ).reshape(sources, pair_rows, qcols)
    key_rot = rotary(key_in.reshape(sources, pair_rows, kv_heads, HD), positions).astype(
        jnp.bfloat16
    ).reshape(sources, pair_rows, kcols)
    pool_pages = cache_keys.shape[0]
    smem = pl.BlockSpec(memory_space=pltpu.SMEM)
    vmem = pl.BlockSpec(memory_space=pltpu.VMEM)
    return pl.pallas_call(
        attention_kernel,
        out_shape=(
            jax.ShapeDtypeStruct((sources, pair_rows, qcols), jnp.bfloat16),
            jax.ShapeDtypeStruct(cache_keys.shape, cache_keys.dtype),
            jax.ShapeDtypeStruct(cache_values.shape, cache_values.dtype),
        ),
        in_specs=[smem, smem, smem, vmem, vmem, vmem, vmem, vmem],
        out_specs=(vmem, vmem, vmem),
        scratch_shapes=[
            pltpu.VMEM((CONTEXT, kcols), jnp.bfloat16),
            pltpu.VMEM((CONTEXT, kcols), jnp.bfloat16),
        ],
        compiler_params=pltpu.CompilerParams(vmem_limit_bytes=48 * 1024 * 1024),
    )(table, priors, lengths, query_rot, key_rot, value_in, cache_keys, cache_values)


def body(
    hidden_in,
    attn_gain,
    mlp_gain,
    w_query,
    w_key,
    w_value,
    w_out,
    w_gate,
    w_up,
    w_down,
    cache_k,
    cache_v,
    owner_of_row,
    new_len,
    prior_len,
    page_table,
):
    peers = lax.axis_size(REQ)
    groups = lax.axis_size("grp")
    row_count = hidden_in.shape[0]
    pair_rows = 2 * row_count // peers
    quarter = row_count // groups
    group_index = lax.axis_index("grp")
    gate_w = lax.all_gather(w_gate, "ry", axis=1, tiled=True)
    up_w = lax.all_gather(w_up, "ry", axis=1, tiled=True)
    ring = lax.axis_size("ry")
    down_parts = [w_down] + [
        lax.ppermute(w_down, "ry", [(i, (i + shift) % ring) for i in range(ring)])
        for shift in range(1, ring)
    ]
    normed = normalize(hidden_in.astype(jnp.float32), attn_gain).astype(jnp.bfloat16)
    qcols = w_query.shape[1]
    kcols = w_key.shape[1]
    query_rows = jnp.dot(normed, w_query, preferred_element_type=jnp.float32).astype(jnp.bfloat16)
    key_rows = jnp.dot(normed, w_key, preferred_element_type=jnp.float32).astype(jnp.bfloat16)
    value_rows = jnp.dot(normed, w_value, preferred_element_type=jnp.float32).astype(jnp.bfloat16)
    qkv_rows = jnp.concatenate([query_rows, key_rows, value_rows], axis=1)
    gather_rows, back_rows = source_layout(owner_of_row, peers, pair_rows)
    send_qkv = jnp.take(qkv_rows, gather_rows, axis=0, mode="fill", fill_value=0).reshape(
        peers, pair_rows, -1
    )
    recv_qkv = lax.all_to_all(send_qkv, REQ, split_axis=0, concat_axis=0, tiled=True)
    recv_query = recv_qkv[..., :qcols]
    recv_key = recv_qkv[..., qcols : qcols + kcols]
    recv_value = recv_qkv[..., qcols + kcols :]
    mixed, keys_out, values_out = owner_attention(
        recv_query, recv_key, recv_value, cache_k, cache_v, new_len[0], prior_len[0], page_table[0]
    )
    gate_w, up_w, mixed = lax.optimization_barrier((gate_w, up_w, mixed))
    returned = lax.all_to_all(mixed, REQ, split_axis=0, concat_axis=0, tiled=True)
    attn_rows = jnp.take(returned.reshape(peers * pair_rows, -1), back_rows, axis=0)
    projected = jnp.dot(attn_rows, w_out, preferred_element_type=jnp.float32)
    attn_part = lax.psum_scatter(
        projected.astype(jnp.bfloat16), "grp", scatter_dimension=0, tiled=True
    ).astype(jnp.float32)
    own_rows = lax.dynamic_slice_in_dim(hidden_in, group_index * quarter, quarter, 0).astype(
        jnp.float32
    )
    residual = own_rows + RESIDUAL_MULT * attn_part
    mlp_in = normalize(residual, mlp_gain).astype(jnp.bfloat16)
    piece = lax.all_gather(mlp_in, "rzc", axis=0, tiled=True)
    gate = jnp.dot(piece, gate_w, preferred_element_type=jnp.float32)
    upper = jnp.dot(piece, up_w, preferred_element_type=jnp.float32)
    hidden = (jax.nn.silu(gate) * upper).astype(jnp.bfloat16)
    down_parts, hidden = lax.optimization_barrier((down_parts, hidden))
    units = w_down.shape[0]
    partial = None
    for shift, part in enumerate(down_parts):
        block = (lax.axis_index("ry") - shift) % ring
        term = jnp.dot(
            lax.dynamic_slice_in_dim(hidden, block * units, units, axis=1),
            part,
            preferred_element_type=jnp.float32,
        )
        partial = term if partial is None else partial + term
    down = lax.psum_scatter(
        partial.astype(jnp.bfloat16),
        "rzc",
        scatter_dimension=0,
        tiled=True,
    ).astype(jnp.float32)
    layer_out = (residual + RESIDUAL_MULT * down).astype(jnp.bfloat16)
    return (layer_out, keys_out, values_out)


REQ = ("ry", "rzc")


def solution(mesh):
    req_size = mesh.shape["req"]
    major = 4
    inner = Mesh(
        mesh.devices.reshape(major, req_size // major, mesh.shape["grp"]), ("ry", "rzc", "grp")
    )
    in_specs = (
        P(REQ, None),
        P(),
        P(),
        P(None, "grp"),
        P(None, "grp"),
        P(None, "grp"),
        P("grp", None),
        P(None, REQ),
        P(None, REQ),
        P(REQ, None),
        P(REQ, None, "grp"),
        P(REQ, None, "grp"),
        P(REQ),
        P(REQ, None),
        P(REQ, None),
        P(REQ, None),
    )
    out_specs = (P(REQ + ("grp",), None), P(REQ, None, "grp"), P(REQ, None, "grp"))
    return jax.shard_map(body, mesh=inner, in_specs=in_specs, out_specs=out_specs, check_vma=False)
```

```python
import functools

import jax
import jax.numpy as jnp
from jax import lax
from jax.experimental import pallas as pl
from jax.experimental.pallas import tpu as pltpu
from jax.sharding import Mesh, PartitionSpec as P

HD = 64
PAGE = 16
MAXP = 16
CONTEXT = 256


EPSILON = 1e-05
RESIDUAL_MULT = 0.22
SCORE_MULT = 0.015625
ROPE_BASE = 10000000.0


def normalize(values, gain):
    mean_square = jnp.mean(values * values, axis=-1, keepdims=True)
    return values * lax.rsqrt(mean_square + EPSILON) * gain


def rotary(values, positions):
    dim = values.shape[-1]
    half = dim // 2
    freq = jnp.power(ROPE_BASE, -2.0 * jnp.arange(half, dtype=jnp.int32).astype(jnp.float32) / dim)
    angle = positions.astype(jnp.float32)[:, :, None] * freq
    cosine = jnp.cos(angle)[:, :, None, :]
    sine = jnp.sin(angle)[:, :, None, :]
    first = values[..., :half].astype(jnp.float32)
    second = values[..., half:].astype(jnp.float32)
    return jnp.concatenate(
        [first * cosine - second * sine, second * cosine + first * sine], axis=-1
    )


def source_layout(owner_block, peers, pair_rows):
    row_count = owner_block.shape[0]
    owners = jnp.arange(peers, dtype=jnp.int32)
    member = owner_block[None, :] == owners[:, None]
    counts = jnp.sum(member.astype(jnp.int32), axis=1)
    row_ids = jnp.arange(row_count, dtype=jnp.int32)
    starts = jnp.min(jnp.where(member, row_ids[None, :], row_count), axis=1)
    slots = jnp.arange(pair_rows, dtype=jnp.int32)
    gather_rows = jnp.where(
        slots[None, :] < counts[:, None], starts[:, None] + slots[None, :], row_count
    )
    row_start = jnp.sum(jnp.where(member, starts[:, None], 0), axis=0)
    back_rows = owner_block * pair_rows + (row_ids - row_start)
    return (gather_rows.reshape(-1), back_rows)


def attention_kernel(table_ref, prior_ref, len_ref, q_ref, k_ref, v_ref, ck_ref, cv_ref,
                     out_ref, nk_ref, nv_ref, kbuf, vbuf):
    sources, pair_rows, qcols = q_ref.shape
    kcols = k_ref.shape[-1]
    kv_heads = kcols // HD
    group = qcols // kcols

    def per_source(s, carry):
        prior = prior_ref[s]
        length = len_ref[s]
        for i in range(MAXP):
            page = table_ref[s * MAXP + i]
            kbuf[i * PAGE:(i + 1) * PAGE, :] = ck_ref[page]
            vbuf[i * PAGE:(i + 1) * PAGE, :] = cv_ref[page]
        j_col = lax.broadcasted_iota(jnp.int32, (CONTEXT, pair_rows), 0)
        t_row = lax.broadcasted_iota(jnp.int32, (CONTEXT, pair_rows), 1)
        select = jnp.logical_and(j_col == prior + t_row, t_row < length).astype(jnp.bfloat16)
        j_only = lax.broadcasted_iota(jnp.int32, (CONTEXT, kcols), 0)
        fresh = jnp.logical_and(j_only >= prior, j_only < prior + length)
        k_new = jnp.dot(select, k_ref[s], preferred_element_type=jnp.float32).astype(jnp.bfloat16)
        v_new = jnp.dot(select, v_ref[s], preferred_element_type=jnp.float32).astype(jnp.bfloat16)
        keys = jnp.where(fresh, k_new, kbuf[...])
        values = jnp.where(fresh, v_new, vbuf[...])
        for i in range(MAXP):
            page = table_ref[s * MAXP + i]
            nk_ref[page] = keys[i * PAGE:(i + 1) * PAGE, :]
            nv_ref[page] = values[i * PAGE:(i + 1) * PAGE, :]
        q_all = q_ref[s]
        rows = group * pair_rows
        r_idx = lax.broadcasted_iota(jnp.int32, (rows, CONTEXT), 0)
        j_idx = lax.broadcasted_iota(jnp.int32, (rows, CONTEXT), 1)
        allowed = j_idx <= prior + r_idx % pair_rows
        for h in range(kv_heads):
            q_h = jnp.concatenate(
                [q_all[:, (h * group + g) * HD:(h * group + g + 1) * HD] for g in range(group)],
                axis=0,
            )
            k_h = keys[:, h * HD:(h + 1) * HD]
            v_h = values[:, h * HD:(h + 1) * HD]
            scores = lax.dot_general(
                q_h, k_h, (((1,), (1,)), ((), ())), preferred_element_type=jnp.float32
            ) * SCORE_MULT
            scores = jnp.where(allowed, scores, -jnp.inf)
            top = jnp.max(scores, axis=-1, keepdims=True)
            weights = jnp.exp(scores - top)
            probs = (weights / jnp.sum(weights, axis=-1, keepdims=True)).astype(jnp.bfloat16)
            mixed = jnp.dot(probs, v_h, preferred_element_type=jnp.float32).astype(jnp.bfloat16)
            for g in range(group):
                c = h * group + g
                out_ref[s, :, c * HD:(c + 1) * HD] = mixed[g * pair_rows:(g + 1) * pair_rows, :]
        return carry

    lax.fori_loop(0, sources, per_source, 0)


def owner_attention(query_in, key_in, value_in, cache_keys, cache_values, lengths, priors, table):
    sources, pair_rows, qcols = query_in.shape
    kcols = key_in.shape[-1]
    kv_heads = kcols // HD
    slots = jnp.arange(pair_rows, dtype=jnp.int32)
    positions = priors[:, None] + slots[None, :]
    query_rot = rotary(query_in.reshape(sources, pair_rows, qcols // HD, HD), positions).astype(
        jnp.bfloat16
    ).reshape(sources, pair_rows, qcols)
    key_rot = rotary(key_in.reshape(sources, pair_rows, kv_heads, HD), positions).astype(
        jnp.bfloat16
    ).reshape(sources, pair_rows, kcols)
    pool_pages = cache_keys.shape[0]
    smem = pl.BlockSpec(memory_space=pltpu.SMEM)
    vmem = pl.BlockSpec(memory_space=pltpu.VMEM)
    return pl.pallas_call(
        attention_kernel,
        out_shape=(
            jax.ShapeDtypeStruct((sources, pair_rows, qcols), jnp.bfloat16),
            jax.ShapeDtypeStruct(cache_keys.shape, cache_keys.dtype),
            jax.ShapeDtypeStruct(cache_values.shape, cache_values.dtype),
        ),
        in_specs=[smem, smem, smem, vmem, vmem, vmem, vmem, vmem],
        out_specs=(vmem, vmem, vmem),
        scratch_shapes=[
            pltpu.VMEM((CONTEXT, kcols), jnp.bfloat16),
            pltpu.VMEM((CONTEXT, kcols), jnp.bfloat16),
        ],
        compiler_params=pltpu.CompilerParams(vmem_limit_bytes=48 * 1024 * 1024),
    )(table, priors, lengths, query_rot, key_rot, value_in, cache_keys, cache_values)


def exchange_kernel(shape, x_ref, o_ref, local_sem, send_sems, recv_sems):
    rows_axis, cols_axis = shape
    peers = rows_axis * cols_axis
    me = lax.axis_index("ry") * cols_axis + lax.axis_index("rzc")
    grp = lax.axis_index("grp")

    def device(peer):
        return (peer // cols_axis, peer % cols_axis, grp)

    barrier = pltpu.get_barrier_semaphore()

    def greet(k, carry):
        pl.semaphore_signal(
            barrier, inc=1, device_id=device((me + k) % peers), device_id_type=pl.DeviceIdType.MESH
        )
        return carry

    lax.fori_loop(1, peers, greet, 0)
    pl.semaphore_wait(barrier, peers - 1)
    local = pltpu.make_async_copy(x_ref.at[me], o_ref.at[me], local_sem)
    local.start()

    def remote(k):
        peer = (me + k) % peers
        return pltpu.make_async_remote_copy(
            src_ref=x_ref.at[peer],
            dst_ref=o_ref.at[me],
            send_sem=send_sems.at[k],
            recv_sem=recv_sems.at[k],
            device_id=device(peer),
            device_id_type=pl.DeviceIdType.MESH,
        )

    def send(k, carry):
        remote(k).start()
        return carry

    def finish(k, carry):
        remote(k).wait()
        return carry

    lax.fori_loop(1, peers, send, 0)
    local.wait()
    lax.fori_loop(1, peers, finish, 0)


def exchange(x, collective_id):
    shape = (lax.axis_size("ry"), lax.axis_size("rzc"))
    peers = shape[0] * shape[1]
    any_space = pl.BlockSpec(memory_space=pl.ANY)
    return pl.pallas_call(
        functools.partial(exchange_kernel, shape),
        out_shape=jax.ShapeDtypeStruct(x.shape, x.dtype),
        in_specs=[any_space],
        out_specs=any_space,
        scratch_shapes=[
            pltpu.SemaphoreType.DMA,
            pltpu.SemaphoreType.DMA((peers,)),
            pltpu.SemaphoreType.DMA((peers,)),
        ],
        compiler_params=pltpu.CompilerParams(collective_id=collective_id, has_side_effects=True),
    )(x)


def body(
    hidden_in,
    attn_gain,
    mlp_gain,
    w_query,
    w_key,
    w_value,
    w_out,
    w_gate,
    w_up,
    w_down,
    cache_k,
    cache_v,
    owner_of_row,
    new_len,
    prior_len,
    page_table,
):
    peers = lax.axis_size(REQ)
    groups = lax.axis_size("grp")
    row_count = hidden_in.shape[0]
    pair_rows = 2 * row_count // peers
    quarter = row_count // groups
    group_index = lax.axis_index("grp")
    gate_w = lax.all_gather(w_gate, "ry", axis=1, tiled=True)
    up_w = lax.all_gather(w_up, "ry", axis=1, tiled=True)
    ring = lax.axis_size("ry")
    down_parts = [w_down] + [
        lax.ppermute(w_down, "ry", [(i, (i + shift) % ring) for i in range(ring)])
        for shift in range(1, ring)
    ]
    normed = normalize(hidden_in.astype(jnp.float32), attn_gain).astype(jnp.bfloat16)
    qcols = w_query.shape[1]
    kcols = w_key.shape[1]
    query_rows = jnp.dot(normed, w_query, preferred_element_type=jnp.float32).astype(jnp.bfloat16)
    key_rows = jnp.dot(normed, w_key, preferred_element_type=jnp.float32).astype(jnp.bfloat16)
    value_rows = jnp.dot(normed, w_value, preferred_element_type=jnp.float32).astype(jnp.bfloat16)
    qkv_rows = jnp.concatenate([query_rows, key_rows, value_rows], axis=1)
    gather_rows, back_rows = source_layout(owner_of_row, peers, pair_rows)
    send_qkv = jnp.take(qkv_rows, gather_rows, axis=0, mode="fill", fill_value=0).reshape(
        peers, pair_rows, -1
    )
    recv_qkv = exchange(send_qkv, 0)
    recv_query = recv_qkv[..., :qcols]
    recv_key = recv_qkv[..., qcols : qcols + kcols]
    recv_value = recv_qkv[..., qcols + kcols :]
    mixed, keys_out, values_out = owner_attention(
        recv_query, recv_key, recv_value, cache_k, cache_v, new_len[0], prior_len[0], page_table[0]
    )
    gate_w, up_w, mixed = lax.optimization_barrier((gate_w, up_w, mixed))
    returned = exchange(mixed, 1)
    attn_rows = jnp.take(returned.reshape(peers * pair_rows, -1), back_rows, axis=0)
    projected = jnp.dot(attn_rows, w_out, preferred_element_type=jnp.float32)
    attn_part = lax.psum_scatter(
        projected.astype(jnp.bfloat16), "grp", scatter_dimension=0, tiled=True
    ).astype(jnp.float32)
    own_rows = lax.dynamic_slice_in_dim(hidden_in, group_index * quarter, quarter, 0).astype(
        jnp.float32
    )
    residual = own_rows + RESIDUAL_MULT * attn_part
    mlp_in = normalize(residual, mlp_gain).astype(jnp.bfloat16)
    piece = lax.all_gather(mlp_in, "rzc", axis=0, tiled=True)
    gate = jnp.dot(piece, gate_w, preferred_element_type=jnp.float32)
    upper = jnp.dot(piece, up_w, preferred_element_type=jnp.float32)
    hidden = (jax.nn.silu(gate) * upper).astype(jnp.bfloat16)
    down_parts, hidden = lax.optimization_barrier((down_parts, hidden))
    units = w_down.shape[0]
    partial = None
    for shift, part in enumerate(down_parts):
        block = (lax.axis_index("ry") - shift) % ring
        term = jnp.dot(
            lax.dynamic_slice_in_dim(hidden, block * units, units, axis=1),
            part,
            preferred_element_type=jnp.float32,
        )
        partial = term if partial is None else partial + term
    down = lax.psum_scatter(
        partial.astype(jnp.bfloat16),
        "rzc",
        scatter_dimension=0,
        tiled=True,
    ).astype(jnp.float32)
    layer_out = (residual + RESIDUAL_MULT * down).astype(jnp.bfloat16)
    return (layer_out, keys_out, values_out)


REQ = ("ry", "rzc")


def solution(mesh):
    req_size = mesh.shape["req"]
    major = 4
    inner = Mesh(
        mesh.devices.reshape(major, req_size // major, mesh.shape["grp"]), ("ry", "rzc", "grp")
    )
    in_specs = (
        P(REQ, None),
        P(),
        P(),
        P(None, "grp"),
        P(None, "grp"),
        P(None, "grp"),
        P("grp", None),
        P(None, REQ),
        P(None, REQ),
        P(REQ, None),
        P(REQ, None, "grp"),
        P(REQ, None, "grp"),
        P(REQ),
        P(REQ, None),
        P(REQ, None),
        P(REQ, None),
    )
    out_specs = (P(REQ + ("grp",), None), P(REQ, None, "grp"), P(REQ, None, "grp"))
    return jax.shard_map(body, mesh=inner, in_specs=in_specs, out_specs=out_specs, check_vma=False)
```

```python
import jax
import jax.numpy as jnp
from jax import lax
from jax.experimental import pallas as pl
from jax.experimental.pallas import tpu as pltpu
from jax.sharding import Mesh, PartitionSpec as P

HD = 64
PAGE = 16
MAXP = 16
CONTEXT = 256


EPSILON = 1e-05
RESIDUAL_MULT = 0.22
SCORE_MULT = 0.015625
ROPE_BASE = 10000000.0


def normalize(values, gain):
    mean_square = jnp.mean(values * values, axis=-1, keepdims=True)
    return values * lax.rsqrt(mean_square + EPSILON) * gain


def rotary(values, positions):
    dim = values.shape[-1]
    half = dim // 2
    freq = jnp.power(ROPE_BASE, -2.0 * jnp.arange(half, dtype=jnp.int32).astype(jnp.float32) / dim)
    angle = positions.astype(jnp.float32)[:, :, None] * freq
    cosine = jnp.cos(angle)[:, :, None, :]
    sine = jnp.sin(angle)[:, :, None, :]
    first = values[..., :half].astype(jnp.float32)
    second = values[..., half:].astype(jnp.float32)
    return jnp.concatenate(
        [first * cosine - second * sine, second * cosine + first * sine], axis=-1
    )


def source_layout(owner_block, peers, pair_rows):
    row_count = owner_block.shape[0]
    owners = jnp.arange(peers, dtype=jnp.int32)
    member = owner_block[None, :] == owners[:, None]
    counts = jnp.sum(member.astype(jnp.int32), axis=1)
    row_ids = jnp.arange(row_count, dtype=jnp.int32)
    starts = jnp.min(jnp.where(member, row_ids[None, :], row_count), axis=1)
    slots = jnp.arange(pair_rows, dtype=jnp.int32)
    gather_rows = jnp.where(
        slots[None, :] < counts[:, None], starts[:, None] + slots[None, :], row_count
    )
    row_start = jnp.sum(jnp.where(member, starts[:, None], 0), axis=0)
    back_rows = owner_block * pair_rows + (row_ids - row_start)
    return (gather_rows.reshape(-1), back_rows)


def attention_kernel(table_ref, prior_ref, len_ref, q_ref, k_ref, v_ref, ck_ref, cv_ref,
                     out_ref, nk_ref, nv_ref, kbuf, vbuf):
    sources, pair_rows, qcols = q_ref.shape
    kcols = k_ref.shape[-1]
    kv_heads = kcols // HD
    group = qcols // kcols

    def per_source(s, carry):
        prior = prior_ref[s]
        length = len_ref[s]
        for i in range(MAXP):
            page = table_ref[s * MAXP + i]
            kbuf[i * PAGE:(i + 1) * PAGE, :] = ck_ref[page]
            vbuf[i * PAGE:(i + 1) * PAGE, :] = cv_ref[page]
        j_col = lax.broadcasted_iota(jnp.int32, (CONTEXT, pair_rows), 0)
        t_row = lax.broadcasted_iota(jnp.int32, (CONTEXT, pair_rows), 1)
        select = jnp.logical_and(j_col == prior + t_row, t_row < length).astype(jnp.bfloat16)
        j_only = lax.broadcasted_iota(jnp.int32, (CONTEXT, kcols), 0)
        fresh = jnp.logical_and(j_only >= prior, j_only < prior + length)
        k_new = jnp.dot(select, k_ref[s], preferred_element_type=jnp.float32).astype(jnp.bfloat16)
        v_new = jnp.dot(select, v_ref[s], preferred_element_type=jnp.float32).astype(jnp.bfloat16)
        keys = jnp.where(fresh, k_new, kbuf[...])
        values = jnp.where(fresh, v_new, vbuf[...])
        for i in range(MAXP):
            page = table_ref[s * MAXP + i]
            nk_ref[page] = keys[i * PAGE:(i + 1) * PAGE, :]
            nv_ref[page] = values[i * PAGE:(i + 1) * PAGE, :]
        q_all = q_ref[s]
        rows = group * pair_rows
        r_idx = lax.broadcasted_iota(jnp.int32, (rows, CONTEXT), 0)
        j_idx = lax.broadcasted_iota(jnp.int32, (rows, CONTEXT), 1)
        allowed = j_idx <= prior + r_idx % pair_rows
        for h in range(kv_heads):
            q_h = jnp.concatenate(
                [q_all[:, (h * group + g) * HD:(h * group + g + 1) * HD] for g in range(group)],
                axis=0,
            )
            k_h = keys[:, h * HD:(h + 1) * HD]
            v_h = values[:, h * HD:(h + 1) * HD]
            scores = lax.dot_general(
                q_h, k_h, (((1,), (1,)), ((), ())), preferred_element_type=jnp.float32
            ) * SCORE_MULT
            scores = jnp.where(allowed, scores, -jnp.inf)
            top = jnp.max(scores, axis=-1, keepdims=True)
            weights = jnp.exp(scores - top)
            probs = (weights / jnp.sum(weights, axis=-1, keepdims=True)).astype(jnp.bfloat16)
            mixed = jnp.dot(probs, v_h, preferred_element_type=jnp.float32).astype(jnp.bfloat16)
            for g in range(group):
                c = h * group + g
                out_ref[s, :, c * HD:(c + 1) * HD] = mixed[g * pair_rows:(g + 1) * pair_rows, :]
        return carry

    lax.fori_loop(0, sources, per_source, 0)


def owner_attention(query_in, key_in, value_in, cache_keys, cache_values, lengths, priors, table):
    sources, pair_rows, qcols = query_in.shape
    kcols = key_in.shape[-1]
    kv_heads = kcols // HD
    slots = jnp.arange(pair_rows, dtype=jnp.int32)
    positions = priors[:, None] + slots[None, :]
    query_rot = rotary(query_in.reshape(sources, pair_rows, qcols // HD, HD), positions).astype(
        jnp.bfloat16
    ).reshape(sources, pair_rows, qcols)
    key_rot = rotary(key_in.reshape(sources, pair_rows, kv_heads, HD), positions).astype(
        jnp.bfloat16
    ).reshape(sources, pair_rows, kcols)
    pool_pages = cache_keys.shape[0]
    smem = pl.BlockSpec(memory_space=pltpu.SMEM)
    vmem = pl.BlockSpec(memory_space=pltpu.VMEM)
    return pl.pallas_call(
        attention_kernel,
        out_shape=(
            jax.ShapeDtypeStruct((sources, pair_rows, qcols), jnp.bfloat16),
            jax.ShapeDtypeStruct(cache_keys.shape, cache_keys.dtype),
            jax.ShapeDtypeStruct(cache_values.shape, cache_values.dtype),
        ),
        in_specs=[smem, smem, smem, vmem, vmem, vmem, vmem, vmem],
        out_specs=(vmem, vmem, vmem),
        scratch_shapes=[
            pltpu.VMEM((CONTEXT, kcols), jnp.bfloat16),
            pltpu.VMEM((CONTEXT, kcols), jnp.bfloat16),
        ],
        compiler_params=pltpu.CompilerParams(vmem_limit_bytes=48 * 1024 * 1024),
    )(table, priors, lengths, query_rot, key_rot, value_in, cache_keys, cache_values)


def body(
    hidden_in,
    attn_gain,
    mlp_gain,
    w_query,
    w_key,
    w_value,
    w_out,
    w_gate,
    w_up,
    w_down,
    cache_k,
    cache_v,
    owner_of_row,
    new_len,
    prior_len,
    page_table,
):
    peers = lax.axis_size(REQ)
    groups = lax.axis_size("grp")
    row_count = hidden_in.shape[0]
    pair_rows = 2 * row_count // peers
    quarter = row_count // groups
    group_index = lax.axis_index("grp")
    gate_w = lax.all_gather(w_gate, "ry", axis=1, tiled=True)
    up_w = lax.all_gather(w_up, "ry", axis=1, tiled=True)
    ring = lax.axis_size("ry")
    down_parts = [w_down] + [
        lax.ppermute(w_down, "ry", [(i, (i + shift) % ring) for i in range(ring)])
        for shift in range(1, ring)
    ]
    normed = normalize(hidden_in.astype(jnp.float32), attn_gain).astype(jnp.bfloat16)
    qcols = w_query.shape[1]
    kcols = w_key.shape[1]
    query_rows = jnp.dot(normed, w_query, preferred_element_type=jnp.float32).astype(jnp.bfloat16)
    key_rows = jnp.dot(normed, w_key, preferred_element_type=jnp.float32).astype(jnp.bfloat16)
    value_rows = jnp.dot(normed, w_value, preferred_element_type=jnp.float32).astype(jnp.bfloat16)
    qkv_rows = jnp.concatenate([query_rows, key_rows, value_rows], axis=1)
    gather_rows, back_rows = source_layout(owner_of_row, peers, pair_rows)
    send_qkv = jnp.take(qkv_rows, gather_rows, axis=0, mode="fill", fill_value=0).reshape(
        peers, pair_rows, -1
    )
    recv_qkv = lax.all_to_all(send_qkv, REQ, split_axis=0, concat_axis=0, tiled=True)
    recv_query = recv_qkv[..., :qcols]
    recv_key = recv_qkv[..., qcols : qcols + kcols]
    recv_value = recv_qkv[..., qcols + kcols :]
    mixed, keys_out, values_out = owner_attention(
        recv_query, recv_key, recv_value, cache_k, cache_v, new_len[0], prior_len[0], page_table[0]
    )
    gate_w, up_w, mixed = lax.optimization_barrier((gate_w, up_w, mixed))
    returned = lax.all_to_all(mixed, REQ, split_axis=0, concat_axis=0, tiled=True)
    attn_rows = jnp.take(returned.reshape(peers * pair_rows, -1), back_rows, axis=0)
    projected = jnp.dot(attn_rows, w_out, preferred_element_type=jnp.float32)
    attn_part = lax.psum_scatter(
        projected.astype(jnp.bfloat16), "grp", scatter_dimension=0, tiled=True
    ).astype(jnp.float32)
    own_rows = lax.dynamic_slice_in_dim(hidden_in, group_index * quarter, quarter, 0).astype(
        jnp.float32
    )
    residual = own_rows + RESIDUAL_MULT * attn_part
    mlp_in = normalize(residual, mlp_gain).astype(jnp.bfloat16)
    halves = []
    half_rows = mlp_in.shape[0] // 2
    for half in range(2):
        piece = lax.all_gather(
            mlp_in[half * half_rows:(half + 1) * half_rows], "rzc", axis=0, tiled=True
        )
        gate = jnp.dot(piece, gate_w, preferred_element_type=jnp.float32)
        upper = jnp.dot(piece, up_w, preferred_element_type=jnp.float32)
        hidden = (jax.nn.silu(gate) * upper).astype(jnp.bfloat16)
        if half == 0:
            down_parts, hidden = lax.optimization_barrier((down_parts, hidden))
        units = w_down.shape[0]
        partial = None
        for shift, part in enumerate(down_parts):
            block = (lax.axis_index("ry") - shift) % ring
            term = jnp.dot(
                lax.dynamic_slice_in_dim(hidden, block * units, units, axis=1),
                part,
                preferred_element_type=jnp.float32,
            )
            partial = term if partial is None else partial + term
        halves.append(
            lax.psum_scatter(partial.astype(jnp.bfloat16), "rzc", scatter_dimension=0, tiled=True)
        )
    down = jnp.concatenate(halves, axis=0).astype(jnp.float32)
    layer_out = (residual + RESIDUAL_MULT * down).astype(jnp.bfloat16)
    return (layer_out, keys_out, values_out)


REQ = ("ry", "rzc")


def solution(mesh):
    req_size = mesh.shape["req"]
    major = 4
    inner = Mesh(
        mesh.devices.reshape(major, req_size // major, mesh.shape["grp"]), ("ry", "rzc", "grp")
    )
    in_specs = (
        P(REQ, None),
        P(),
        P(),
        P(None, "grp"),
        P(None, "grp"),
        P(None, "grp"),
        P("grp", None),
        P(None, REQ),
        P(None, REQ),
        P(REQ, None),
        P(REQ, None, "grp"),
        P(REQ, None, "grp"),
        P(REQ),
        P(REQ, None),
        P(REQ, None),
        P(REQ, None),
    )
    out_specs = (P(REQ + ("grp",), None), P(REQ, None, "grp"), P(REQ, None, "grp"))
    return jax.shard_map(body, mesh=inner, in_specs=in_specs, out_specs=out_specs, check_vma=False)
```

```python
import jax
import jax.numpy as jnp
from jax import lax
from jax.experimental import pallas as pl
from jax.experimental.pallas import tpu as pltpu
from jax.sharding import Mesh, PartitionSpec as P

HD = 64
PAGE = 16
MAXP = 16
CONTEXT = 256


EPSILON = 1e-05
RESIDUAL_MULT = 0.22
SCORE_MULT = 0.015625
ROPE_BASE = 10000000.0


def normalize(values, gain):
    mean_square = jnp.mean(values * values, axis=-1, keepdims=True)
    return values * lax.rsqrt(mean_square + EPSILON) * gain


def rotary(values, positions):
    dim = values.shape[-1]
    half = dim // 2
    freq = jnp.power(ROPE_BASE, -2.0 * jnp.arange(half, dtype=jnp.int32).astype(jnp.float32) / dim)
    angle = positions.astype(jnp.float32)[:, :, None] * freq
    cosine = jnp.cos(angle)[:, :, None, :]
    sine = jnp.sin(angle)[:, :, None, :]
    first = values[..., :half].astype(jnp.float32)
    second = values[..., half:].astype(jnp.float32)
    return jnp.concatenate(
        [first * cosine - second * sine, second * cosine + first * sine], axis=-1
    )


def source_layout(owner_block, peers, pair_rows):
    row_count = owner_block.shape[0]
    owners = jnp.arange(peers, dtype=jnp.int32)
    member = owner_block[None, :] == owners[:, None]
    counts = jnp.sum(member.astype(jnp.int32), axis=1)
    row_ids = jnp.arange(row_count, dtype=jnp.int32)
    starts = jnp.min(jnp.where(member, row_ids[None, :], row_count), axis=1)
    slots = jnp.arange(pair_rows, dtype=jnp.int32)
    gather_rows = jnp.where(
        slots[None, :] < counts[:, None], starts[:, None] + slots[None, :], row_count
    )
    row_start = jnp.sum(jnp.where(member, starts[:, None], 0), axis=0)
    back_rows = owner_block * pair_rows + (row_ids - row_start)
    return (gather_rows.reshape(-1), back_rows)


def attention_kernel(table_ref, prior_ref, len_ref, q_ref, k_ref, v_ref, ck_ref, cv_ref,
                     out_ref, nk_ref, nv_ref, kbuf, vbuf):
    sources, pair_rows, qcols = q_ref.shape
    kcols = k_ref.shape[-1]
    kv_heads = kcols // HD
    group = qcols // kcols

    def per_source(s, carry):
        prior = prior_ref[s]
        length = len_ref[s]
        for i in range(MAXP):
            page = table_ref[s * MAXP + i]
            kbuf[i * PAGE:(i + 1) * PAGE, :] = ck_ref[page]
            vbuf[i * PAGE:(i + 1) * PAGE, :] = cv_ref[page]
        j_col = lax.broadcasted_iota(jnp.int32, (CONTEXT, pair_rows), 0)
        t_row = lax.broadcasted_iota(jnp.int32, (CONTEXT, pair_rows), 1)
        select = jnp.logical_and(j_col == prior + t_row, t_row < length).astype(jnp.bfloat16)
        j_only = lax.broadcasted_iota(jnp.int32, (CONTEXT, kcols), 0)
        fresh = jnp.logical_and(j_only >= prior, j_only < prior + length)
        k_new = jnp.dot(select, k_ref[s], preferred_element_type=jnp.float32).astype(jnp.bfloat16)
        v_new = jnp.dot(select, v_ref[s], preferred_element_type=jnp.float32).astype(jnp.bfloat16)
        keys = jnp.where(fresh, k_new, kbuf[...])
        values = jnp.where(fresh, v_new, vbuf[...])
        for i in range(MAXP):
            page = table_ref[s * MAXP + i]
            nk_ref[page] = keys[i * PAGE:(i + 1) * PAGE, :]
            nv_ref[page] = values[i * PAGE:(i + 1) * PAGE, :]
        q_all = q_ref[s]
        rows = group * pair_rows
        r_idx = lax.broadcasted_iota(jnp.int32, (rows, CONTEXT), 0)
        j_idx = lax.broadcasted_iota(jnp.int32, (rows, CONTEXT), 1)
        allowed = j_idx <= prior + r_idx % pair_rows
        for h in range(kv_heads):
            q_h = jnp.concatenate(
                [q_all[:, (h * group + g) * HD:(h * group + g + 1) * HD] for g in range(group)],
                axis=0,
            )
            k_h = keys[:, h * HD:(h + 1) * HD]
            v_h = values[:, h * HD:(h + 1) * HD]
            scores = lax.dot_general(
                q_h, k_h, (((1,), (1,)), ((), ())), preferred_element_type=jnp.float32
            ) * SCORE_MULT
            scores = jnp.where(allowed, scores, -jnp.inf)
            top = jnp.max(scores, axis=-1, keepdims=True)
            weights = jnp.exp(scores - top)
            probs = (weights / jnp.sum(weights, axis=-1, keepdims=True)).astype(jnp.bfloat16)
            mixed = jnp.dot(probs, v_h, preferred_element_type=jnp.float32).astype(jnp.bfloat16)
            for g in range(group):
                c = h * group + g
                out_ref[s, :, c * HD:(c + 1) * HD] = mixed[g * pair_rows:(g + 1) * pair_rows, :]
        return carry

    lax.fori_loop(0, sources, per_source, 0)


def owner_attention(query_in, key_in, value_in, cache_keys, cache_values, lengths, priors, table):
    sources, pair_rows, qcols = query_in.shape
    kcols = key_in.shape[-1]
    kv_heads = kcols // HD
    slots = jnp.arange(pair_rows, dtype=jnp.int32)
    positions = priors[:, None] + slots[None, :]
    query_rot = rotary(query_in.reshape(sources, pair_rows, qcols // HD, HD), positions).astype(
        jnp.bfloat16
    ).reshape(sources, pair_rows, qcols)
    key_rot = rotary(key_in.reshape(sources, pair_rows, kv_heads, HD), positions).astype(
        jnp.bfloat16
    ).reshape(sources, pair_rows, kcols)
    pool_pages = cache_keys.shape[0]
    smem = pl.BlockSpec(memory_space=pltpu.SMEM)
    vmem = pl.BlockSpec(memory_space=pltpu.VMEM)
    return pl.pallas_call(
        attention_kernel,
        out_shape=(
            jax.ShapeDtypeStruct((sources, pair_rows, qcols), jnp.bfloat16),
            jax.ShapeDtypeStruct(cache_keys.shape, cache_keys.dtype),
            jax.ShapeDtypeStruct(cache_values.shape, cache_values.dtype),
        ),
        in_specs=[smem, smem, smem, vmem, vmem, vmem, vmem, vmem],
        out_specs=(vmem, vmem, vmem),
        scratch_shapes=[
            pltpu.VMEM((CONTEXT, kcols), jnp.bfloat16),
            pltpu.VMEM((CONTEXT, kcols), jnp.bfloat16),
        ],
        compiler_params=pltpu.CompilerParams(vmem_limit_bytes=48 * 1024 * 1024),
    )(table, priors, lengths, query_rot, key_rot, value_in, cache_keys, cache_values)


def body(
    hidden_in,
    attn_gain,
    mlp_gain,
    w_query,
    w_key,
    w_value,
    w_out,
    w_gate,
    w_up,
    w_down,
    cache_k,
    cache_v,
    owner_of_row,
    new_len,
    prior_len,
    page_table,
):
    peers = lax.axis_size(REQ)
    groups = lax.axis_size("grp")
    row_count = hidden_in.shape[0]
    pair_rows = 2 * row_count // peers
    quarter = row_count // groups
    group_index = lax.axis_index("grp")
    gate_w = lax.all_gather(w_gate, "ry", axis=1, tiled=True)
    up_w = lax.all_gather(w_up, "ry", axis=1, tiled=True)
    ring = lax.axis_size("ry")
    down_parts = [w_down] + [
        lax.ppermute(w_down, "ry", [(i, (i + shift) % ring) for i in range(ring)])
        for shift in range(1, ring)
    ]
    out_parts = [w_out] + [
        lax.ppermute(w_out, "grp", [(i, (i + shift) % groups) for i in range(groups)])
        for shift in range(1, groups)
    ]
    normed = normalize(hidden_in.astype(jnp.float32), attn_gain).astype(jnp.bfloat16)
    qcols = w_query.shape[1]
    kcols = w_key.shape[1]
    query_rows = jnp.dot(normed, w_query, preferred_element_type=jnp.float32).astype(jnp.bfloat16)
    key_rows = jnp.dot(normed, w_key, preferred_element_type=jnp.float32).astype(jnp.bfloat16)
    value_rows = jnp.dot(normed, w_value, preferred_element_type=jnp.float32).astype(jnp.bfloat16)
    qkv_rows = jnp.concatenate([query_rows, key_rows, value_rows], axis=1)
    gather_rows, back_rows = source_layout(owner_of_row, peers, pair_rows)
    send_qkv = jnp.take(qkv_rows, gather_rows, axis=0, mode="fill", fill_value=0).reshape(
        peers, pair_rows, -1
    )
    recv_qkv = lax.all_to_all(send_qkv, REQ, split_axis=0, concat_axis=0, tiled=True)
    recv_query = recv_qkv[..., :qcols]
    recv_key = recv_qkv[..., qcols : qcols + kcols]
    recv_value = recv_qkv[..., qcols + kcols :]
    mixed, keys_out, values_out = owner_attention(
        recv_query, recv_key, recv_value, cache_k, cache_v, new_len[0], prior_len[0], page_table[0]
    )
    gate_w, up_w, out_parts, mixed = lax.optimization_barrier((gate_w, up_w, out_parts, mixed))
    returned = lax.all_to_all(mixed, REQ, split_axis=0, concat_axis=0, tiled=True)
    attn_rows = jnp.take(returned.reshape(peers * pair_rows, -1), back_rows, axis=0)
    quarters = lax.all_to_all(
        attn_rows.reshape(groups, quarter, -1), "grp", split_axis=0, concat_axis=0, tiled=True
    )
    attn_part = None
    for shift, part in enumerate(out_parts):
        block = (group_index - shift) % groups
        term = jnp.dot(quarters[block], part, preferred_element_type=jnp.float32)
        term = term.astype(jnp.bfloat16).astype(jnp.float32)
        attn_part = term if attn_part is None else attn_part + term
    own_rows = lax.dynamic_slice_in_dim(hidden_in, group_index * quarter, quarter, 0).astype(
        jnp.float32
    )
    residual = own_rows + RESIDUAL_MULT * attn_part
    mlp_in = normalize(residual, mlp_gain).astype(jnp.bfloat16)
    piece = lax.all_gather(mlp_in, "rzc", axis=0, tiled=True)
    gate = jnp.dot(piece, gate_w, preferred_element_type=jnp.float32)
    upper = jnp.dot(piece, up_w, preferred_element_type=jnp.float32)
    hidden = (jax.nn.silu(gate) * upper).astype(jnp.bfloat16)
    down_parts, hidden = lax.optimization_barrier((down_parts, hidden))
    units = w_down.shape[0]
    partial = None
    for shift, part in enumerate(down_parts):
        block = (lax.axis_index("ry") - shift) % ring
        term = jnp.dot(
            lax.dynamic_slice_in_dim(hidden, block * units, units, axis=1),
            part,
            preferred_element_type=jnp.float32,
        )
        partial = term if partial is None else partial + term
    down = lax.psum_scatter(
        partial.astype(jnp.bfloat16),
        "rzc",
        scatter_dimension=0,
        tiled=True,
    ).astype(jnp.float32)
    layer_out = (residual + RESIDUAL_MULT * down).astype(jnp.bfloat16)
    return (layer_out, keys_out, values_out)


REQ = ("ry", "rzc")


def solution(mesh):
    req_size = mesh.shape["req"]
    major = 4
    inner = Mesh(
        mesh.devices.reshape(major, req_size // major, mesh.shape["grp"]), ("ry", "rzc", "grp")
    )
    in_specs = (
        P(REQ, None),
        P(),
        P(),
        P(None, "grp"),
        P(None, "grp"),
        P(None, "grp"),
        P("grp", None),
        P(None, REQ),
        P(None, REQ),
        P(REQ, None),
        P(REQ, None, "grp"),
        P(REQ, None, "grp"),
        P(REQ),
        P(REQ, None),
        P(REQ, None),
        P(REQ, None),
    )
    out_specs = (P(REQ + ("grp",), None), P(REQ, None, "grp"), P(REQ, None, "grp"))
    return jax.shard_map(body, mesh=inner, in_specs=in_specs, out_specs=out_specs, check_vma=False)
```

```python
import jax
import jax.numpy as jnp
from jax import lax
from jax.experimental import pallas as pl
from jax.experimental.pallas import tpu as pltpu
from jax.sharding import Mesh, PartitionSpec as P

HD = 64
PAGE = 16
MAXP = 16
CONTEXT = 256


EPSILON = 1e-05
RESIDUAL_MULT = 0.22
SCORE_MULT = 0.015625
ROPE_BASE = 10000000.0


def normalize(values, gain):
    mean_square = jnp.mean(values * values, axis=-1, keepdims=True)
    return values * lax.rsqrt(mean_square + EPSILON) * gain


def rotary(values, positions):
    dim = values.shape[-1]
    half = dim // 2
    freq = jnp.power(ROPE_BASE, -2.0 * jnp.arange(half, dtype=jnp.int32).astype(jnp.float32) / dim)
    angle = positions.astype(jnp.float32)[:, :, None] * freq
    cosine = jnp.cos(angle)[:, :, None, :]
    sine = jnp.sin(angle)[:, :, None, :]
    first = values[..., :half].astype(jnp.float32)
    second = values[..., half:].astype(jnp.float32)
    return jnp.concatenate(
        [first * cosine - second * sine, second * cosine + first * sine], axis=-1
    )


def source_layout(owner_block, peers, pair_rows):
    row_count = owner_block.shape[0]
    owners = jnp.arange(peers, dtype=jnp.int32)
    member = owner_block[None, :] == owners[:, None]
    counts = jnp.sum(member.astype(jnp.int32), axis=1)
    row_ids = jnp.arange(row_count, dtype=jnp.int32)
    starts = jnp.min(jnp.where(member, row_ids[None, :], row_count), axis=1)
    slots = jnp.arange(pair_rows, dtype=jnp.int32)
    gather_rows = jnp.where(
        slots[None, :] < counts[:, None], starts[:, None] + slots[None, :], row_count
    )
    row_start = jnp.sum(jnp.where(member, starts[:, None], 0), axis=0)
    back_rows = owner_block * pair_rows + (row_ids - row_start)
    return (gather_rows.reshape(-1), back_rows)


def attention_kernel(table_ref, prior_ref, len_ref, q_ref, k_ref, v_ref, ck_ref, cv_ref,
                     out_ref, nk_ref, nv_ref, kbuf, vbuf):
    sources, pair_rows, qcols = q_ref.shape
    kcols = k_ref.shape[-1]
    kv_heads = kcols // HD
    group = qcols // kcols

    def per_source(s, carry):
        prior = prior_ref[s]
        length = len_ref[s]
        for i in range(MAXP):
            page = table_ref[s * MAXP + i]
            kbuf[i * PAGE:(i + 1) * PAGE, :] = ck_ref[page]
            vbuf[i * PAGE:(i + 1) * PAGE, :] = cv_ref[page]
        j_col = lax.broadcasted_iota(jnp.int32, (CONTEXT, pair_rows), 0)
        t_row = lax.broadcasted_iota(jnp.int32, (CONTEXT, pair_rows), 1)
        select = jnp.logical_and(j_col == prior + t_row, t_row < length).astype(jnp.bfloat16)
        j_only = lax.broadcasted_iota(jnp.int32, (CONTEXT, kcols), 0)
        fresh = jnp.logical_and(j_only >= prior, j_only < prior + length)
        k_new = jnp.dot(select, k_ref[s], preferred_element_type=jnp.float32).astype(jnp.bfloat16)
        v_new = jnp.dot(select, v_ref[s], preferred_element_type=jnp.float32).astype(jnp.bfloat16)
        keys = jnp.where(fresh, k_new, kbuf[...])
        values = jnp.where(fresh, v_new, vbuf[...])
        for i in range(MAXP):
            page = table_ref[s * MAXP + i]
            nk_ref[page] = keys[i * PAGE:(i + 1) * PAGE, :]
            nv_ref[page] = values[i * PAGE:(i + 1) * PAGE, :]
        q_all = q_ref[s]
        rows = group * pair_rows
        r_idx = lax.broadcasted_iota(jnp.int32, (rows, CONTEXT), 0)
        j_idx = lax.broadcasted_iota(jnp.int32, (rows, CONTEXT), 1)
        allowed = j_idx <= prior + r_idx % pair_rows
        for h in range(kv_heads):
            q_h = jnp.concatenate(
                [q_all[:, (h * group + g) * HD:(h * group + g + 1) * HD] for g in range(group)],
                axis=0,
            )
            k_h = keys[:, h * HD:(h + 1) * HD]
            v_h = values[:, h * HD:(h + 1) * HD]
            scores = lax.dot_general(
                q_h, k_h, (((1,), (1,)), ((), ())), preferred_element_type=jnp.float32
            ) * SCORE_MULT
            scores = jnp.where(allowed, scores, -jnp.inf)
            top = jnp.max(scores, axis=-1, keepdims=True)
            weights = jnp.exp(scores - top)
            probs = (weights / jnp.sum(weights, axis=-1, keepdims=True)).astype(jnp.bfloat16)
            mixed = jnp.dot(probs, v_h, preferred_element_type=jnp.float32).astype(jnp.bfloat16)
            for g in range(group):
                c = h * group + g
                out_ref[s, :, c * HD:(c + 1) * HD] = mixed[g * pair_rows:(g + 1) * pair_rows, :]
        return carry

    lax.fori_loop(0, sources, per_source, 0)


def owner_attention(query_in, key_in, value_in, cache_keys, cache_values, lengths, priors, table):
    sources, pair_rows, qcols = query_in.shape
    kcols = key_in.shape[-1]
    kv_heads = kcols // HD
    slots = jnp.arange(pair_rows, dtype=jnp.int32)
    positions = priors[:, None] + slots[None, :]
    query_rot = rotary(query_in.reshape(sources, pair_rows, qcols // HD, HD), positions).astype(
        jnp.bfloat16
    ).reshape(sources, pair_rows, qcols)
    key_rot = rotary(key_in.reshape(sources, pair_rows, kv_heads, HD), positions).astype(
        jnp.bfloat16
    ).reshape(sources, pair_rows, kcols)
    pool_pages = cache_keys.shape[0]
    smem = pl.BlockSpec(memory_space=pltpu.SMEM)
    vmem = pl.BlockSpec(memory_space=pltpu.VMEM)
    return pl.pallas_call(
        attention_kernel,
        out_shape=(
            jax.ShapeDtypeStruct((sources, pair_rows, qcols), jnp.bfloat16),
            jax.ShapeDtypeStruct(cache_keys.shape, cache_keys.dtype),
            jax.ShapeDtypeStruct(cache_values.shape, cache_values.dtype),
        ),
        in_specs=[smem, smem, smem, vmem, vmem, vmem, vmem, vmem],
        out_specs=(vmem, vmem, vmem),
        scratch_shapes=[
            pltpu.VMEM((CONTEXT, kcols), jnp.bfloat16),
            pltpu.VMEM((CONTEXT, kcols), jnp.bfloat16),
        ],
        compiler_params=pltpu.CompilerParams(vmem_limit_bytes=48 * 1024 * 1024),
    )(table, priors, lengths, query_rot, key_rot, value_in, cache_keys, cache_values)


def body(
    hidden_in,
    attn_gain,
    mlp_gain,
    w_query,
    w_key,
    w_value,
    w_out,
    w_gate,
    w_up,
    w_down,
    cache_k,
    cache_v,
    owner_of_row,
    new_len,
    prior_len,
    page_table,
):
    peers = lax.axis_size(REQ)
    groups = lax.axis_size("grp")
    row_count = hidden_in.shape[0]
    pair_rows = 2 * row_count // peers
    quarter = row_count // groups
    group_index = lax.axis_index("grp")
    gate_w = lax.all_gather(w_gate, "ry", axis=1, tiled=True)
    up_w = lax.all_gather(w_up, "ry", axis=1, tiled=True)
    ring = lax.axis_size("ry")
    down_parts = [w_down] + [
        lax.ppermute(w_down, "ry", [(i, (i + shift) % ring) for i in range(ring)])
        for shift in range(1, ring)
    ]
    out_parts = [w_out] + [
        lax.ppermute(w_out, "grp", [(i, (i + shift) % groups) for i in range(groups)])
        for shift in range(1, groups)
    ]
    normed = normalize(hidden_in.astype(jnp.float32), attn_gain).astype(jnp.bfloat16)
    qcols = w_query.shape[1]
    kcols = w_key.shape[1]
    query_rows = jnp.dot(normed, w_query, preferred_element_type=jnp.float32).astype(jnp.bfloat16)
    key_rows = jnp.dot(normed, w_key, preferred_element_type=jnp.float32).astype(jnp.bfloat16)
    value_rows = jnp.dot(normed, w_value, preferred_element_type=jnp.float32).astype(jnp.bfloat16)
    qkv_rows = jnp.concatenate([query_rows, key_rows, value_rows], axis=1)
    gather_rows, back_rows = source_layout(owner_of_row, peers, pair_rows)
    send_qkv = jnp.take(qkv_rows, gather_rows, axis=0, mode="fill", fill_value=0).reshape(
        peers, pair_rows, -1
    )
    recv_qkv = lax.all_to_all(send_qkv, REQ, split_axis=0, concat_axis=0, tiled=True)
    recv_query = recv_qkv[..., :qcols]
    recv_key = recv_qkv[..., qcols : qcols + kcols]
    recv_value = recv_qkv[..., qcols + kcols :]
    mixed, keys_out, values_out = owner_attention(
        recv_query, recv_key, recv_value, cache_k, cache_v, new_len[0], prior_len[0], page_table[0]
    )
    mixed = lax.optimization_barrier(mixed)
    returned = lax.all_to_all(mixed, REQ, split_axis=0, concat_axis=0, tiled=True)
    gate_w, up_w, out_parts, returned = lax.optimization_barrier((gate_w, up_w, out_parts, returned))
    attn_rows = jnp.take(returned.reshape(peers * pair_rows, -1), back_rows, axis=0)
    quarters = lax.all_to_all(
        attn_rows.reshape(groups, quarter, -1), "grp", split_axis=0, concat_axis=0, tiled=True
    )
    attn_part = None
    for shift, part in enumerate(out_parts):
        block = (group_index - shift) % groups
        term = jnp.dot(quarters[block], part, preferred_element_type=jnp.float32)
        term = term.astype(jnp.bfloat16).astype(jnp.float32)
        attn_part = term if attn_part is None else attn_part + term
    own_rows = lax.dynamic_slice_in_dim(hidden_in, group_index * quarter, quarter, 0).astype(
        jnp.float32
    )
    residual = own_rows + RESIDUAL_MULT * attn_part
    mlp_in = normalize(residual, mlp_gain).astype(jnp.bfloat16)
    piece = lax.all_gather(mlp_in, "rzc", axis=0, tiled=True)
    gate = jnp.dot(piece, gate_w, preferred_element_type=jnp.float32)
    upper = jnp.dot(piece, up_w, preferred_element_type=jnp.float32)
    hidden = (jax.nn.silu(gate) * upper).astype(jnp.bfloat16)
    down_parts, hidden = lax.optimization_barrier((down_parts, hidden))
    units = w_down.shape[0]
    partial = None
    for shift, part in enumerate(down_parts):
        block = (lax.axis_index("ry") - shift) % ring
        term = jnp.dot(
            lax.dynamic_slice_in_dim(hidden, block * units, units, axis=1),
            part,
            preferred_element_type=jnp.float32,
        )
        partial = term if partial is None else partial + term
    down = lax.psum_scatter(
        partial.astype(jnp.bfloat16),
        "rzc",
        scatter_dimension=0,
        tiled=True,
    ).astype(jnp.float32)
    layer_out = (residual + RESIDUAL_MULT * down).astype(jnp.bfloat16)
    return (layer_out, keys_out, values_out)


REQ = ("ry", "rzc")


def solution(mesh):
    req_size = mesh.shape["req"]
    major = 4
    inner = Mesh(
        mesh.devices.reshape(major, req_size // major, mesh.shape["grp"]), ("ry", "rzc", "grp")
    )
    in_specs = (
        P(REQ, None),
        P(),
        P(),
        P(None, "grp"),
        P(None, "grp"),
        P(None, "grp"),
        P("grp", None),
        P(None, REQ),
        P(None, REQ),
        P(REQ, None),
        P(REQ, None, "grp"),
        P(REQ, None, "grp"),
        P(REQ),
        P(REQ, None),
        P(REQ, None),
        P(REQ, None),
    )
    out_specs = (P(REQ + ("grp",), None), P(REQ, None, "grp"), P(REQ, None, "grp"))
    return jax.shard_map(body, mesh=inner, in_specs=in_specs, out_specs=out_specs, check_vma=False)
```

```python
import jax
import jax.numpy as jnp
from jax import lax
from jax.experimental import pallas as pl
from jax.experimental.pallas import tpu as pltpu
from jax.sharding import Mesh, PartitionSpec as P

HD = 64
PAGE = 16
MAXP = 16
CONTEXT = 256


EPSILON = 1e-05
RESIDUAL_MULT = 0.22
SCORE_MULT = 0.015625
ROPE_BASE = 10000000.0


def normalize(values, gain):
    mean_square = jnp.mean(values * values, axis=-1, keepdims=True)
    return values * lax.rsqrt(mean_square + EPSILON) * gain


def rotary(values, positions):
    dim = values.shape[-1]
    half = dim // 2
    freq = jnp.power(ROPE_BASE, -2.0 * jnp.arange(half, dtype=jnp.int32).astype(jnp.float32) / dim)
    angle = positions.astype(jnp.float32)[:, :, None] * freq
    cosine = jnp.cos(angle)[:, :, None, :]
    sine = jnp.sin(angle)[:, :, None, :]
    first = values[..., :half].astype(jnp.float32)
    second = values[..., half:].astype(jnp.float32)
    return jnp.concatenate(
        [first * cosine - second * sine, second * cosine + first * sine], axis=-1
    )


def source_layout(owner_block, peers, pair_rows):
    row_count = owner_block.shape[0]
    owners = jnp.arange(peers, dtype=jnp.int32)
    member = owner_block[None, :] == owners[:, None]
    counts = jnp.sum(member.astype(jnp.int32), axis=1)
    row_ids = jnp.arange(row_count, dtype=jnp.int32)
    starts = jnp.min(jnp.where(member, row_ids[None, :], row_count), axis=1)
    slots = jnp.arange(pair_rows, dtype=jnp.int32)
    gather_rows = jnp.where(
        slots[None, :] < counts[:, None], starts[:, None] + slots[None, :], row_count
    )
    row_start = jnp.sum(jnp.where(member, starts[:, None], 0), axis=0)
    back_rows = owner_block * pair_rows + (row_ids - row_start)
    return (gather_rows.reshape(-1), back_rows)


def attention_kernel(table_ref, prior_ref, len_ref, qkv_ref, k_ref, cos_ref, sin_ref, ck_ref,
                     cv_ref, out_ref, nk_ref, nv_ref, kbuf, vbuf):
    sources, pair_rows, kcols = k_ref.shape
    qcols = qkv_ref.shape[-1] - 2 * kcols
    kv_heads = kcols // HD
    group = qcols // kcols
    half = HD // 2

    def per_source(s, carry):
        prior = prior_ref[s]
        length = len_ref[s]
        for i in range(MAXP):
            page = table_ref[s * MAXP + i]
            kbuf[i * PAGE:(i + 1) * PAGE, :] = ck_ref[page]
            vbuf[i * PAGE:(i + 1) * PAGE, :] = cv_ref[page]
        j_col = lax.broadcasted_iota(jnp.int32, (CONTEXT, pair_rows), 0)
        t_row = lax.broadcasted_iota(jnp.int32, (CONTEXT, pair_rows), 1)
        select = jnp.logical_and(j_col == prior + t_row, t_row < length).astype(jnp.bfloat16)
        j_only = lax.broadcasted_iota(jnp.int32, (CONTEXT, kcols), 0)
        fresh = jnp.logical_and(j_only >= prior, j_only < prior + length)
        v_in = qkv_ref[s, :, qcols + kcols:qcols + 2 * kcols]
        k_new = jnp.dot(select, k_ref[s], preferred_element_type=jnp.float32).astype(jnp.bfloat16)
        v_new = jnp.dot(select, v_in, preferred_element_type=jnp.float32).astype(jnp.bfloat16)
        keys = jnp.where(fresh, k_new, kbuf[...])
        values = jnp.where(fresh, v_new, vbuf[...])
        for i in range(MAXP):
            page = table_ref[s * MAXP + i]
            nk_ref[page] = keys[i * PAGE:(i + 1) * PAGE, :]
            nv_ref[page] = values[i * PAGE:(i + 1) * PAGE, :]
        cosine = cos_ref[s]
        sine = sin_ref[s]
        rows = group * pair_rows
        r_idx = lax.broadcasted_iota(jnp.int32, (rows, CONTEXT), 0)
        j_idx = lax.broadcasted_iota(jnp.int32, (rows, CONTEXT), 1)
        allowed = j_idx <= prior + r_idx % pair_rows
        for h in range(kv_heads):
            firsts, seconds = [], []
            for g in range(group):
                c = h * group + g
                u = qkv_ref[s, :, c * HD:c * HD + half].astype(jnp.float32)
                w = qkv_ref[s, :, c * HD + half:(c + 1) * HD].astype(jnp.float32)
                firsts.append((u * cosine - w * sine).astype(jnp.bfloat16))
                seconds.append((w * cosine + u * sine).astype(jnp.bfloat16))
            q_first = jnp.concatenate(firsts, axis=0)
            q_second = jnp.concatenate(seconds, axis=0)
            k_first = keys[:, h * HD:h * HD + half]
            k_second = keys[:, h * HD + half:(h + 1) * HD]
            v_h = values[:, h * HD:(h + 1) * HD]
            dims = (((1,), (1,)), ((), ()))
            scores = lax.dot_general(q_first, k_first, dims, preferred_element_type=jnp.float32)
            scores = scores + lax.dot_general(
                q_second, k_second, dims, preferred_element_type=jnp.float32
            )
            scores = jnp.where(allowed, scores * SCORE_MULT, -jnp.inf)
            top = jnp.max(scores, axis=-1, keepdims=True)
            weights = jnp.exp(scores - top)
            probs = (weights / jnp.sum(weights, axis=-1, keepdims=True)).astype(jnp.bfloat16)
            mixed = jnp.dot(probs, v_h, preferred_element_type=jnp.float32).astype(jnp.bfloat16)
            for g in range(group):
                c = h * group + g
                out_ref[s, :, c * HD:(c + 1) * HD] = mixed[g * pair_rows:(g + 1) * pair_rows, :]
        return carry

    lax.fori_loop(0, sources, per_source, 0)


def owner_attention(qkv_in, qcols, cache_keys, cache_values, lengths, priors, table):
    sources, pair_rows, width = qkv_in.shape
    kcols = (width - qcols) // 2
    kv_heads = kcols // HD
    slots = jnp.arange(pair_rows, dtype=jnp.int32)
    positions = priors[:, None] + slots[None, :]
    key_in = qkv_in[..., qcols:qcols + kcols]
    key_rot = rotary(key_in.reshape(sources, pair_rows, kv_heads, HD), positions).astype(
        jnp.bfloat16
    ).reshape(sources, pair_rows, kcols)
    freq = jnp.power(ROPE_BASE, -2.0 * jnp.arange(HD // 2, dtype=jnp.int32).astype(jnp.float32) / HD)
    angle = positions.astype(jnp.float32)[:, :, None] * freq
    cosine = jnp.cos(angle)
    sine = jnp.sin(angle)
    smem = pl.BlockSpec(memory_space=pltpu.SMEM)
    vmem = pl.BlockSpec(memory_space=pltpu.VMEM)
    return pl.pallas_call(
        attention_kernel,
        out_shape=(
            jax.ShapeDtypeStruct((sources, pair_rows, qcols), jnp.bfloat16),
            jax.ShapeDtypeStruct(cache_keys.shape, cache_keys.dtype),
            jax.ShapeDtypeStruct(cache_values.shape, cache_values.dtype),
        ),
        in_specs=[smem, smem, smem] + [vmem] * 6,
        out_specs=(vmem, vmem, vmem),
        scratch_shapes=[
            pltpu.VMEM((CONTEXT, kcols), jnp.bfloat16),
            pltpu.VMEM((CONTEXT, kcols), jnp.bfloat16),
        ],
        compiler_params=pltpu.CompilerParams(vmem_limit_bytes=48 * 1024 * 1024),
    )(table, priors, lengths, qkv_in, key_rot, cosine, sine, cache_keys, cache_values)


def body(
    hidden_in,
    attn_gain,
    mlp_gain,
    w_query,
    w_key,
    w_value,
    w_out,
    w_gate,
    w_up,
    w_down,
    cache_k,
    cache_v,
    owner_of_row,
    new_len,
    prior_len,
    page_table,
):
    peers = lax.axis_size(REQ)
    groups = lax.axis_size("grp")
    row_count = hidden_in.shape[0]
    pair_rows = 2 * row_count // peers
    quarter = row_count // groups
    group_index = lax.axis_index("grp")
    gate_w = lax.all_gather(w_gate, "ry", axis=1, tiled=True)
    up_w = lax.all_gather(w_up, "ry", axis=1, tiled=True)
    ring = lax.axis_size("ry")
    down_parts = [w_down] + [
        lax.ppermute(w_down, "ry", [(i, (i + shift) % ring) for i in range(ring)])
        for shift in range(1, ring)
    ]
    out_parts = [w_out] + [
        lax.ppermute(w_out, "grp", [(i, (i + shift) % groups) for i in range(groups)])
        for shift in range(1, groups)
    ]
    normed = normalize(hidden_in.astype(jnp.float32), attn_gain).astype(jnp.bfloat16)
    qcols = w_query.shape[1]
    kcols = w_key.shape[1]
    query_rows = jnp.dot(normed, w_query, preferred_element_type=jnp.float32).astype(jnp.bfloat16)
    key_rows = jnp.dot(normed, w_key, preferred_element_type=jnp.float32).astype(jnp.bfloat16)
    value_rows = jnp.dot(normed, w_value, preferred_element_type=jnp.float32).astype(jnp.bfloat16)
    qkv_rows = jnp.concatenate([query_rows, key_rows, value_rows], axis=1)
    gather_rows, back_rows = source_layout(owner_of_row, peers, pair_rows)
    send_qkv = jnp.take(qkv_rows, gather_rows, axis=0, mode="fill", fill_value=0).reshape(
        peers, pair_rows, -1
    )
    recv_qkv = lax.all_to_all(send_qkv, REQ, split_axis=0, concat_axis=0, tiled=True)
    mixed, keys_out, values_out = owner_attention(
        recv_qkv, qcols, cache_k, cache_v, new_len[0], prior_len[0], page_table[0]
    )
    mixed = lax.optimization_barrier(mixed)
    returned = lax.all_to_all(mixed, REQ, split_axis=0, concat_axis=0, tiled=True)
    gate_w, up_w, out_parts, returned = lax.optimization_barrier((gate_w, up_w, out_parts, returned))
    attn_rows = jnp.take(returned.reshape(peers * pair_rows, -1), back_rows, axis=0)
    quarters = lax.all_to_all(
        attn_rows.reshape(groups, quarter, -1), "grp", split_axis=0, concat_axis=0, tiled=True
    )
    attn_part = None
    for shift, part in enumerate(out_parts):
        block = (group_index - shift) % groups
        term = jnp.dot(quarters[block], part, preferred_element_type=jnp.float32)
        term = term.astype(jnp.bfloat16).astype(jnp.float32)
        attn_part = term if attn_part is None else attn_part + term
    own_rows = lax.dynamic_slice_in_dim(hidden_in, group_index * quarter, quarter, 0).astype(
        jnp.float32
    )
    residual = own_rows + RESIDUAL_MULT * attn_part
    mlp_in = normalize(residual, mlp_gain).astype(jnp.bfloat16)
    piece = lax.all_gather(mlp_in, "rzc", axis=0, tiled=True)
    gate = jnp.dot(piece, gate_w, preferred_element_type=jnp.float32)
    upper = jnp.dot(piece, up_w, preferred_element_type=jnp.float32)
    hidden = (jax.nn.silu(gate) * upper).astype(jnp.bfloat16)
    down_parts, hidden = lax.optimization_barrier((down_parts, hidden))
    units = w_down.shape[0]
    partial = None
    for shift, part in enumerate(down_parts):
        block = (lax.axis_index("ry") - shift) % ring
        term = jnp.dot(
            lax.dynamic_slice_in_dim(hidden, block * units, units, axis=1),
            part,
            preferred_element_type=jnp.float32,
        )
        partial = term if partial is None else partial + term
    down = lax.psum_scatter(
        partial.astype(jnp.bfloat16),
        "rzc",
        scatter_dimension=0,
        tiled=True,
    ).astype(jnp.float32)
    layer_out = (residual + RESIDUAL_MULT * down).astype(jnp.bfloat16)
    return (layer_out, keys_out, values_out)


REQ = ("ry", "rzc")


def solution(mesh):
    req_size = mesh.shape["req"]
    major = 4
    inner = Mesh(
        mesh.devices.reshape(major, req_size // major, mesh.shape["grp"]), ("ry", "rzc", "grp")
    )
    in_specs = (
        P(REQ, None),
        P(),
        P(),
        P(None, "grp"),
        P(None, "grp"),
        P(None, "grp"),
        P("grp", None),
        P(None, REQ),
        P(None, REQ),
        P(REQ, None),
        P(REQ, None, "grp"),
        P(REQ, None, "grp"),
        P(REQ),
        P(REQ, None),
        P(REQ, None),
        P(REQ, None),
    )
    out_specs = (P(REQ + ("grp",), None), P(REQ, None, "grp"), P(REQ, None, "grp"))
    return jax.shard_map(body, mesh=inner, in_specs=in_specs, out_specs=out_specs, check_vma=False)
```

```python
import jax
import jax.numpy as jnp
from jax import lax
from jax.experimental import pallas as pl
from jax.experimental.pallas import tpu as pltpu
from jax.sharding import Mesh, PartitionSpec as P

HD = 64
PAGE = 16
MAXP = 16
CONTEXT = 256


EPSILON = 1e-05
RESIDUAL_MULT = 0.22
SCORE_MULT = 0.015625
ROPE_BASE = 10000000.0


def normalize(values, gain):
    mean_square = jnp.mean(values * values, axis=-1, keepdims=True)
    return values * lax.rsqrt(mean_square + EPSILON) * gain


def rotary(values, positions):
    dim = values.shape[-1]
    half = dim // 2
    freq = jnp.power(ROPE_BASE, -2.0 * jnp.arange(half, dtype=jnp.int32).astype(jnp.float32) / dim)
    angle = positions.astype(jnp.float32)[:, :, None] * freq
    cosine = jnp.cos(angle)[:, :, None, :]
    sine = jnp.sin(angle)[:, :, None, :]
    first = values[..., :half].astype(jnp.float32)
    second = values[..., half:].astype(jnp.float32)
    return jnp.concatenate(
        [first * cosine - second * sine, second * cosine + first * sine], axis=-1
    )


def source_layout(owner_block, peers, pair_rows):
    row_count = owner_block.shape[0]
    owners = jnp.arange(peers, dtype=jnp.int32)
    member = owner_block[None, :] == owners[:, None]
    counts = jnp.sum(member.astype(jnp.int32), axis=1)
    row_ids = jnp.arange(row_count, dtype=jnp.int32)
    starts = jnp.min(jnp.where(member, row_ids[None, :], row_count), axis=1)
    slots = jnp.arange(pair_rows, dtype=jnp.int32)
    gather_rows = jnp.where(
        slots[None, :] < counts[:, None], starts[:, None] + slots[None, :], row_count
    )
    row_start = jnp.sum(jnp.where(member, starts[:, None], 0), axis=0)
    back_rows = owner_block * pair_rows + (row_ids - row_start)
    return (gather_rows.reshape(-1), back_rows)


def attention_kernel(table_ref, prior_ref, len_ref, q_ref, k_ref, v_ref, ck_ref, cv_ref,
                     out_ref, nk_ref, nv_ref, kbuf, vbuf):
    sources, pair_rows, qcols = q_ref.shape
    kcols = k_ref.shape[-1]
    kv_heads = kcols // HD
    group = qcols // kcols

    def per_source(s, carry):
        prior = prior_ref[s]
        length = len_ref[s]
        for i in range(MAXP):
            page = table_ref[s * MAXP + i]
            kbuf[i * PAGE:(i + 1) * PAGE, :] = ck_ref[page]
            vbuf[i * PAGE:(i + 1) * PAGE, :] = cv_ref[page]
        j_col = lax.broadcasted_iota(jnp.int32, (CONTEXT, pair_rows), 0)
        t_row = lax.broadcasted_iota(jnp.int32, (CONTEXT, pair_rows), 1)
        select = jnp.logical_and(j_col == prior + t_row, t_row < length).astype(jnp.bfloat16)
        j_only = lax.broadcasted_iota(jnp.int32, (CONTEXT, kcols), 0)
        fresh = jnp.logical_and(j_only >= prior, j_only < prior + length)
        k_new = jnp.dot(select, k_ref[s], preferred_element_type=jnp.float32).astype(jnp.bfloat16)
        v_new = jnp.dot(select, v_ref[s], preferred_element_type=jnp.float32).astype(jnp.bfloat16)
        keys = jnp.where(fresh, k_new, kbuf[...])
        values = jnp.where(fresh, v_new, vbuf[...])
        for i in range(MAXP):
            page = table_ref[s * MAXP + i]
            nk_ref[page] = keys[i * PAGE:(i + 1) * PAGE, :]
            nv_ref[page] = values[i * PAGE:(i + 1) * PAGE, :]
        q_all = q_ref[s]
        rows = group * pair_rows
        r_idx = lax.broadcasted_iota(jnp.int32, (rows, CONTEXT), 0)
        j_idx = lax.broadcasted_iota(jnp.int32, (rows, CONTEXT), 1)
        allowed = j_idx <= prior + r_idx % pair_rows
        for h in range(kv_heads):
            q_h = jnp.concatenate(
                [q_all[:, (h * group + g) * HD:(h * group + g + 1) * HD] for g in range(group)],
                axis=0,
            )
            k_h = keys[:, h * HD:(h + 1) * HD]
            v_h = values[:, h * HD:(h + 1) * HD]
            scores = lax.dot_general(
                q_h, k_h, (((1,), (1,)), ((), ())), preferred_element_type=jnp.float32
            ) * SCORE_MULT
            scores = jnp.where(allowed, scores, -jnp.inf)
            top = jnp.max(scores, axis=-1, keepdims=True)
            weights = jnp.exp(scores - top)
            probs = (weights / jnp.sum(weights, axis=-1, keepdims=True)).astype(jnp.bfloat16)
            mixed = jnp.dot(probs, v_h, preferred_element_type=jnp.float32).astype(jnp.bfloat16)
            for g in range(group):
                c = h * group + g
                out_ref[s, :, c * HD:(c + 1) * HD] = mixed[g * pair_rows:(g + 1) * pair_rows, :]
        return carry

    lax.fori_loop(0, sources, per_source, 0)


def owner_attention(query_in, key_in, value_in, cache_keys, cache_values, lengths, priors, table):
    sources, pair_rows, qcols = query_in.shape
    kcols = key_in.shape[-1]
    kv_heads = kcols // HD
    slots = jnp.arange(pair_rows, dtype=jnp.int32)
    positions = priors[:, None] + slots[None, :]
    query_rot = rotary(query_in.reshape(sources, pair_rows, qcols // HD, HD), positions).astype(
        jnp.bfloat16
    ).reshape(sources, pair_rows, qcols)
    key_rot = rotary(key_in.reshape(sources, pair_rows, kv_heads, HD), positions).astype(
        jnp.bfloat16
    ).reshape(sources, pair_rows, kcols)
    pool_pages = cache_keys.shape[0]
    smem = pl.BlockSpec(memory_space=pltpu.SMEM)
    vmem = pl.BlockSpec(memory_space=pltpu.VMEM)
    return pl.pallas_call(
        attention_kernel,
        out_shape=(
            jax.ShapeDtypeStruct((sources, pair_rows, qcols), jnp.bfloat16),
            jax.ShapeDtypeStruct(cache_keys.shape, cache_keys.dtype),
            jax.ShapeDtypeStruct(cache_values.shape, cache_values.dtype),
        ),
        in_specs=[smem, smem, smem, vmem, vmem, vmem, vmem, vmem],
        out_specs=(vmem, vmem, vmem),
        scratch_shapes=[
            pltpu.VMEM((CONTEXT, kcols), jnp.bfloat16),
            pltpu.VMEM((CONTEXT, kcols), jnp.bfloat16),
        ],
        compiler_params=pltpu.CompilerParams(vmem_limit_bytes=48 * 1024 * 1024),
    )(table, priors, lengths, query_rot, key_rot, value_in, cache_keys, cache_values)


def body(
    hidden_in,
    attn_gain,
    mlp_gain,
    w_query,
    w_key,
    w_value,
    w_out,
    w_gate,
    w_up,
    w_down,
    cache_k,
    cache_v,
    owner_of_row,
    new_len,
    prior_len,
    page_table,
):
    peers = lax.axis_size(REQ)
    groups = lax.axis_size("grp")
    row_count = hidden_in.shape[0]
    pair_rows = 2 * row_count // peers
    quarter = row_count // groups
    group_index = lax.axis_index("grp")
    gate_w = lax.all_gather(w_gate, "ry", axis=1, tiled=True)
    up_w = lax.all_gather(w_up, "ry", axis=1, tiled=True)
    ring = lax.axis_size("ry")
    down_parts = [w_down] + [
        lax.ppermute(w_down, "ry", [(i, (i + shift) % ring) for i in range(ring)])
        for shift in range(1, ring)
    ]
    out_parts = [w_out] + [
        lax.ppermute(w_out, "grp", [(i, (i + shift) % groups) for i in range(groups)])
        for shift in range(1, groups)
    ]
    normed = normalize(hidden_in.astype(jnp.float32), attn_gain).astype(jnp.bfloat16)
    qcols = w_query.shape[1]
    kcols = w_key.shape[1]
    query_rows = jnp.dot(normed, w_query, preferred_element_type=jnp.float32).astype(jnp.bfloat16)
    key_rows = jnp.dot(normed, w_key, preferred_element_type=jnp.float32).astype(jnp.bfloat16)
    value_rows = jnp.dot(normed, w_value, preferred_element_type=jnp.float32).astype(jnp.bfloat16)
    qkv_rows = jnp.concatenate([query_rows, key_rows, value_rows], axis=1)
    gather_rows, back_rows = source_layout(owner_of_row, peers, pair_rows)
    send_qkv = jnp.take(qkv_rows, gather_rows, axis=0, mode="fill", fill_value=0).reshape(
        peers, pair_rows, -1
    )
    recv_qkv = lax.all_to_all(send_qkv, REQ, split_axis=0, concat_axis=0, tiled=True)
    recv_query = recv_qkv[..., :qcols]
    recv_key = recv_qkv[..., qcols : qcols + kcols]
    recv_value = recv_qkv[..., qcols + kcols :]
    mixed, keys_out, values_out = owner_attention(
        recv_query, recv_key, recv_value, cache_k, cache_v, new_len[0], prior_len[0], page_table[0]
    )
    mixed = lax.optimization_barrier(mixed)
    returned = lax.all_to_all(mixed, REQ, split_axis=0, concat_axis=0, tiled=True)
    gate_w, up_w, out_parts, returned = lax.optimization_barrier((gate_w, up_w, out_parts, returned))
    attn_rows = jnp.take(returned.reshape(peers * pair_rows, -1), back_rows, axis=0)
    quarters = lax.all_to_all(
        attn_rows.reshape(groups, quarter, -1), "grp", split_axis=0, concat_axis=0, tiled=True
    )
    attn_part = None
    for shift, part in enumerate(out_parts):
        block = (group_index - shift) % groups
        term = jnp.dot(quarters[block], part, preferred_element_type=jnp.float32)
        term = term.astype(jnp.bfloat16).astype(jnp.float32)
        attn_part = term if attn_part is None else attn_part + term
    own_rows = lax.dynamic_slice_in_dim(hidden_in, group_index * quarter, quarter, 0).astype(
        jnp.float32
    )
    residual = own_rows + RESIDUAL_MULT * attn_part
    mlp_in = normalize(residual, mlp_gain).astype(jnp.bfloat16)
    piece = lax.all_gather(mlp_in, "rzc", axis=0, tiled=True)
    gate = jnp.dot(piece, gate_w, preferred_element_type=jnp.float32)
    upper = jnp.dot(piece, up_w, preferred_element_type=jnp.float32)
    hidden = (jax.nn.silu(gate) * upper).astype(jnp.bfloat16)
    down_parts, hidden = lax.optimization_barrier((down_parts, hidden))
    units = w_down.shape[0]
    hidden = jnp.concatenate(
        [
            lax.dynamic_slice_in_dim(
                hidden, ((lax.axis_index("ry") - shift) % ring) * units, units, axis=1
            )
            for shift in range(ring)
        ],
        axis=1,
    )
    partial = jnp.dot(
        hidden, jnp.concatenate(down_parts, axis=0), preferred_element_type=jnp.float32
    )
    down = lax.psum_scatter(
        partial.astype(jnp.bfloat16),
        "rzc",
        scatter_dimension=0,
        tiled=True,
    ).astype(jnp.float32)
    layer_out = (residual + RESIDUAL_MULT * down).astype(jnp.bfloat16)
    return (layer_out, keys_out, values_out)


REQ = ("ry", "rzc")


def solution(mesh):
    req_size = mesh.shape["req"]
    major = 4
    inner = Mesh(
        mesh.devices.reshape(major, req_size // major, mesh.shape["grp"]), ("ry", "rzc", "grp")
    )
    in_specs = (
        P(REQ, None),
        P(),
        P(),
        P(None, "grp"),
        P(None, "grp"),
        P(None, "grp"),
        P("grp", None),
        P(None, REQ),
        P(None, REQ),
        P(REQ, None),
        P(REQ, None, "grp"),
        P(REQ, None, "grp"),
        P(REQ),
        P(REQ, None),
        P(REQ, None),
        P(REQ, None),
    )
    out_specs = (P(REQ + ("grp",), None), P(REQ, None, "grp"), P(REQ, None, "grp"))
    return jax.shard_map(body, mesh=inner, in_specs=in_specs, out_specs=out_specs, check_vma=False)
```

```python
import jax
import jax.numpy as jnp
from jax import lax
from jax.experimental import pallas as pl
from jax.experimental.pallas import tpu as pltpu
from jax.sharding import Mesh, PartitionSpec as P

HD = 64
PAGE = 16
MAXP = 16
CONTEXT = 256


EPSILON = 1e-05
RESIDUAL_MULT = 0.22
SCORE_MULT = 0.015625
ROPE_BASE = 10000000.0


def normalize(values, gain):
    mean_square = jnp.mean(values * values, axis=-1, keepdims=True)
    return values * lax.rsqrt(mean_square + EPSILON) * gain


def rotary(values, positions):
    dim = values.shape[-1]
    half = dim // 2
    freq = jnp.power(ROPE_BASE, -2.0 * jnp.arange(half, dtype=jnp.int32).astype(jnp.float32) / dim)
    angle = positions.astype(jnp.float32)[:, :, None] * freq
    cosine = jnp.cos(angle)[:, :, None, :]
    sine = jnp.sin(angle)[:, :, None, :]
    first = values[..., :half].astype(jnp.float32)
    second = values[..., half:].astype(jnp.float32)
    return jnp.concatenate(
        [first * cosine - second * sine, second * cosine + first * sine], axis=-1
    )


def source_layout(owner_block, peers, pair_rows):
    row_count = owner_block.shape[0]
    owners = jnp.arange(peers, dtype=jnp.int32)
    member = owner_block[None, :] == owners[:, None]
    counts = jnp.sum(member.astype(jnp.int32), axis=1)
    row_ids = jnp.arange(row_count, dtype=jnp.int32)
    starts = jnp.min(jnp.where(member, row_ids[None, :], row_count), axis=1)
    slots = jnp.arange(pair_rows, dtype=jnp.int32)
    gather_rows = jnp.where(
        slots[None, :] < counts[:, None], starts[:, None] + slots[None, :], row_count
    )
    row_start = jnp.sum(jnp.where(member, starts[:, None], 0), axis=0)
    back_rows = owner_block * pair_rows + (row_ids - row_start)
    return (gather_rows.reshape(-1), back_rows)


def attention_kernel(table_ref, prior_ref, len_ref, q_ref, k_ref, v_ref, ck_ref, cv_ref,
                     out_ref, nk_ref, nv_ref, kbuf, vbuf):
    sources, pair_rows, qcols = q_ref.shape
    kcols = k_ref.shape[-1]
    kv_heads = kcols // HD
    group = qcols // kcols

    def per_source(s, carry):
        prior = prior_ref[s]
        length = len_ref[s]
        for i in range(MAXP):
            page = table_ref[s * MAXP + i]
            kbuf[i * PAGE:(i + 1) * PAGE, :] = ck_ref[page]
            vbuf[i * PAGE:(i + 1) * PAGE, :] = cv_ref[page]
        j_col = lax.broadcasted_iota(jnp.int32, (CONTEXT, pair_rows), 0)
        t_row = lax.broadcasted_iota(jnp.int32, (CONTEXT, pair_rows), 1)
        select = jnp.logical_and(j_col == prior + t_row, t_row < length).astype(jnp.bfloat16)
        j_only = lax.broadcasted_iota(jnp.int32, (CONTEXT, kcols), 0)
        fresh = jnp.logical_and(j_only >= prior, j_only < prior + length)
        k_new = jnp.dot(select, k_ref[s], preferred_element_type=jnp.float32).astype(jnp.bfloat16)
        v_new = jnp.dot(select, v_ref[s], preferred_element_type=jnp.float32).astype(jnp.bfloat16)
        keys = jnp.where(fresh, k_new, kbuf[...])
        values = jnp.where(fresh, v_new, vbuf[...])
        for i in range(MAXP):
            page = table_ref[s * MAXP + i]
            nk_ref[page] = keys[i * PAGE:(i + 1) * PAGE, :]
            nv_ref[page] = values[i * PAGE:(i + 1) * PAGE, :]
        q_all = q_ref[s]
        rows = group * pair_rows
        r_idx = lax.broadcasted_iota(jnp.int32, (rows, CONTEXT), 0)
        j_idx = lax.broadcasted_iota(jnp.int32, (rows, CONTEXT), 1)
        allowed = j_idx <= prior + r_idx % pair_rows
        for h in range(kv_heads):
            q_h = jnp.concatenate(
                [q_all[:, (h * group + g) * HD:(h * group + g + 1) * HD] for g in range(group)],
                axis=0,
            )
            k_h = keys[:, h * HD:(h + 1) * HD]
            v_h = values[:, h * HD:(h + 1) * HD]
            scores = lax.dot_general(
                q_h, k_h, (((1,), (1,)), ((), ())), preferred_element_type=jnp.float32
            ) * SCORE_MULT
            scores = jnp.where(allowed, scores, -jnp.inf)
            top = jnp.max(scores, axis=-1, keepdims=True)
            weights = jnp.exp(scores - top)
            probs = (weights / jnp.sum(weights, axis=-1, keepdims=True)).astype(jnp.bfloat16)
            mixed = jnp.dot(probs, v_h, preferred_element_type=jnp.float32).astype(jnp.bfloat16)
            for g in range(group):
                c = h * group + g
                out_ref[s, :, c * HD:(c + 1) * HD] = mixed[g * pair_rows:(g + 1) * pair_rows, :]
        return carry

    lax.fori_loop(0, sources, per_source, 0)


def owner_attention(query_in, key_in, value_in, cache_keys, cache_values, lengths, priors, table):
    sources, pair_rows, qcols = query_in.shape
    kcols = key_in.shape[-1]
    kv_heads = kcols // HD
    slots = jnp.arange(pair_rows, dtype=jnp.int32)
    positions = priors[:, None] + slots[None, :]
    query_rot = rotary(query_in.reshape(sources, pair_rows, qcols // HD, HD), positions).astype(
        jnp.bfloat16
    ).reshape(sources, pair_rows, qcols)
    key_rot = rotary(key_in.reshape(sources, pair_rows, kv_heads, HD), positions).astype(
        jnp.bfloat16
    ).reshape(sources, pair_rows, kcols)
    pool_pages = cache_keys.shape[0]
    smem = pl.BlockSpec(memory_space=pltpu.SMEM)
    vmem = pl.BlockSpec(memory_space=pltpu.VMEM)
    return pl.pallas_call(
        attention_kernel,
        out_shape=(
            jax.ShapeDtypeStruct((sources, pair_rows, qcols), jnp.bfloat16),
            jax.ShapeDtypeStruct(cache_keys.shape, cache_keys.dtype),
            jax.ShapeDtypeStruct(cache_values.shape, cache_values.dtype),
        ),
        in_specs=[smem, smem, smem, vmem, vmem, vmem, vmem, vmem],
        out_specs=(vmem, vmem, vmem),
        scratch_shapes=[
            pltpu.VMEM((CONTEXT, kcols), jnp.bfloat16),
            pltpu.VMEM((CONTEXT, kcols), jnp.bfloat16),
        ],
        compiler_params=pltpu.CompilerParams(vmem_limit_bytes=48 * 1024 * 1024),
    )(table, priors, lengths, query_rot, key_rot, value_in, cache_keys, cache_values)


def body(
    hidden_in,
    attn_gain,
    mlp_gain,
    w_query,
    w_key,
    w_value,
    w_out,
    w_gate,
    w_up,
    w_down,
    cache_k,
    cache_v,
    owner_of_row,
    new_len,
    prior_len,
    page_table,
):
    peers = lax.axis_size(REQ)
    groups = lax.axis_size("grp")
    row_count = hidden_in.shape[0]
    pair_rows = 2 * row_count // peers
    quarter = row_count // groups
    group_index = lax.axis_index("grp")
    gate_up_w = lax.all_gather(jnp.concatenate([w_gate, w_up], axis=1), "ry", axis=1, tiled=True)
    ring = lax.axis_size("ry")
    down_parts = [w_down] + [
        lax.ppermute(w_down, "ry", [(i, (i + shift) % ring) for i in range(ring)])
        for shift in range(1, ring)
    ]
    out_parts = [w_out] + [
        lax.ppermute(w_out, "grp", [(i, (i + shift) % groups) for i in range(groups)])
        for shift in range(1, groups)
    ]
    normed = normalize(hidden_in.astype(jnp.float32), attn_gain).astype(jnp.bfloat16)
    qcols = w_query.shape[1]
    kcols = w_key.shape[1]
    query_rows = jnp.dot(normed, w_query, preferred_element_type=jnp.float32).astype(jnp.bfloat16)
    key_rows = jnp.dot(normed, w_key, preferred_element_type=jnp.float32).astype(jnp.bfloat16)
    value_rows = jnp.dot(normed, w_value, preferred_element_type=jnp.float32).astype(jnp.bfloat16)
    qkv_rows = jnp.concatenate([query_rows, key_rows, value_rows], axis=1)
    gather_rows, back_rows = source_layout(owner_of_row, peers, pair_rows)
    send_qkv = jnp.take(qkv_rows, gather_rows, axis=0, mode="fill", fill_value=0).reshape(
        peers, pair_rows, -1
    )
    recv_qkv = lax.all_to_all(send_qkv, REQ, split_axis=0, concat_axis=0, tiled=True)
    recv_query = recv_qkv[..., :qcols]
    recv_key = recv_qkv[..., qcols : qcols + kcols]
    recv_value = recv_qkv[..., qcols + kcols :]
    mixed, keys_out, values_out = owner_attention(
        recv_query, recv_key, recv_value, cache_k, cache_v, new_len[0], prior_len[0], page_table[0]
    )
    mixed = lax.optimization_barrier(mixed)
    returned = lax.all_to_all(mixed, REQ, split_axis=0, concat_axis=0, tiled=True)
    gate_up_w, out_parts, returned = lax.optimization_barrier((gate_up_w, out_parts, returned))
    attn_rows = jnp.take(returned.reshape(peers * pair_rows, -1), back_rows, axis=0)
    quarters = lax.all_to_all(
        attn_rows.reshape(groups, quarter, -1), "grp", split_axis=0, concat_axis=0, tiled=True
    )
    attn_part = None
    for shift, part in enumerate(out_parts):
        block = (group_index - shift) % groups
        term = jnp.dot(quarters[block], part, preferred_element_type=jnp.float32)
        term = term.astype(jnp.bfloat16).astype(jnp.float32)
        attn_part = term if attn_part is None else attn_part + term
    own_rows = lax.dynamic_slice_in_dim(hidden_in, group_index * quarter, quarter, 0).astype(
        jnp.float32
    )
    residual = own_rows + RESIDUAL_MULT * attn_part
    mlp_in = normalize(residual, mlp_gain).astype(jnp.bfloat16)
    piece = lax.all_gather(mlp_in, "rzc", axis=0, tiled=True)
    both = jnp.dot(piece, gate_up_w, preferred_element_type=jnp.float32)
    width = w_gate.shape[1]
    hidden = jnp.concatenate(
        [
            jax.nn.silu(both[:, 2 * k * width:(2 * k + 1) * width])
            * both[:, (2 * k + 1) * width:(2 * k + 2) * width]
            for k in range(ring)
        ],
        axis=1,
    ).astype(jnp.bfloat16)
    down_parts, hidden = lax.optimization_barrier((down_parts, hidden))
    units = w_down.shape[0]
    hidden = jnp.concatenate(
        [
            lax.dynamic_slice_in_dim(
                hidden, ((lax.axis_index("ry") - shift) % ring) * units, units, axis=1
            )
            for shift in range(ring)
        ],
        axis=1,
    )
    partial = jnp.dot(
        hidden, jnp.concatenate(down_parts, axis=0), preferred_element_type=jnp.float32
    )
    down = lax.psum_scatter(
        partial.astype(jnp.bfloat16),
        "rzc",
        scatter_dimension=0,
        tiled=True,
    ).astype(jnp.float32)
    layer_out = (residual + RESIDUAL_MULT * down).astype(jnp.bfloat16)
    return (layer_out, keys_out, values_out)


REQ = ("ry", "rzc")


def solution(mesh):
    req_size = mesh.shape["req"]
    major = 4
    inner = Mesh(
        mesh.devices.reshape(major, req_size // major, mesh.shape["grp"]), ("ry", "rzc", "grp")
    )
    in_specs = (
        P(REQ, None),
        P(),
        P(),
        P(None, "grp"),
        P(None, "grp"),
        P(None, "grp"),
        P("grp", None),
        P(None, REQ),
        P(None, REQ),
        P(REQ, None),
        P(REQ, None, "grp"),
        P(REQ, None, "grp"),
        P(REQ),
        P(REQ, None),
        P(REQ, None),
        P(REQ, None),
    )
    out_specs = (P(REQ + ("grp",), None), P(REQ, None, "grp"), P(REQ, None, "grp"))
    return jax.shard_map(body, mesh=inner, in_specs=in_specs, out_specs=out_specs, check_vma=False)
```

```python
import jax
import jax.numpy as jnp
from jax import lax
from jax.experimental import pallas as pl
from jax.experimental.pallas import tpu as pltpu
from jax.sharding import Mesh, PartitionSpec as P

HD = 64
PAGE = 16
MAXP = 16
CONTEXT = 256


EPSILON = 1e-05
RESIDUAL_MULT = 0.22
SCORE_MULT = 0.015625
ROPE_BASE = 10000000.0


def normalize(values, gain):
    mean_square = jnp.mean(values * values, axis=-1, keepdims=True)
    return values * lax.rsqrt(mean_square + EPSILON) * gain


def rotary(values, positions):
    dim = values.shape[-1]
    half = dim // 2
    freq = jnp.power(ROPE_BASE, -2.0 * jnp.arange(half, dtype=jnp.int32).astype(jnp.float32) / dim)
    angle = positions.astype(jnp.float32)[:, :, None] * freq
    cosine = jnp.cos(angle)[:, :, None, :]
    sine = jnp.sin(angle)[:, :, None, :]
    first = values[..., :half].astype(jnp.float32)
    second = values[..., half:].astype(jnp.float32)
    return jnp.concatenate(
        [first * cosine - second * sine, second * cosine + first * sine], axis=-1
    )


def source_layout(owner_block, peers, pair_rows):
    row_count = owner_block.shape[0]
    owners = jnp.arange(peers, dtype=jnp.int32)
    member = owner_block[None, :] == owners[:, None]
    counts = jnp.sum(member.astype(jnp.int32), axis=1)
    row_ids = jnp.arange(row_count, dtype=jnp.int32)
    starts = jnp.min(jnp.where(member, row_ids[None, :], row_count), axis=1)
    slots = jnp.arange(pair_rows, dtype=jnp.int32)
    gather_rows = jnp.where(
        slots[None, :] < counts[:, None], starts[:, None] + slots[None, :], row_count
    )
    row_start = jnp.sum(jnp.where(member, starts[:, None], 0), axis=0)
    back_rows = owner_block * pair_rows + (row_ids - row_start)
    return (gather_rows.reshape(-1), back_rows)


def attention_kernel(table_ref, prior_ref, len_ref, q_ref, k_ref, v_ref, ck_ref, cv_ref,
                     out_ref, nk_ref, nv_ref, kbuf, vbuf):
    sources, pair_rows, qcols = q_ref.shape
    kcols = k_ref.shape[-1]
    kv_heads = kcols // HD
    group = qcols // kcols

    def per_source(s, carry):
        prior = prior_ref[s]
        length = len_ref[s]
        for i in range(MAXP):
            page = table_ref[s * MAXP + i]
            kbuf[i * PAGE:(i + 1) * PAGE, :] = ck_ref[page]
            vbuf[i * PAGE:(i + 1) * PAGE, :] = cv_ref[page]
        j_col = lax.broadcasted_iota(jnp.int32, (CONTEXT, pair_rows), 0)
        t_row = lax.broadcasted_iota(jnp.int32, (CONTEXT, pair_rows), 1)
        select = jnp.logical_and(j_col == prior + t_row, t_row < length).astype(jnp.bfloat16)
        j_only = lax.broadcasted_iota(jnp.int32, (CONTEXT, kcols), 0)
        fresh = jnp.logical_and(j_only >= prior, j_only < prior + length)
        k_new = jnp.dot(select, k_ref[s], preferred_element_type=jnp.float32).astype(jnp.bfloat16)
        v_new = jnp.dot(select, v_ref[s], preferred_element_type=jnp.float32).astype(jnp.bfloat16)
        keys = jnp.where(fresh, k_new, kbuf[...])
        values = jnp.where(fresh, v_new, vbuf[...])
        for i in range(MAXP):
            page = table_ref[s * MAXP + i]
            nk_ref[page] = keys[i * PAGE:(i + 1) * PAGE, :]
            nv_ref[page] = values[i * PAGE:(i + 1) * PAGE, :]
        q_all = q_ref[s]
        rows = group * pair_rows
        r_idx = lax.broadcasted_iota(jnp.int32, (rows, CONTEXT), 0)
        j_idx = lax.broadcasted_iota(jnp.int32, (rows, CONTEXT), 1)
        allowed = j_idx <= prior + r_idx % pair_rows
        for h in range(kv_heads):
            q_h = jnp.concatenate(
                [q_all[:, (h * group + g) * HD:(h * group + g + 1) * HD] for g in range(group)],
                axis=0,
            )
            k_h = keys[:, h * HD:(h + 1) * HD]
            v_h = values[:, h * HD:(h + 1) * HD]
            scores = lax.dot_general(
                q_h, k_h, (((1,), (1,)), ((), ())), preferred_element_type=jnp.float32
            ) * SCORE_MULT
            scores = jnp.where(allowed, scores, -jnp.inf)
            top = jnp.max(scores, axis=-1, keepdims=True)
            weights = jnp.exp(scores - top)
            probs = (weights / jnp.sum(weights, axis=-1, keepdims=True)).astype(jnp.bfloat16)
            mixed = jnp.dot(probs, v_h, preferred_element_type=jnp.float32).astype(jnp.bfloat16)
            for g in range(group):
                c = h * group + g
                out_ref[s, :, c * HD:(c + 1) * HD] = mixed[g * pair_rows:(g + 1) * pair_rows, :]
        return carry

    lax.fori_loop(0, sources, per_source, 0)


def owner_attention(query_in, key_in, value_in, cache_keys, cache_values, lengths, priors, table):
    sources, pair_rows, qcols = query_in.shape
    kcols = key_in.shape[-1]
    kv_heads = kcols // HD
    slots = jnp.arange(pair_rows, dtype=jnp.int32)
    positions = priors[:, None] + slots[None, :]
    query_rot = rotary(query_in.reshape(sources, pair_rows, qcols // HD, HD), positions).astype(
        jnp.bfloat16
    ).reshape(sources, pair_rows, qcols)
    key_rot = rotary(key_in.reshape(sources, pair_rows, kv_heads, HD), positions).astype(
        jnp.bfloat16
    ).reshape(sources, pair_rows, kcols)
    pool_pages = cache_keys.shape[0]
    smem = pl.BlockSpec(memory_space=pltpu.SMEM)
    vmem = pl.BlockSpec(memory_space=pltpu.VMEM)
    return pl.pallas_call(
        attention_kernel,
        out_shape=(
            jax.ShapeDtypeStruct((sources, pair_rows, qcols), jnp.bfloat16),
            jax.ShapeDtypeStruct(cache_keys.shape, cache_keys.dtype),
            jax.ShapeDtypeStruct(cache_values.shape, cache_values.dtype),
        ),
        in_specs=[smem, smem, smem, vmem, vmem, vmem, vmem, vmem],
        out_specs=(vmem, vmem, vmem),
        scratch_shapes=[
            pltpu.VMEM((CONTEXT, kcols), jnp.bfloat16),
            pltpu.VMEM((CONTEXT, kcols), jnp.bfloat16),
        ],
        compiler_params=pltpu.CompilerParams(vmem_limit_bytes=48 * 1024 * 1024),
    )(table, priors, lengths, query_rot, key_rot, value_in, cache_keys, cache_values)


def body(
    hidden_in,
    attn_gain,
    mlp_gain,
    w_query,
    w_key,
    w_value,
    w_out,
    w_gate,
    w_up,
    w_down,
    cache_k,
    cache_v,
    owner_of_row,
    new_len,
    prior_len,
    page_table,
):
    peers = lax.axis_size(REQ)
    groups = lax.axis_size("grp")
    row_count = hidden_in.shape[0]
    pair_rows = 2 * row_count // peers
    quarter = row_count // groups
    group_index = lax.axis_index("grp")
    gate_up_w = lax.all_gather(jnp.concatenate([w_gate, w_up], axis=1), "ry", axis=1, tiled=True)
    ring = lax.axis_size("ry")
    down_parts = [w_down] + [
        lax.ppermute(w_down, "ry", [(i, (i + shift) % ring) for i in range(ring)])
        for shift in range(1, ring)
    ]
    out_parts = [w_out] + [
        lax.ppermute(w_out, "grp", [(i, (i + shift) % groups) for i in range(groups)])
        for shift in range(1, groups)
    ]
    normed = normalize(hidden_in.astype(jnp.float32), attn_gain).astype(jnp.bfloat16)
    qcols = w_query.shape[1]
    kcols = w_key.shape[1]
    query_rows = jnp.dot(normed, w_query, preferred_element_type=jnp.float32).astype(jnp.bfloat16)
    key_rows = jnp.dot(normed, w_key, preferred_element_type=jnp.float32).astype(jnp.bfloat16)
    value_rows = jnp.dot(normed, w_value, preferred_element_type=jnp.float32).astype(jnp.bfloat16)
    qkv_rows = jnp.concatenate([query_rows, key_rows, value_rows], axis=1)
    gather_rows, back_rows = source_layout(owner_of_row, peers, pair_rows)
    send_qkv = jnp.take(qkv_rows, gather_rows, axis=0, mode="fill", fill_value=0).reshape(
        peers, pair_rows, -1
    )
    recv_qkv = lax.all_to_all(send_qkv, REQ, split_axis=0, concat_axis=0, tiled=True)
    recv_query = recv_qkv[..., :qcols]
    recv_key = recv_qkv[..., qcols : qcols + kcols]
    recv_value = recv_qkv[..., qcols + kcols :]
    mixed, keys_out, values_out = owner_attention(
        recv_query, recv_key, recv_value, cache_k, cache_v, new_len[0], prior_len[0], page_table[0]
    )
    mixed = lax.optimization_barrier(mixed)
    returned = lax.all_to_all(mixed, REQ, split_axis=0, concat_axis=0, tiled=True)
    gate_up_w, out_parts, down_parts, returned = lax.optimization_barrier(
        (gate_up_w, out_parts, down_parts, returned)
    )
    attn_rows = jnp.take(returned.reshape(peers * pair_rows, -1), back_rows, axis=0)
    quarters = lax.all_to_all(
        attn_rows.reshape(groups, quarter, -1), "grp", split_axis=0, concat_axis=0, tiled=True
    )
    attn_part = None
    for shift, part in enumerate(out_parts):
        block = (group_index - shift) % groups
        term = jnp.dot(quarters[block], part, preferred_element_type=jnp.float32)
        term = term.astype(jnp.bfloat16).astype(jnp.float32)
        attn_part = term if attn_part is None else attn_part + term
    own_rows = lax.dynamic_slice_in_dim(hidden_in, group_index * quarter, quarter, 0).astype(
        jnp.float32
    )
    residual = own_rows + RESIDUAL_MULT * attn_part
    mlp_in = normalize(residual, mlp_gain).astype(jnp.bfloat16)
    piece = lax.all_gather(mlp_in, "rzc", axis=0, tiled=True)
    both = jnp.dot(piece, gate_up_w, preferred_element_type=jnp.float32)
    width = w_gate.shape[1]
    hidden = jnp.concatenate(
        [
            jax.nn.silu(both[:, 2 * k * width:(2 * k + 1) * width])
            * both[:, (2 * k + 1) * width:(2 * k + 2) * width]
            for k in range(ring)
        ],
        axis=1,
    ).astype(jnp.bfloat16)
    units = w_down.shape[0]
    hidden = jnp.concatenate(
        [
            lax.dynamic_slice_in_dim(
                hidden, ((lax.axis_index("ry") - shift) % ring) * units, units, axis=1
            )
            for shift in range(ring)
        ],
        axis=1,
    )
    partial = jnp.dot(
        hidden, jnp.concatenate(down_parts, axis=0), preferred_element_type=jnp.float32
    )
    down = lax.psum_scatter(
        partial.astype(jnp.bfloat16),
        "rzc",
        scatter_dimension=0,
        tiled=True,
    ).astype(jnp.float32)
    layer_out = (residual + RESIDUAL_MULT * down).astype(jnp.bfloat16)
    return (layer_out, keys_out, values_out)


REQ = ("ry", "rzc")


def solution(mesh):
    req_size = mesh.shape["req"]
    major = 4
    inner = Mesh(
        mesh.devices.reshape(major, req_size // major, mesh.shape["grp"]), ("ry", "rzc", "grp")
    )
    in_specs = (
        P(REQ, None),
        P(),
        P(),
        P(None, "grp"),
        P(None, "grp"),
        P(None, "grp"),
        P("grp", None),
        P(None, REQ),
        P(None, REQ),
        P(REQ, None),
        P(REQ, None, "grp"),
        P(REQ, None, "grp"),
        P(REQ),
        P(REQ, None),
        P(REQ, None),
        P(REQ, None),
    )
    out_specs = (P(REQ + ("grp",), None), P(REQ, None, "grp"), P(REQ, None, "grp"))
    return jax.shard_map(body, mesh=inner, in_specs=in_specs, out_specs=out_specs, check_vma=False)
```

```python
import jax
import jax.numpy as jnp
from jax import lax
from jax.experimental import pallas as pl
from jax.experimental.pallas import tpu as pltpu
from jax.sharding import Mesh, PartitionSpec as P

HD = 64
PAGE = 16
MAXP = 16
CONTEXT = 256


EPSILON = 1e-05
RESIDUAL_MULT = 0.22
SCORE_MULT = 0.015625
ROPE_BASE = 10000000.0


def normalize(values, gain):
    mean_square = jnp.mean(values * values, axis=-1, keepdims=True)
    return values * lax.rsqrt(mean_square + EPSILON) * gain


def rotary(values, positions):
    dim = values.shape[-1]
    half = dim // 2
    freq = jnp.power(ROPE_BASE, -2.0 * jnp.arange(half, dtype=jnp.int32).astype(jnp.float32) / dim)
    angle = positions.astype(jnp.float32)[:, :, None] * freq
    cosine = jnp.cos(angle)[:, :, None, :]
    sine = jnp.sin(angle)[:, :, None, :]
    first = values[..., :half].astype(jnp.float32)
    second = values[..., half:].astype(jnp.float32)
    return jnp.concatenate(
        [first * cosine - second * sine, second * cosine + first * sine], axis=-1
    )


def source_layout(owner_block, peers, pair_rows):
    row_count = owner_block.shape[0]
    owners = jnp.arange(peers, dtype=jnp.int32)
    member = owner_block[None, :] == owners[:, None]
    counts = jnp.sum(member.astype(jnp.int32), axis=1)
    row_ids = jnp.arange(row_count, dtype=jnp.int32)
    starts = jnp.min(jnp.where(member, row_ids[None, :], row_count), axis=1)
    slots = jnp.arange(pair_rows, dtype=jnp.int32)
    gather_rows = jnp.where(
        slots[None, :] < counts[:, None], starts[:, None] + slots[None, :], row_count
    )
    row_start = jnp.sum(jnp.where(member, starts[:, None], 0), axis=0)
    back_rows = owner_block * pair_rows + (row_ids - row_start)
    return (gather_rows.reshape(-1), back_rows)


def attention_kernel(table_ref, prior_ref, len_ref, q_ref, k_ref, v_ref, ck_ref, cv_ref,
                     out_ref, nk_ref, nv_ref, kbuf, vbuf):
    sources, pair_rows, qcols = q_ref.shape
    kcols = k_ref.shape[-1]
    kv_heads = kcols // HD
    group = qcols // kcols

    def per_source(s, carry):
        prior = prior_ref[s]
        length = len_ref[s]
        for i in range(MAXP):
            page = table_ref[s * MAXP + i]
            kbuf[i * PAGE:(i + 1) * PAGE, :] = ck_ref[page]
            vbuf[i * PAGE:(i + 1) * PAGE, :] = cv_ref[page]
        j_col = lax.broadcasted_iota(jnp.int32, (CONTEXT, pair_rows), 0)
        t_row = lax.broadcasted_iota(jnp.int32, (CONTEXT, pair_rows), 1)
        select = jnp.logical_and(j_col == prior + t_row, t_row < length).astype(jnp.bfloat16)
        j_only = lax.broadcasted_iota(jnp.int32, (CONTEXT, kcols), 0)
        fresh = jnp.logical_and(j_only >= prior, j_only < prior + length)
        k_new = jnp.dot(select, k_ref[s], preferred_element_type=jnp.float32).astype(jnp.bfloat16)
        v_new = jnp.dot(select, v_ref[s], preferred_element_type=jnp.float32).astype(jnp.bfloat16)
        keys = jnp.where(fresh, k_new, kbuf[...])
        values = jnp.where(fresh, v_new, vbuf[...])
        for i in range(MAXP):
            page = table_ref[s * MAXP + i]
            nk_ref[page] = keys[i * PAGE:(i + 1) * PAGE, :]
            nv_ref[page] = values[i * PAGE:(i + 1) * PAGE, :]
        q_all = q_ref[s]
        rows = group * pair_rows
        r_idx = lax.broadcasted_iota(jnp.int32, (rows, CONTEXT), 0)
        j_idx = lax.broadcasted_iota(jnp.int32, (rows, CONTEXT), 1)
        allowed = j_idx <= prior + r_idx % pair_rows
        for h in range(kv_heads):
            q_h = jnp.concatenate(
                [q_all[:, (h * group + g) * HD:(h * group + g + 1) * HD] for g in range(group)],
                axis=0,
            )
            k_h = keys[:, h * HD:(h + 1) * HD]
            v_h = values[:, h * HD:(h + 1) * HD]
            scores = lax.dot_general(
                q_h, k_h, (((1,), (1,)), ((), ())), preferred_element_type=jnp.float32
            ) * SCORE_MULT
            scores = jnp.where(allowed, scores, -jnp.inf)
            top = jnp.max(scores, axis=-1, keepdims=True)
            weights = jnp.exp(scores - top)
            probs = (weights / jnp.sum(weights, axis=-1, keepdims=True)).astype(jnp.bfloat16)
            mixed = jnp.dot(probs, v_h, preferred_element_type=jnp.float32).astype(jnp.bfloat16)
            for g in range(group):
                c = h * group + g
                out_ref[s, :, c * HD:(c + 1) * HD] = mixed[g * pair_rows:(g + 1) * pair_rows, :]
        return carry

    lax.fori_loop(0, sources, per_source, 0)


def owner_attention(query_in, key_in, value_in, cache_keys, cache_values, lengths, priors, table):
    sources, pair_rows, qcols = query_in.shape
    kcols = key_in.shape[-1]
    kv_heads = kcols // HD
    slots = jnp.arange(pair_rows, dtype=jnp.int32)
    positions = priors[:, None] + slots[None, :]
    query_rot = rotary(query_in.reshape(sources, pair_rows, qcols // HD, HD), positions).astype(
        jnp.bfloat16
    ).reshape(sources, pair_rows, qcols)
    key_rot = rotary(key_in.reshape(sources, pair_rows, kv_heads, HD), positions).astype(
        jnp.bfloat16
    ).reshape(sources, pair_rows, kcols)
    pool_pages = cache_keys.shape[0]
    smem = pl.BlockSpec(memory_space=pltpu.SMEM)
    vmem = pl.BlockSpec(memory_space=pltpu.VMEM)
    return pl.pallas_call(
        attention_kernel,
        out_shape=(
            jax.ShapeDtypeStruct((sources, pair_rows, qcols), jnp.bfloat16),
            jax.ShapeDtypeStruct(cache_keys.shape, cache_keys.dtype),
            jax.ShapeDtypeStruct(cache_values.shape, cache_values.dtype),
        ),
        in_specs=[smem, smem, smem, vmem, vmem, vmem, vmem, vmem],
        out_specs=(vmem, vmem, vmem),
        scratch_shapes=[
            pltpu.VMEM((CONTEXT, kcols), jnp.bfloat16),
            pltpu.VMEM((CONTEXT, kcols), jnp.bfloat16),
        ],
        compiler_params=pltpu.CompilerParams(vmem_limit_bytes=48 * 1024 * 1024),
    )(table, priors, lengths, query_rot, key_rot, value_in, cache_keys, cache_values)


def body(
    hidden_in,
    attn_gain,
    mlp_gain,
    w_query,
    w_key,
    w_value,
    w_out,
    w_gate,
    w_up,
    w_down,
    cache_k,
    cache_v,
    owner_of_row,
    new_len,
    prior_len,
    page_table,
):
    peers = lax.axis_size(REQ)
    groups = lax.axis_size("grp")
    row_count = hidden_in.shape[0]
    pair_rows = 2 * row_count // peers
    quarter = row_count // groups
    group_index = lax.axis_index("grp")
    gate_up_w = lax.all_gather(jnp.concatenate([w_gate, w_up], axis=1), "ry", axis=1, tiled=True)
    ring = lax.axis_size("ry")
    down_parts = [w_down] + [
        lax.ppermute(w_down, "ry", [(i, (i + shift) % ring) for i in range(ring)])
        for shift in range(1, ring)
    ]
    out_parts = [w_out] + [
        lax.ppermute(w_out, "grp", [(i, (i + shift) % groups) for i in range(groups)])
        for shift in range(1, groups)
    ]
    normed = normalize(hidden_in.astype(jnp.float32), attn_gain).astype(jnp.bfloat16)
    qcols = w_query.shape[1]
    kcols = w_key.shape[1]
    query_rows = jnp.dot(normed, w_query, preferred_element_type=jnp.float32).astype(jnp.bfloat16)
    key_rows = jnp.dot(normed, w_key, preferred_element_type=jnp.float32).astype(jnp.bfloat16)
    value_rows = jnp.dot(normed, w_value, preferred_element_type=jnp.float32).astype(jnp.bfloat16)
    qkv_rows = jnp.concatenate([query_rows, key_rows, value_rows], axis=1)
    gather_rows, back_rows = source_layout(owner_of_row, peers, pair_rows)
    send_qkv = jnp.take(qkv_rows, gather_rows, axis=0, mode="fill", fill_value=0).reshape(
        peers, pair_rows, -1
    )
    recv_qkv = lax.all_to_all(send_qkv, REQ, split_axis=0, concat_axis=0, tiled=True)
    recv_query = recv_qkv[..., :qcols]
    recv_key = recv_qkv[..., qcols : qcols + kcols]
    recv_value = recv_qkv[..., qcols + kcols :]
    mixed, keys_out, values_out = owner_attention(
        recv_query, recv_key, recv_value, cache_k, cache_v, new_len[0], prior_len[0], page_table[0]
    )
    mixed = lax.optimization_barrier(mixed)
    returned = lax.all_to_all(mixed, REQ, split_axis=0, concat_axis=0, tiled=True)
    out_w = jnp.concatenate(out_parts, axis=0)
    gate_up_w, out_w, returned = lax.optimization_barrier((gate_up_w, out_w, returned))
    attn_rows = jnp.take(returned.reshape(peers * pair_rows, -1), back_rows, axis=0)
    quarters = lax.all_to_all(
        attn_rows.reshape(groups, quarter, -1), "grp", split_axis=0, concat_axis=0, tiled=True
    )
    ordered = jnp.concatenate(
        [quarters[(group_index - shift) % groups] for shift in range(groups)], axis=1
    )
    attn_part = jnp.dot(ordered, out_w, preferred_element_type=jnp.float32)
    own_rows = lax.dynamic_slice_in_dim(hidden_in, group_index * quarter, quarter, 0).astype(
        jnp.float32
    )
    residual = own_rows + RESIDUAL_MULT * attn_part
    mlp_in = normalize(residual, mlp_gain).astype(jnp.bfloat16)
    piece = lax.all_gather(mlp_in, "rzc", axis=0, tiled=True)
    both = jnp.dot(piece, gate_up_w, preferred_element_type=jnp.float32)
    width = w_gate.shape[1]
    hidden = jnp.concatenate(
        [
            jax.nn.silu(both[:, 2 * k * width:(2 * k + 1) * width])
            * both[:, (2 * k + 1) * width:(2 * k + 2) * width]
            for k in range(ring)
        ],
        axis=1,
    ).astype(jnp.bfloat16)
    down_parts, hidden = lax.optimization_barrier((down_parts, hidden))
    units = w_down.shape[0]
    hidden = jnp.concatenate(
        [
            lax.dynamic_slice_in_dim(
                hidden, ((lax.axis_index("ry") - shift) % ring) * units, units, axis=1
            )
            for shift in range(ring)
        ],
        axis=1,
    )
    partial = jnp.dot(
        hidden, jnp.concatenate(down_parts, axis=0), preferred_element_type=jnp.float32
    )
    down = lax.psum_scatter(
        partial.astype(jnp.bfloat16),
        "rzc",
        scatter_dimension=0,
        tiled=True,
    ).astype(jnp.float32)
    layer_out = (residual + RESIDUAL_MULT * down).astype(jnp.bfloat16)
    return (layer_out, keys_out, values_out)


REQ = ("ry", "rzc")


def solution(mesh):
    req_size = mesh.shape["req"]
    major = 4
    inner = Mesh(
        mesh.devices.reshape(major, req_size // major, mesh.shape["grp"]), ("ry", "rzc", "grp")
    )
    in_specs = (
        P(REQ, None),
        P(),
        P(),
        P(None, "grp"),
        P(None, "grp"),
        P(None, "grp"),
        P("grp", None),
        P(None, REQ),
        P(None, REQ),
        P(REQ, None),
        P(REQ, None, "grp"),
        P(REQ, None, "grp"),
        P(REQ),
        P(REQ, None),
        P(REQ, None),
        P(REQ, None),
    )
    out_specs = (P(REQ + ("grp",), None), P(REQ, None, "grp"), P(REQ, None, "grp"))
    return jax.shard_map(body, mesh=inner, in_specs=in_specs, out_specs=out_specs, check_vma=False)
```

```python
import jax
import jax.numpy as jnp
from jax import lax
from jax.experimental import pallas as pl
from jax.experimental.pallas import tpu as pltpu
from jax.sharding import Mesh, PartitionSpec as P

HD = 64
PAGE = 16
MAXP = 16
CONTEXT = 256


EPSILON = 1e-05
RESIDUAL_MULT = 0.22
SCORE_MULT = 0.015625
ROPE_BASE = 10000000.0


def normalize(values, gain):
    mean_square = jnp.mean(values * values, axis=-1, keepdims=True)
    return values * lax.rsqrt(mean_square + EPSILON) * gain


def rotary(values, positions):
    dim = values.shape[-1]
    half = dim // 2
    freq = jnp.power(ROPE_BASE, -2.0 * jnp.arange(half, dtype=jnp.int32).astype(jnp.float32) / dim)
    angle = positions.astype(jnp.float32)[:, :, None] * freq
    cosine = jnp.cos(angle)[:, :, None, :]
    sine = jnp.sin(angle)[:, :, None, :]
    first = values[..., :half].astype(jnp.float32)
    second = values[..., half:].astype(jnp.float32)
    return jnp.concatenate(
        [first * cosine - second * sine, second * cosine + first * sine], axis=-1
    )


def source_layout(owner_block, peers, pair_rows):
    row_count = owner_block.shape[0]
    owners = jnp.arange(peers, dtype=jnp.int32)
    member = owner_block[None, :] == owners[:, None]
    counts = jnp.sum(member.astype(jnp.int32), axis=1)
    row_ids = jnp.arange(row_count, dtype=jnp.int32)
    starts = jnp.min(jnp.where(member, row_ids[None, :], row_count), axis=1)
    slots = jnp.arange(pair_rows, dtype=jnp.int32)
    gather_rows = jnp.where(
        slots[None, :] < counts[:, None], starts[:, None] + slots[None, :], row_count
    )
    row_start = jnp.sum(jnp.where(member, starts[:, None], 0), axis=0)
    back_rows = owner_block * pair_rows + (row_ids - row_start)
    return (gather_rows.reshape(-1), back_rows)


def attention_kernel(table_ref, prior_ref, len_ref, q_ref, k_ref, v_ref, ck_ref, cv_ref,
                     out_ref, nk_ref, nv_ref, kbuf, vbuf):
    sources, pair_rows, qcols = q_ref.shape
    kcols = k_ref.shape[-1]
    kv_heads = kcols // HD
    group = qcols // kcols

    def per_source(s, carry):
        prior = prior_ref[s]
        length = len_ref[s]
        for i in range(MAXP):
            page = table_ref[s * MAXP + i]
            kbuf[i * PAGE:(i + 1) * PAGE, :] = ck_ref[page]
            vbuf[i * PAGE:(i + 1) * PAGE, :] = cv_ref[page]
        j_col = lax.broadcasted_iota(jnp.int32, (CONTEXT, pair_rows), 0)
        t_row = lax.broadcasted_iota(jnp.int32, (CONTEXT, pair_rows), 1)
        select = jnp.logical_and(j_col == prior + t_row, t_row < length).astype(jnp.bfloat16)
        j_only = lax.broadcasted_iota(jnp.int32, (CONTEXT, kcols), 0)
        fresh = jnp.logical_and(j_only >= prior, j_only < prior + length)
        k_new = jnp.dot(select, k_ref[s], preferred_element_type=jnp.float32).astype(jnp.bfloat16)
        v_new = jnp.dot(select, v_ref[s], preferred_element_type=jnp.float32).astype(jnp.bfloat16)
        keys = jnp.where(fresh, k_new, kbuf[...])
        values = jnp.where(fresh, v_new, vbuf[...])
        for i in range(MAXP):
            page = table_ref[s * MAXP + i]
            nk_ref[page] = keys[i * PAGE:(i + 1) * PAGE, :]
            nv_ref[page] = values[i * PAGE:(i + 1) * PAGE, :]
        q_all = q_ref[s]
        rows = group * pair_rows
        r_idx = lax.broadcasted_iota(jnp.int32, (rows, CONTEXT), 0)
        j_idx = lax.broadcasted_iota(jnp.int32, (rows, CONTEXT), 1)
        allowed = j_idx <= prior + r_idx % pair_rows
        for h in range(kv_heads):
            q_h = jnp.concatenate(
                [q_all[:, (h * group + g) * HD:(h * group + g + 1) * HD] for g in range(group)],
                axis=0,
            )
            k_h = keys[:, h * HD:(h + 1) * HD]
            v_h = values[:, h * HD:(h + 1) * HD]
            scores = lax.dot_general(
                q_h, k_h, (((1,), (1,)), ((), ())), preferred_element_type=jnp.float32
            ) * SCORE_MULT
            scores = jnp.where(allowed, scores, -jnp.inf)
            top = jnp.max(scores, axis=-1, keepdims=True)
            weights = jnp.exp(scores - top)
            probs = (weights / jnp.sum(weights, axis=-1, keepdims=True)).astype(jnp.bfloat16)
            mixed = jnp.dot(probs, v_h, preferred_element_type=jnp.float32).astype(jnp.bfloat16)
            for g in range(group):
                c = h * group + g
                out_ref[s, :, c * HD:(c + 1) * HD] = mixed[g * pair_rows:(g + 1) * pair_rows, :]
        return carry

    lax.fori_loop(0, sources, per_source, 0)


def owner_attention(query_in, key_in, value_in, cache_keys, cache_values, lengths, priors, table):
    sources, pair_rows, qcols = query_in.shape
    kcols = key_in.shape[-1]
    kv_heads = kcols // HD
    slots = jnp.arange(pair_rows, dtype=jnp.int32)
    positions = priors[:, None] + slots[None, :]
    query_rot = rotary(query_in.reshape(sources, pair_rows, qcols // HD, HD), positions).astype(
        jnp.bfloat16
    ).reshape(sources, pair_rows, qcols)
    key_rot = rotary(key_in.reshape(sources, pair_rows, kv_heads, HD), positions).astype(
        jnp.bfloat16
    ).reshape(sources, pair_rows, kcols)
    pool_pages = cache_keys.shape[0]
    smem = pl.BlockSpec(memory_space=pltpu.SMEM)
    vmem = pl.BlockSpec(memory_space=pltpu.VMEM)
    return pl.pallas_call(
        attention_kernel,
        out_shape=(
            jax.ShapeDtypeStruct((sources, pair_rows, qcols), jnp.bfloat16),
            jax.ShapeDtypeStruct(cache_keys.shape, cache_keys.dtype),
            jax.ShapeDtypeStruct(cache_values.shape, cache_values.dtype),
        ),
        in_specs=[smem, smem, smem, vmem, vmem, vmem, vmem, vmem],
        out_specs=(vmem, vmem, vmem),
        scratch_shapes=[
            pltpu.VMEM((CONTEXT, kcols), jnp.bfloat16),
            pltpu.VMEM((CONTEXT, kcols), jnp.bfloat16),
        ],
        compiler_params=pltpu.CompilerParams(vmem_limit_bytes=48 * 1024 * 1024),
    )(table, priors, lengths, query_rot, key_rot, value_in, cache_keys, cache_values)


def body(
    hidden_in,
    attn_gain,
    mlp_gain,
    w_query,
    w_key,
    w_value,
    w_out,
    w_gate,
    w_up,
    w_down,
    cache_k,
    cache_v,
    owner_of_row,
    new_len,
    prior_len,
    page_table,
):
    peers = lax.axis_size(REQ)
    groups = lax.axis_size("grp")
    row_count = hidden_in.shape[0]
    pair_rows = 2 * row_count // peers
    quarter = row_count // groups
    group_index = lax.axis_index("grp")
    gate_up_w = lax.all_gather(jnp.concatenate([w_gate, w_up], axis=1), "ry", axis=1, tiled=True)
    ring = lax.axis_size("ry")
    down_parts = [w_down] + [
        lax.ppermute(w_down, "ry", [(i, (i + shift) % ring) for i in range(ring)])
        for shift in range(1, ring)
    ]
    out_parts = [w_out] + [
        lax.ppermute(w_out, "grp", [(i, (i + shift) % groups) for i in range(groups)])
        for shift in range(1, groups)
    ]
    normed = normalize(hidden_in.astype(jnp.float32), attn_gain).astype(jnp.bfloat16)
    qcols = w_query.shape[1]
    kcols = w_key.shape[1]
    query_rows = jnp.dot(normed, w_query, preferred_element_type=jnp.float32).astype(jnp.bfloat16)
    key_rows = jnp.dot(normed, w_key, preferred_element_type=jnp.float32).astype(jnp.bfloat16)
    value_rows = jnp.dot(normed, w_value, preferred_element_type=jnp.float32).astype(jnp.bfloat16)
    qkv_rows = jnp.concatenate([query_rows, key_rows, value_rows], axis=1)
    gather_rows, back_rows = source_layout(owner_of_row, peers, pair_rows)
    send_qkv = jnp.take(qkv_rows, gather_rows, axis=0, mode="fill", fill_value=0).reshape(
        peers, pair_rows, -1
    )
    recv_qkv = lax.all_to_all(send_qkv, REQ, split_axis=0, concat_axis=0, tiled=True)
    recv_query = recv_qkv[..., :qcols]
    recv_key = recv_qkv[..., qcols : qcols + kcols]
    recv_value = recv_qkv[..., qcols + kcols :]
    mixed, keys_out, values_out = owner_attention(
        recv_query, recv_key, recv_value, cache_k, cache_v, new_len[0], prior_len[0], page_table[0]
    )
    mixed = lax.optimization_barrier(mixed)
    returned = lax.all_to_all(mixed, REQ, split_axis=0, concat_axis=0, tiled=True)
    out_w = jnp.concatenate(out_parts, axis=0)
    gate_up_w, out_w, returned = lax.optimization_barrier((gate_up_w, out_w, returned))
    attn_rows = jnp.take(returned.reshape(peers * pair_rows, -1), back_rows, axis=0)
    quarters = lax.all_to_all(
        attn_rows.reshape(groups, quarter, -1), "grp", split_axis=0, concat_axis=0, tiled=True
    )
    ordered = jnp.concatenate(
        [quarters[(group_index - shift) % groups] for shift in range(groups)], axis=1
    )
    attn_part = jnp.dot(ordered, out_w, preferred_element_type=jnp.float32)
    own_rows = lax.dynamic_slice_in_dim(hidden_in, group_index * quarter, quarter, 0).astype(
        jnp.float32
    )
    residual = own_rows + RESIDUAL_MULT * attn_part
    mlp_in = normalize(residual, mlp_gain).astype(jnp.bfloat16)
    piece = lax.all_gather(mlp_in, "rzc", axis=0, tiled=True)
    both = jnp.dot(piece, gate_up_w, preferred_element_type=jnp.float32)
    width = w_gate.shape[1]
    units = w_down.shape[0]
    blocks = []
    for shift in range(ring):
        block = (lax.axis_index("ry") - shift) % ring
        gate = lax.dynamic_slice_in_dim(both, 2 * block * width, width, axis=1)
        upper = lax.dynamic_slice_in_dim(both, (2 * block + 1) * width, width, axis=1)
        blocks.append(jax.nn.silu(gate) * upper)
    hidden = jnp.concatenate(blocks, axis=1).astype(jnp.bfloat16)
    down_parts, hidden = lax.optimization_barrier((down_parts, hidden))
    partial = jnp.dot(
        hidden, jnp.concatenate(down_parts, axis=0), preferred_element_type=jnp.float32
    )
    down = lax.psum_scatter(
        partial.astype(jnp.bfloat16),
        "rzc",
        scatter_dimension=0,
        tiled=True,
    ).astype(jnp.float32)
    layer_out = (residual + RESIDUAL_MULT * down).astype(jnp.bfloat16)
    return (layer_out, keys_out, values_out)


REQ = ("ry", "rzc")


def solution(mesh):
    req_size = mesh.shape["req"]
    major = 4
    inner = Mesh(
        mesh.devices.reshape(major, req_size // major, mesh.shape["grp"]), ("ry", "rzc", "grp")
    )
    in_specs = (
        P(REQ, None),
        P(),
        P(),
        P(None, "grp"),
        P(None, "grp"),
        P(None, "grp"),
        P("grp", None),
        P(None, REQ),
        P(None, REQ),
        P(REQ, None),
        P(REQ, None, "grp"),
        P(REQ, None, "grp"),
        P(REQ),
        P(REQ, None),
        P(REQ, None),
        P(REQ, None),
    )
    out_specs = (P(REQ + ("grp",), None), P(REQ, None, "grp"), P(REQ, None, "grp"))
    return jax.shard_map(body, mesh=inner, in_specs=in_specs, out_specs=out_specs, check_vma=False)
```

```python
import jax
import jax.numpy as jnp
from jax import lax
from jax.experimental import pallas as pl
from jax.experimental.pallas import tpu as pltpu
from jax.sharding import Mesh, PartitionSpec as P

HD = 64
PAGE = 16
MAXP = 16
CONTEXT = 256


EPSILON = 1e-05
RESIDUAL_MULT = 0.22
SCORE_MULT = 0.015625
ROPE_BASE = 10000000.0


def normalize(values, gain):
    mean_square = jnp.mean(values * values, axis=-1, keepdims=True)
    return values * lax.rsqrt(mean_square + EPSILON) * gain


def rotary(values, positions):
    dim = values.shape[-1]
    half = dim // 2
    freq = jnp.power(ROPE_BASE, -2.0 * jnp.arange(half, dtype=jnp.int32).astype(jnp.float32) / dim)
    angle = positions.astype(jnp.float32)[:, :, None] * freq
    cosine = jnp.cos(angle)[:, :, None, :]
    sine = jnp.sin(angle)[:, :, None, :]
    first = values[..., :half].astype(jnp.float32)
    second = values[..., half:].astype(jnp.float32)
    return jnp.concatenate(
        [first * cosine - second * sine, second * cosine + first * sine], axis=-1
    )


def source_layout(owner_block, peers, pair_rows):
    row_count = owner_block.shape[0]
    owners = jnp.arange(peers, dtype=jnp.int32)
    member = owner_block[None, :] == owners[:, None]
    counts = jnp.sum(member.astype(jnp.int32), axis=1)
    row_ids = jnp.arange(row_count, dtype=jnp.int32)
    starts = jnp.min(jnp.where(member, row_ids[None, :], row_count), axis=1)
    slots = jnp.arange(pair_rows, dtype=jnp.int32)
    gather_rows = jnp.where(
        slots[None, :] < counts[:, None], starts[:, None] + slots[None, :], row_count
    )
    row_start = jnp.sum(jnp.where(member, starts[:, None], 0), axis=0)
    back_rows = owner_block * pair_rows + (row_ids - row_start)
    return (gather_rows.reshape(-1), back_rows)


def attention_kernel(table_ref, prior_ref, len_ref, q_ref, k_ref, v_ref, ck_ref, cv_ref,
                     out_ref, nk_ref, nv_ref, kbuf, vbuf):
    sources, pair_rows, qcols = q_ref.shape
    kcols = k_ref.shape[-1]
    kv_heads = kcols // HD
    group = qcols // kcols

    def per_source(s, carry):
        prior = prior_ref[s]
        length = len_ref[s]
        pages = [table_ref[s * MAXP + i] for i in range(MAXP)]
        old_keys = jnp.concatenate([ck_ref[page] for page in pages], axis=0)
        old_values = jnp.concatenate([cv_ref[page] for page in pages], axis=0)
        j_col = lax.broadcasted_iota(jnp.int32, (CONTEXT, pair_rows), 0)
        t_row = lax.broadcasted_iota(jnp.int32, (CONTEXT, pair_rows), 1)
        select = jnp.logical_and(j_col == prior + t_row, t_row < length).astype(jnp.bfloat16)
        j_only = lax.broadcasted_iota(jnp.int32, (CONTEXT, kcols), 0)
        fresh = jnp.logical_and(j_only >= prior, j_only < prior + length)
        k_new = jnp.dot(select, k_ref[s], preferred_element_type=jnp.float32).astype(jnp.bfloat16)
        v_new = jnp.dot(select, v_ref[s], preferred_element_type=jnp.float32).astype(jnp.bfloat16)
        keys = jnp.where(fresh, k_new, old_keys)
        values = jnp.where(fresh, v_new, old_values)
        for i in range(MAXP):
            page = table_ref[s * MAXP + i]
            nk_ref[page] = keys[i * PAGE:(i + 1) * PAGE, :]
            nv_ref[page] = values[i * PAGE:(i + 1) * PAGE, :]
        q_all = q_ref[s]
        rows = group * pair_rows
        r_idx = lax.broadcasted_iota(jnp.int32, (rows, CONTEXT), 0)
        j_idx = lax.broadcasted_iota(jnp.int32, (rows, CONTEXT), 1)
        allowed = j_idx <= prior + r_idx % pair_rows
        for h in range(kv_heads):
            q_h = jnp.concatenate(
                [q_all[:, (h * group + g) * HD:(h * group + g + 1) * HD] for g in range(group)],
                axis=0,
            )
            k_h = keys[:, h * HD:(h + 1) * HD]
            v_h = values[:, h * HD:(h + 1) * HD]
            scores = lax.dot_general(
                q_h, k_h, (((1,), (1,)), ((), ())), preferred_element_type=jnp.float32
            ) * SCORE_MULT
            scores = jnp.where(allowed, scores, -jnp.inf)
            top = jnp.max(scores, axis=-1, keepdims=True)
            weights = jnp.exp(scores - top)
            probs = (weights / jnp.sum(weights, axis=-1, keepdims=True)).astype(jnp.bfloat16)
            mixed = jnp.dot(probs, v_h, preferred_element_type=jnp.float32).astype(jnp.bfloat16)
            for g in range(group):
                c = h * group + g
                out_ref[s, :, c * HD:(c + 1) * HD] = mixed[g * pair_rows:(g + 1) * pair_rows, :]
        return carry

    lax.fori_loop(0, sources, per_source, 0)


def owner_attention(query_in, key_in, value_in, cache_keys, cache_values, lengths, priors, table):
    sources, pair_rows, qcols = query_in.shape
    kcols = key_in.shape[-1]
    kv_heads = kcols // HD
    slots = jnp.arange(pair_rows, dtype=jnp.int32)
    positions = priors[:, None] + slots[None, :]
    query_rot = rotary(query_in.reshape(sources, pair_rows, qcols // HD, HD), positions).astype(
        jnp.bfloat16
    ).reshape(sources, pair_rows, qcols)
    key_rot = rotary(key_in.reshape(sources, pair_rows, kv_heads, HD), positions).astype(
        jnp.bfloat16
    ).reshape(sources, pair_rows, kcols)
    pool_pages = cache_keys.shape[0]
    smem = pl.BlockSpec(memory_space=pltpu.SMEM)
    vmem = pl.BlockSpec(memory_space=pltpu.VMEM)
    return pl.pallas_call(
        attention_kernel,
        out_shape=(
            jax.ShapeDtypeStruct((sources, pair_rows, qcols), jnp.bfloat16),
            jax.ShapeDtypeStruct(cache_keys.shape, cache_keys.dtype),
            jax.ShapeDtypeStruct(cache_values.shape, cache_values.dtype),
        ),
        in_specs=[smem, smem, smem, vmem, vmem, vmem, vmem, vmem],
        out_specs=(vmem, vmem, vmem),
        scratch_shapes=[
            pltpu.VMEM((CONTEXT, kcols), jnp.bfloat16),
            pltpu.VMEM((CONTEXT, kcols), jnp.bfloat16),
        ],
        compiler_params=pltpu.CompilerParams(vmem_limit_bytes=48 * 1024 * 1024),
    )(table, priors, lengths, query_rot, key_rot, value_in, cache_keys, cache_values)


def body(
    hidden_in,
    attn_gain,
    mlp_gain,
    w_query,
    w_key,
    w_value,
    w_out,
    w_gate,
    w_up,
    w_down,
    cache_k,
    cache_v,
    owner_of_row,
    new_len,
    prior_len,
    page_table,
):
    peers = lax.axis_size(REQ)
    groups = lax.axis_size("grp")
    row_count = hidden_in.shape[0]
    pair_rows = 2 * row_count // peers
    quarter = row_count // groups
    group_index = lax.axis_index("grp")
    gate_up_w = lax.all_gather(jnp.concatenate([w_gate, w_up], axis=1), "ry", axis=1, tiled=True)
    ring = lax.axis_size("ry")
    down_parts = [w_down] + [
        lax.ppermute(w_down, "ry", [(i, (i + shift) % ring) for i in range(ring)])
        for shift in range(1, ring)
    ]
    out_parts = [w_out] + [
        lax.ppermute(w_out, "grp", [(i, (i + shift) % groups) for i in range(groups)])
        for shift in range(1, groups)
    ]
    normed = normalize(hidden_in.astype(jnp.float32), attn_gain).astype(jnp.bfloat16)
    qcols = w_query.shape[1]
    kcols = w_key.shape[1]
    query_rows = jnp.dot(normed, w_query, preferred_element_type=jnp.float32).astype(jnp.bfloat16)
    key_rows = jnp.dot(normed, w_key, preferred_element_type=jnp.float32).astype(jnp.bfloat16)
    value_rows = jnp.dot(normed, w_value, preferred_element_type=jnp.float32).astype(jnp.bfloat16)
    qkv_rows = jnp.concatenate([query_rows, key_rows, value_rows], axis=1)
    gather_rows, back_rows = source_layout(owner_of_row, peers, pair_rows)
    send_qkv = jnp.take(qkv_rows, gather_rows, axis=0, mode="fill", fill_value=0).reshape(
        peers, pair_rows, -1
    )
    recv_qkv = lax.all_to_all(send_qkv, REQ, split_axis=0, concat_axis=0, tiled=True)
    recv_query = recv_qkv[..., :qcols]
    recv_key = recv_qkv[..., qcols : qcols + kcols]
    recv_value = recv_qkv[..., qcols + kcols :]
    mixed, keys_out, values_out = owner_attention(
        recv_query, recv_key, recv_value, cache_k, cache_v, new_len[0], prior_len[0], page_table[0]
    )
    mixed = lax.optimization_barrier(mixed)
    returned = lax.all_to_all(mixed, REQ, split_axis=0, concat_axis=0, tiled=True)
    out_w = jnp.concatenate(out_parts, axis=0)
    gate_up_w, out_w, returned = lax.optimization_barrier((gate_up_w, out_w, returned))
    attn_rows = jnp.take(returned.reshape(peers * pair_rows, -1), back_rows, axis=0)
    quarters = lax.all_to_all(
        attn_rows.reshape(groups, quarter, -1), "grp", split_axis=0, concat_axis=0, tiled=True
    )
    ordered = jnp.concatenate(
        [quarters[(group_index - shift) % groups] for shift in range(groups)], axis=1
    )
    attn_part = jnp.dot(ordered, out_w, preferred_element_type=jnp.float32)
    own_rows = lax.dynamic_slice_in_dim(hidden_in, group_index * quarter, quarter, 0).astype(
        jnp.float32
    )
    residual = own_rows + RESIDUAL_MULT * attn_part
    mlp_in = normalize(residual, mlp_gain).astype(jnp.bfloat16)
    piece = lax.all_gather(mlp_in, "rzc", axis=0, tiled=True)
    both = jnp.dot(piece, gate_up_w, preferred_element_type=jnp.float32)
    width = w_gate.shape[1]
    hidden = jnp.concatenate(
        [
            jax.nn.silu(both[:, 2 * k * width:(2 * k + 1) * width])
            * both[:, (2 * k + 1) * width:(2 * k + 2) * width]
            for k in range(ring)
        ],
        axis=1,
    ).astype(jnp.bfloat16)
    down_parts, hidden = lax.optimization_barrier((down_parts, hidden))
    units = w_down.shape[0]
    hidden = jnp.concatenate(
        [
            lax.dynamic_slice_in_dim(
                hidden, ((lax.axis_index("ry") - shift) % ring) * units, units, axis=1
            )
            for shift in range(ring)
        ],
        axis=1,
    )
    partial = jnp.dot(
        hidden, jnp.concatenate(down_parts, axis=0), preferred_element_type=jnp.float32
    )
    down = lax.psum_scatter(
        partial.astype(jnp.bfloat16),
        "rzc",
        scatter_dimension=0,
        tiled=True,
    ).astype(jnp.float32)
    layer_out = (residual + RESIDUAL_MULT * down).astype(jnp.bfloat16)
    return (layer_out, keys_out, values_out)


REQ = ("ry", "rzc")


def solution(mesh):
    req_size = mesh.shape["req"]
    major = 4
    inner = Mesh(
        mesh.devices.reshape(major, req_size // major, mesh.shape["grp"]), ("ry", "rzc", "grp")
    )
    in_specs = (
        P(REQ, None),
        P(),
        P(),
        P(None, "grp"),
        P(None, "grp"),
        P(None, "grp"),
        P("grp", None),
        P(None, REQ),
        P(None, REQ),
        P(REQ, None),
        P(REQ, None, "grp"),
        P(REQ, None, "grp"),
        P(REQ),
        P(REQ, None),
        P(REQ, None),
        P(REQ, None),
    )
    out_specs = (P(REQ + ("grp",), None), P(REQ, None, "grp"), P(REQ, None, "grp"))
    return jax.shard_map(body, mesh=inner, in_specs=in_specs, out_specs=out_specs, check_vma=False)
```
